32 devices in a mesh: gx: 8 (over y, x, core), gy: 4 (over z).
Axes of the slice: x: 2, y: 2, z: 4, core: 2. Of those that a mesh axis runs over, the one named last changes fastest.
Arguments:
- e_field: float32 [3, 3, 2048, 2048], P(None, None, 'gx', 'gy'), may hold values from -6 to 6
- h_field: float32 [3, 3, 2048, 2048], P(None, None, 'gx', 'gy'), may hold values from -6 to 6
- material: int32 [3, 2048, 2048], P(None, 'gx', 'gy'), may hold values from 0 to 7
- eps_table: float32 [8], replicated, may hold values from 1 to 12
- src_pos: int32 [1024, 3], replicated, may hold values from 0 to 2047, as said below
- src_amp: float32 [1024], replicated, may hold values from -40 to 40
- freqs: float32 [2], replicated, may hold values from 0.3 to 2.8
Outputs:
- e_out: float32 [3, 3, 2048, 2048], P(None, None, 'gx', 'gy')
- h_out: float32 [3, 3, 2048, 2048], P(None, None, 'gx', 'gy')
- far_field: float32 [1024, 8, 2, 1024], P('gx', None, None, 'gy')
The draws below stay inside these ranges and needn't reach their ends.
Inputs may be any that keep to these rules, and one draw needn't show every extreme that they name: `src_pos`: each row is a cell (layer, row, column) of the slab; several sources may share a cell.
All inputs are finite; a program needn't handle non-finite values.
Results may differ from the reference program's by a relative error of at most 0.0054.
Values may be sent and summed in bfloat16 or wider, within the bound.
A program may use at most 192 MiB of HBM per device.

```python
import math
import jax
import jax.numpy as jnp
from jax import lax

NX = 2048
NY = 2048
LZ = 3
FACE = 1
STEPS = 2
NF = 2
ITEMS = 8
NA = 1024
NMAT = 8
NSRC = 1024


def draw_src_pos(key, part):
    key_layer, key_row, key_col = jax.random.split(jax.random.fold_in(key, 17), 3)
    layers = jax.random.randint(key_layer, (NSRC,), 0, LZ)
    rows_drawn = jax.random.randint(key_row, (NSRC,), 0, NX)
    cols_drawn = jax.random.randint(key_col, (NSRC,), 0, NY)
    positions = jnp.stack([layers, rows_drawn, cols_drawn], 1).astype(jnp.int32)
    corner = jnp.array([0, NX - 1, NY - 1], jnp.int32)
    return positions.at[0].set(corner)


def place_ends(entries, stream_key, low, high):
    index_at = [jax.random.randint(jax.random.fold_in(stream_key, axis), (), 0, length) for axis, length in enumerate(entries.shape)]
    widest = entries.shape.index(max(entries.shape))
    next_to = index_at[:widest] + [(index_at[widest] + 1) % entries.shape[widest]] + index_at[widest + 1:]
    return entries.at[tuple(index_at)].set(low).at[tuple(next_to)].set(high)


def levels(stream_key, shape, cuts, smallest, high):
    level = 1.0
    for position, parts in cuts:
        heights = jax.random.uniform(jax.random.fold_in(jax.random.fold_in(stream_key, 6), position), (parts,), jnp.float32, smallest / len(cuts), high / len(cuts))
        level = level * jnp.repeat(jnp.exp(heights), shape[position] // parts).reshape((-1,) + (1,) * (len(shape) - 1 - position))
    return level


def normal_values(rng, dims, spread, reach, shards=(), held_as=jnp.bfloat16):
    drawn = jax.random.normal(rng, dims, jnp.float32) * spread
    if len(shards) > 0:
        drawn = levels(rng, dims, shards, -0.22, 0.18) * drawn
    return jnp.clip(drawn, min=-reach, max=reach).astype(held_as)


def setup_inputs(seed: int = 0) -> dict:
    key_list = jax.random.split(jax.random.key(seed), 8)
    e_field = normal_values(key_list[0], (3, LZ, NX, NY), 1.0, 6.0, ((2, 8), (3, 4)), jnp.float32)
    h_field = normal_values(key_list[1], (3, LZ, NX, NY), 1.0, 6.0, ((2, 8), (3, 4)), jnp.float32)
    material = place_ends(jax.random.randint(key_list[2], (LZ, NX, NY), 0, NMAT), jax.random.fold_in(key_list[2], 1), 0, NMAT - 1).astype(jnp.int32)
    eps_table = jnp.clip(jnp.exp(jax.random.uniform(key_list[3], (NMAT,), jnp.float32, math.log(1.0), math.log(12.0))), 1.0, 12.0)
    src_pos = draw_src_pos(jax.random.fold_in(key_list[7], 71), 0)
    src_amp = normal_values(key_list[5], (NSRC,), 8.0, 40.0, (), jnp.float32)
    freqs = jnp.clip(jax.random.uniform(key_list[6], (NF,), jnp.float32, 0.3, 2.8), 0.3, 2.8)
    return {"e_field": e_field, "h_field": h_field, "material": material, "eps_table": eps_table, "src_pos": src_pos, "src_amp": src_amp, "freqs": freqs}


courant = 0.5
source_rate = 0.7
zoom_factor = 4

def chirp(freq_index, cell_index, period):
    remainder = jnp.remainder(freq_index * cell_index, period)
    phase_angle = remainder.astype(jnp.float32) * (2.0 * math.pi / period)
    return (jnp.cos(phase_angle), -jnp.sin(phase_angle))

def forward(field, dimension, boundary):
    inner = lax.slice_in_dim(field, 1, field.shape[dimension], axis=dimension)
    return jnp.concatenate([inner, jnp.expand_dims(boundary, dimension)], dimension)

def backward(field, dimension, boundary):
    inner = lax.slice_in_dim(field, 0, field.shape[dimension] - 1, axis=dimension)
    return jnp.concatenate([jnp.expand_dims(boundary, dimension), inner], dimension)

def curl_forward(electric, row_rim, col_rim):
    field_x, field_y, field_z = (electric[0], electric[1], electric[2])
    zero_layer = jnp.zeros(field_x.shape[1:], jnp.float32)
    curl_x = forward(field_z, 2, col_rim[1]) - field_z - (forward(field_y, 0, zero_layer) - field_y)
    curl_y = forward(field_x, 0, zero_layer) - field_x - (forward(field_z, 1, row_rim[1]) - field_z)
    curl_z = forward(field_y, 1, row_rim[0]) - field_y - (forward(field_x, 2, col_rim[0]) - field_x)
    return jnp.stack([curl_x, curl_y, curl_z])

def curl_backward(magnetic, row_rim, col_rim):
    field_x, field_y, field_z = (magnetic[0], magnetic[1], magnetic[2])
    zero_layer = jnp.zeros(field_x.shape[1:], jnp.float32)
    curl_x = field_z - backward(field_z, 2, col_rim[1]) - (field_y - backward(field_y, 0, zero_layer))
    curl_y = field_x - backward(field_x, 0, zero_layer) - (field_z - backward(field_z, 1, row_rim[1]))
    curl_z = field_y - backward(field_y, 1, row_rim[0]) - (field_x - backward(field_x, 2, col_rim[0]))
    return jnp.stack([curl_x, curl_y, curl_z])

def reference(e_field, h_field, material, eps_table, src_pos, src_amp, freqs):
    update_scale = courant / eps_table[material]
    source_grid = jnp.zeros((LZ, NX, NY), jnp.float32).at[src_pos[:, 0], src_pos[:, 1], src_pos[:, 2]].add(src_amp)
    row_zero = jnp.zeros((2, LZ, NY), jnp.float32)
    col_zero = jnp.zeros((2, LZ, NX), jnp.float32)
    electric, magnetic = (e_field, h_field)
    real_sum = jnp.zeros((NF, 4, NX, NY), jnp.float32)
    imag_sum = jnp.zeros((NF, 4, NX, NY), jnp.float32)
    for step_index in range(STEPS):
        moment = float(step_index + 1)
        magnetic = magnetic - courant * curl_forward(electric, row_zero, col_zero)
        electric = electric + update_scale * curl_backward(magnetic, row_zero, col_zero)
        electric = electric.at[2].add(math.sin(source_rate * moment) * source_grid)
        face_now = jnp.stack([-magnetic[1, FACE], magnetic[0, FACE], electric[1, FACE], -electric[0, FACE]])
        real_sum = real_sum + face_now[None] * jnp.cos(freqs * moment)[:, None, None, None]
        imag_sum = imag_sum + face_now[None] * jnp.sin(freqs * moment)[:, None, None, None]
    currents = jnp.stack([real_sum.reshape(ITEMS, NX, NY), imag_sum.reshape(ITEMS, NX, NY)], 1).astype(jnp.bfloat16)
    u_index = jnp.arange(NA, dtype=jnp.int32)
    x_index = jnp.arange(NX, dtype=jnp.int32)
    y_index = jnp.arange(NY, dtype=jnp.int32)
    x_real, x_imag = chirp((u_index - NA // 2)[:, None], x_index[None, :], zoom_factor * NX)
    x_table = jnp.stack([x_real, x_imag]).astype(jnp.bfloat16).astype(jnp.float32)
    y_real, y_imag = chirp(y_index[:, None], (u_index + NA // 4)[None, :], zoom_factor * NY)
    y_table = jnp.concatenate([y_real, y_imag], 1).astype(jnp.bfloat16).astype(jnp.float32)
    inv_norm = 1.0 / math.sqrt(NX * NY)

    def one_item(item_currents):
        values = item_currents.astype(jnp.float32)
        product = jnp.einsum('aux,bxy->abuy', x_table, values, precision=lax.Precision.HIGHEST)
        sectioned = jnp.stack([product[0, 0] - product[1, 1], product[0, 1] + product[1, 0]]).astype(jnp.bfloat16)
        second = jnp.einsum('buy,yw->buw', sectioned.astype(jnp.float32), y_table, precision=lax.Precision.HIGHEST)
        result = jnp.stack([second[0, :, :NA] - second[1, :, NA:], second[0, :, NA:] + second[1, :, :NA]])
        return result * inv_norm
    far_all = lax.map(one_item, currents)
    far_field = jnp.transpose(far_all, (2, 0, 1, 3))
    return (electric, magnetic, far_field)
```

```python
import functools
import math

import jax
import jax.numpy as jnp
from jax import lax
from jax.experimental import pallas as pl
from jax.experimental.pallas import tpu as pltpu
from jax.sharding import PartitionSpec as P

LZ = 3
FACE = 1
STEPS = 2
NF = 2
NA = 1024
NMAT = 8

courant = 0.5
source_rate = 0.7
zoom_factor = 4

BASE = 32
CHUNK = 16
SETS = 2
EACH = 4 // SETS
LANES = 128
PAD = 128
ANY = pl.BlockSpec(memory_space=pl.ANY)
VM = pl.BlockSpec(memory_space=pltpu.VMEM)
SM = pl.BlockSpec(memory_space=pltpu.SMEM)
BIG = 60 * 1024 * 1024


def shifted(block, axis, distance):
    size = lax.axis_size(axis)
    route = [(i - distance, i) for i in range(size) if 0 <= i - distance < size]
    return lax.ppermute(block, axis, route)


def fields_per_device(gx, cols):
    return 2 * EACH * cols // (gx * LANES)


def yee_kernel(
    grid_rows, grid_cols, per,
    e_hbm, h_hbm, m_hbm, colh, rowh, eps, pos, amp,
    e_out, h_out, *rest,
):
    sd_outs, (e_ext, h_ext, m_main, scale, src, first, sems) = rest[:SETS], rest[SETS:]
    rows, cols = m_main.shape[1:]
    width = cols + PAD
    high = e_ext.shape[1]
    row0 = lax.axis_index("gx") * rows
    col0 = lax.axis_index("gy") * cols
    main_r = pl.ds(BASE, rows)
    copies = [
        pltpu.make_async_copy(e_hbm, e_ext.at[:, main_r, pl.ds(0, cols)], sems.at[0]),
        pltpu.make_async_copy(h_hbm, h_ext.at[:, main_r, pl.ds(0, cols)], sems.at[1]),
        pltpu.make_async_copy(m_hbm, m_main, sems.at[2]),
    ]
    for copy in copies:
        copy.start()
    count = amp.shape[1]
    step = min(count, 1024)
    used = high - 2 * CHUNK
    row_at = row0 + lax.broadcasted_iota(jnp.int32, (used, step), 0) + (CHUNK - BASE)
    lane = lax.broadcasted_iota(jnp.int32, (width, step), 0)
    col_at = col0 + jnp.where(lane < cols + PAD // 2, lane, lane - width)
    for start in range(0, count, step):
        at = pl.ds(start, step)
        amp_now = amp[:, at]
        hi = amp_now.astype(jnp.bfloat16).astype(jnp.float32)
        mid = (amp_now - hi).astype(jnp.bfloat16).astype(jnp.float32)
        low = amp_now - hi - mid
        hit_col = jnp.where(col_at == pos[2:3, at], 1.0, 0.0).astype(jnp.bfloat16)
        hit_row = row_at == pos[1:2, at]
        for layer in range(LZ):
            hit = hit_row & (pos[0:1, at] == layer)
            total = None
            for piece in (hi, mid, low):
                left = jnp.where(hit, piece, 0.0).astype(jnp.bfloat16)
                term = lax.dot_general(
                    left, hit_col, (((1,), (1,)), ((), ())), preferred_element_type=jnp.float32
                )
                total = term if total is None else total + term
            if start == 0:
                src[layer, CHUNK : CHUNK + used, :] = total
            else:
                src[layer, CHUNK : CHUNK + used, :] += total
    copies[2].wait()

    def scale_of(index, row, col):
        value = jnp.full(index.shape, eps[0], jnp.float32)
        for material in range(1, NMAT):
            value = jnp.where(index == material, eps[material], value)
        inside = (row >= 0) & (row < grid_rows) & (col >= 0) & (col < grid_cols)
        return jnp.where(inside, courant / value, 0.0)

    col_main = col0 + lax.broadcasted_iota(jnp.int32, (CHUNK, cols), 1)
    lane_pad = lax.broadcasted_iota(jnp.int32, (CHUNK, PAD), 1)
    col_pad = col0 + jnp.where(lane_pad < PAD // 2, cols + lane_pad, lane_pad - PAD)
    row_chunk = row0 + lax.broadcasted_iota(jnp.int32, (CHUNK, cols), 0)

    def fill(step_index, carry):
        r = pl.multiple_of(step_index * CHUNK, CHUNK)
        near = pl.ds(r, CHUNK)
        far = pl.ds(BASE + r, CHUNK)
        for layer in range(LZ):
            scale[layer, far, :cols] = scale_of(m_main[layer, near, :], row_chunk + r, col_main)
            scale[layer, far, cols:] = scale_of(
                colh[6 * LZ + layer, near, :], row_chunk[:, :PAD] + r, col_pad
            )
        for plane in range(3 * LZ):
            e_ext[plane, far, cols:] = colh[plane, near, :]
            h_ext[plane, far, cols:] = colh[3 * LZ + plane, near, :]
        return carry

    lax.fori_loop(0, rows // CHUNK, fill, 0)
    lane_all = lax.broadcasted_iota(jnp.int32, (8, width), 1)
    col_all = col0 + jnp.where(lane_all < cols + PAD // 2, lane_all, lane_all - width)
    row_eight = row0 + lax.broadcasted_iota(jnp.int32, (8, width), 0)
    blank = jnp.zeros((8, width), jnp.float32)
    for place, target, offset, spare in (
        (0, BASE + rows, rows, BASE + rows + 8),
        (8, BASE - 8, -8, BASE - 16),
    ):
        for layer in range(LZ):
            scale[layer, target : target + 8, :] = scale_of(
                rowh[6 * LZ + layer, place : place + 8, :], row_eight + offset, col_all
            )
            scale[layer, spare : spare + 8, :] = blank
        for plane in range(3 * LZ):
            e_ext[plane, target : target + 8, :] = rowh[plane, place : place + 8, :]
            h_ext[plane, target : target + 8, :] = rowh[3 * LZ + plane, place : place + 8, :]
            e_ext[plane, spare : spare + 8, :] = blank
            h_ext[plane, spare : spare + 8, :] = blank
    for plane in range(3 * LZ):
        e_ext[plane, high - 16 : high, :] = jnp.zeros((16, width), jnp.float32)
        h_ext[plane, 0:16, :] = jnp.zeros((16, width), jnp.float32)
    lane_c = lax.broadcasted_iota(jnp.int32, (CHUNK, width), 1)
    col_c = col0 + jnp.where(lane_c < cols + PAD // 2, lane_c, lane_c - width)
    weight = jnp.where(col_c >= 0, courant, 0.0)
    top = lax.axis_index("gx") == 0
    copies[0].wait()
    copies[1].wait()

    def magnetic_pass(index, carry):
        r = pl.multiple_of(index * CHUNK, CHUNK)
        now = pl.ds(r, CHUNK)
        more = pl.ds(r, CHUNK + 8)
        factor = weight * jnp.where(top & (index * CHUNK < BASE), 0.0, 1.0)
        zero = jnp.zeros((CHUNK, width), jnp.float32)
        ex = [e_ext[layer, now, :] for layer in range(LZ)] + [zero]
        ey = [e_ext[LZ + layer, now, :] for layer in range(LZ)] + [zero]
        for layer in range(LZ):
            ez = e_ext[2 * LZ + layer, now, :]
            ez_row = pltpu.roll(e_ext[2 * LZ + layer, more, :], CHUNK + 7, 0)[:CHUNK]
            ey_row = pltpu.roll(e_ext[LZ + layer, more, :], CHUNK + 7, 0)[:CHUNK]
            ez_col = pltpu.roll(ez, width - 1, 1)
            ex_col = pltpu.roll(ex[layer], width - 1, 1)
            curl_x = ez_col - ez - (ey[layer + 1] - ey[layer])
            curl_y = ex[layer + 1] - ex[layer] - (ez_row - ez)
            curl_z = ey_row - ey[layer] - (ex_col - ex[layer])
            for part, curl in enumerate((curl_x, curl_y, curl_z)):
                plane = part * LZ + layer
                h_ext[plane, now, :] = h_ext[plane, now, :] - factor * curl
        return carry

    def electric_pass(moment, last, index, carry):
        r = pl.multiple_of(index * CHUNK, CHUNK)
        now = pl.ds(r, CHUNK)
        more = pl.ds(pl.multiple_of(r - 8, 8), CHUNK + 8)
        drive = math.sin(source_rate * moment)
        zero = jnp.zeros((CHUNK, width), jnp.float32)
        hx = [zero] + [h_ext[layer, now, :] for layer in range(LZ)]
        hy = [zero] + [h_ext[LZ + layer, now, :] for layer in range(LZ)]
        for layer in range(LZ):
            hz = h_ext[2 * LZ + layer, now, :]
            hz_row = pltpu.roll(h_ext[2 * LZ + layer, more, :], 1, 0)[8:]
            hy_row = pltpu.roll(h_ext[LZ + layer, more, :], 1, 0)[8:]
            hx_now, hy_now = hx[layer + 1], hy[layer + 1]
            hz_col = pltpu.roll(hz, 1, 1)
            hx_col = pltpu.roll(hx_now, 1, 1)
            curl_x = hz - hz_col - (hy_now - hy[layer])
            curl_y = hx_now - hx[layer] - (hz - hz_row)
            curl_z = hy_now - hy_row - (hx_now - hx_col)
            factor = scale[layer, now, :]
            new_x = e_ext[layer, now, :] + factor * curl_x
            new_y = e_ext[LZ + layer, now, :] + factor * curl_y
            new_z = e_ext[2 * LZ + layer, now, :] + factor * curl_z + drive * src[layer, now, :]
            e_ext[layer, now, :] = new_x
            e_ext[LZ + layer, now, :] = new_y
            e_ext[2 * LZ + layer, now, :] = new_z
            if layer == FACE:
                faces = (-hy_now, hx_now, new_y, -new_x)
                for item, face in enumerate(faces):
                    if last:
                        old = first[item, now, :]
                        here = pl.ds(r - BASE, CHUNK)
                        for which, value in enumerate((old + face, face - old)):
                            share, place = divmod(which * EACH + item % EACH, per)
                            for q in range(cols // LANES):
                                piece = value[:, q * LANES : (q + 1) * LANES].astype(jnp.bfloat16)
                                lanes = pl.ds(place * LANES, LANES)
                                sd_outs[item // EACH][q * (2 * EACH // per) + share, here, lanes] = piece
                    else:
                        first[item, now, :] = face
        return carry

    chunks = high // CHUNK
    main0 = BASE // CHUNK
    main1 = main0 + rows // CHUNK
    lax.fori_loop(1, chunks - 1, magnetic_pass, 0)
    lax.fori_loop(1, chunks - 1, functools.partial(electric_pass, 1.0, False), 0)
    lax.fori_loop(1, main1, magnetic_pass, 0)
    out_h = pltpu.make_async_copy(h_ext.at[:, main_r, pl.ds(0, cols)], h_out, sems.at[3])
    out_h.start()
    lax.fori_loop(main0, main1, functools.partial(electric_pass, 2.0, True), 0)
    out_e = pltpu.make_async_copy(e_ext.at[:, main_r, pl.ds(0, cols)], e_out, sems.at[4])
    out_e.start()
    out_h.wait()
    out_e.wait()


def yee(e_field, h_field, material, eps_table, src_pos, src_amp):
    rows, cols = material.shape[1:]
    gx = lax.axis_size("gx")
    per = fields_per_device(gx, cols)
    grid_rows = rows * gx
    grid_cols = cols * lax.axis_size("gy")
    planes = 3 * LZ
    e = e_field.reshape(planes, rows, cols)
    h = h_field.reshape(planes, rows, cols)

    def edge(low, high, dim):
        cut = lambda a: lax.slice_in_dim(a, low, high, axis=dim)
        return jnp.concatenate([cut(e), cut(h), cut(material).astype(jnp.float32)], 0)

    send_prev = jnp.swapaxes(edge(0, 2, 2), 1, 2)
    send_next = jnp.swapaxes(edge(cols - 2, cols, 2), 1, 2)
    right = shifted(send_prev, "gy", -1)
    left = shifted(send_next, "gy", 1)
    right = jnp.swapaxes(right, 1, 2)
    left = jnp.swapaxes(left, 1, 2)
    total = 2 * planes + LZ
    col_halo = jnp.concatenate(
        [right, jnp.zeros((total, rows, PAD - 4), jnp.float32), left], 2
    )
    send_up = jnp.concatenate([edge(0, 2, 1), col_halo[:, 0:2]], 2)
    send_down = jnp.concatenate([edge(rows - 2, rows, 1), col_halo[:, rows - 2 :]], 2)
    below = shifted(send_up, "gx", -1)
    above = shifted(send_down, "gx", 1)
    row_halo = jnp.concatenate(
        [below, jnp.zeros((total, 12, cols + PAD), jnp.float32), above], 1
    )
    high = rows + 2 * BASE
    width = cols + PAD
    f32 = jnp.float32
    out = pl.pallas_call(
        functools.partial(yee_kernel, grid_rows, grid_cols, per),
        out_shape=(
            jax.ShapeDtypeStruct((planes, rows, cols), f32),
            jax.ShapeDtypeStruct((planes, rows, cols), f32),
        )
        + (jax.ShapeDtypeStruct((gx, rows, per * LANES), jnp.bfloat16),) * SETS,
        in_specs=[ANY, ANY, ANY, VM, VM, SM, VM, VM],
        out_specs=(ANY, ANY) + (VM,) * SETS,
        scratch_shapes=[
            pltpu.VMEM((planes, high, width), f32),
            pltpu.VMEM((planes, high, width), f32),
            pltpu.VMEM((LZ, rows, cols), jnp.int32),
            pltpu.VMEM((LZ, high, width), f32),
            pltpu.VMEM((LZ, high, width), f32),
            pltpu.VMEM((4, high, width), f32),
            pltpu.SemaphoreType.DMA((5,)),
        ],
        compiler_params=pltpu.CompilerParams(vmem_limit_bytes=BIG),
        name="yee",
    )(
        e, h, material, col_halo, row_halo,
        eps_table, jnp.swapaxes(src_pos, 0, 1), src_amp[None, :],
    )
    return out


SIN = (-1.0 / 6.0, 1.0 / 120.0, -1.0 / 5040.0, 1.0 / 362880.0)
COS = (-0.5, 1.0 / 24.0, -1.0 / 720.0, 1.0 / 40320.0, -1.0 / 3628800.0)


def unit(phase, period):
    eighth = period // 8
    turn = phase & (period - 1)
    quarter = (turn + eighth) // (2 * eighth)
    x = (turn - quarter * (2 * eighth)).astype(jnp.float32) * (2.0 * math.pi / period)
    square = x * x
    sine = jnp.full_like(x, SIN[-1])
    for factor in SIN[-2::-1]:
        sine = sine * square + factor
    sine = x + x * (square * sine)
    cosine = jnp.full_like(x, COS[-1])
    for factor in COS[-2::-1]:
        cosine = cosine * square + factor
    cosine = 1.0 + square * cosine
    odd = (quarter & 1) == 1
    re = jnp.where(odd, sine, cosine)
    im = jnp.where(odd, cosine, sine)
    re = jnp.where(((quarter + 1) & 2) == 2, -re, re)
    im = jnp.where((quarter & 2) == 2, im, -im)
    return re, im


def far_kernel(grid_rows, grid_cols, mix, *rest):
    sd, out, rest = rest[:SETS], rest[SETS], rest[SETS + 1 :]
    x_tab, y_tab, v, g, left, held, got, *sems = rest
    send_v, recv_v, send_g, recv_g, send_f, recv_f = sems
    gx, gy = lax.axis_size("gx"), lax.axis_size("gy")
    i, z = lax.axis_index("gx"), lax.axis_index("gy")
    me = i * gy + z
    count = gx * gy
    rows = grid_rows // gx
    cols = grid_cols // gy
    per = v.shape[2] // LANES
    split = 2 * EACH // per
    slabs = cols // LANES
    own = x_tab.shape[1]
    nper = own // 2
    vb = NA // gy
    mesh_id = pl.DeviceIdType.MESH

    barrier = pltpu.get_barrier_semaphore()
    for offset in range(1, count):
        peer = lax.rem(me + offset, count)
        pl.semaphore_signal(
            barrier, inc=1, device_id=(lax.div(peer, gy), lax.rem(peer, gy)), device_id_type=mesh_id
        )
    pl.semaphore_wait(barrier, count - 1)

    def v_copy(s, offset):
        peer = lax.rem(i + offset, gx)
        here = pl.ds(pl.multiple_of(i * rows, rows), rows)
        return pltpu.make_async_remote_copy(
            src_ref=sd[s].at[peer],
            dst_ref=v.at[s, here],
            send_sem=send_v.at[s, offset],
            recv_sem=recv_v.at[s, offset],
            device_id=(peer, z),
            device_id_type=mesh_id,
        )

    def v_own(s):
        here = pl.ds(pl.multiple_of(i * rows, rows), rows)
        return pltpu.make_async_copy(sd[s].at[i], v.at[s, here], recv_v.at[s, 0])

    def g_place(s):
        share = lax.rem(i, split) * per
        lane = (z * slabs + lax.div(i, split)) * LANES
        return left.at[s, pl.ds(share, per), :, pl.ds(pl.multiple_of(lane, LANES), LANES)]

    def g_part(s, peer):
        return g.at[s, :, pl.ds(pl.multiple_of(peer * own, own), own), :]

    def g_copy(s, peer):
        offset = lax.rem(peer - me + count, count)
        return pltpu.make_async_remote_copy(
            src_ref=g_part(s, peer),
            dst_ref=g_place(s),
            send_sem=send_g.at[s, offset],
            recv_sem=recv_g.at[s, offset],
            device_id=(lax.div(peer, gy), lax.rem(peer, gy)),
            device_id_type=mesh_id,
        )

    def g_own(s):
        return pltpu.make_async_copy(g_part(s, me), g_place(s), recv_g.at[s, 0])

    def f_copy(s, offset):
        peer = lax.rem(z + offset, gy)
        return pltpu.make_async_remote_copy(
            src_ref=held.at[s, peer],
            dst_ref=got.at[s, z],
            send_sem=send_f.at[s, offset],
            recv_sem=recv_f.at[s, offset],
            device_id=(i, peer),
            device_id_type=mesh_id,
        )

    def build_x():
        low = lax.broadcasted_iota(jnp.int32, (nper, LANES), 1)
        row = lax.broadcasted_iota(jnp.int32, (nper, LANES), 0) - NA // 2

        def body(d, carry):
            u = row + d * nper
            a_re, a_im = unit(u * (low * LANES), zoom_factor * grid_rows)
            b_re, b_im = unit(u * low, zoom_factor * grid_rows)
            for block in range(grid_rows // LANES):
                h_re, h_im = a_re[:, block : block + 1], a_im[:, block : block + 1]
                re = h_re * b_re - h_im * b_im
                im = h_re * b_im + h_im * b_re
                both = jnp.concatenate([re, im], 0).astype(jnp.bfloat16)
                x_tab[d, :, block * LANES : (block + 1) * LANES] = both
            return carry

        lax.fori_loop(0, count, body, 0)

    def build_y():
        tall = 32
        low = lax.broadcasted_iota(jnp.int32, (tall, LANES), 1)
        row = lax.broadcasted_iota(jnp.int32, (tall, LANES), 0)

        def body(d, carry):
            start = pl.multiple_of(d * tall, tall)
            y = row + start
            a_re, a_im = unit(y * (low * LANES + NA // 4), zoom_factor * grid_cols)
            b_re, b_im = unit(y * low, zoom_factor * grid_cols)
            for block in range(NA // LANES):
                h_re, h_im = a_re[:, block : block + 1], a_im[:, block : block + 1]
                at = slice(block * LANES, (block + 1) * LANES)
                y_tab[0, pl.ds(start, tall), at] = (h_re * b_re - h_im * b_im).astype(jnp.bfloat16)
                y_tab[1, pl.ds(start, tall), at] = (h_re * b_im + h_im * b_re).astype(jnp.bfloat16)
            return carry

        lax.fori_loop(0, grid_cols // tall, body, 0)

    dot = functools.partial(jnp.dot, preferred_element_type=jnp.float32)
    group = 2 * gy
    parts = count // group

    def transform_rows(s):
        v_own(s).wait()
        for offset in range(1, gx):
            v_copy(s, offset).wait_recv()

        def body(c, carry):
            chunk = lax.rem(lax.div(me, group) + 1 + c, parts)
            block = x_tab[pl.ds(chunk * group, group)].reshape(group * own, grid_rows)
            both = dot(block, v[s]).astype(jnp.bfloat16)
            here = pl.ds(pl.multiple_of(chunk * (group * own), group * own), group * own)
            for f in range(per):
                g[s, f, here, :] = both[:, f * LANES : (f + 1) * LANES]
            for e in range(group):
                peer = chunk * group + e

                @pl.when(peer != me)
                def _():
                    g_copy(s, peer).start()

                @pl.when(peer == me)
                def _():
                    g_own(s).start()

            return carry

        lax.fori_loop(0, parts, body, 0)

    def transform_cols(s):
        g_own(s).wait()
        for offset in range(1, count):
            g_copy(s, lax.rem(me + offset, count)).wait_recv()
        lhs = left[s].reshape(2 * EACH * own, grid_cols)
        for step in range(1, gy + 1):
            peer = lax.rem(z + step, gy)
            at = pl.ds(pl.multiple_of(peer * vb, vb), vb)
            p_re = dot(lhs, y_tab[0, :, at])
            p_im = dot(lhs, y_tab[1, :, at])
            for f in range(2 * EACH):
                top = slice(f * own, f * own + nper)
                low = slice(f * own + nper, (f + 1) * own)
                re = (p_re[top] - p_im[low]).astype(jnp.bfloat16)
                im = (p_im[top] + p_re[low]).astype(jnp.bfloat16)
                if step < gy:
                    held[s, peer, f, 0] = re
                    held[s, peer, f, 1] = im
                else:
                    got[s, z, f, 0] = re
                    got[s, z, f, 1] = im
            if step < gy:
                f_copy(s, step).start()

    for s in range(SETS):
        v_own(s).start()
        for offset in range(1, gx):
            v_copy(s, offset).start()
    build_x()
    transform_rows(0)
    build_y()
    for s in range(1, SETS):
        transform_rows(s)
    for s in range(SETS):
        transform_cols(s)
    for s in range(SETS):
        for offset in range(1, gy):
            f_copy(s, offset).wait_recv()
        for src in range(gy):
            at = slice(src * nper, (src + 1) * nper)
            for k in range(EACH):
                s_re = got[s, src, k, 0].astype(jnp.float32)
                s_im = got[s, src, k, 1].astype(jnp.float32)
                d_re = got[s, src, EACH + k, 0].astype(jnp.float32)
                d_im = got[s, src, EACH + k, 1].astype(jnp.float32)
                for f in range(NF):
                    p_re, p_im, q_re, q_im = (mix[f, t] for t in range(4))
                    item = f * 4 + s * EACH + k
                    out[item, 0, at, :] = p_re * s_re - p_im * s_im + (q_re * d_re - q_im * d_im)
                    out[item, 1, at, :] = p_re * s_im + p_im * s_re + (q_re * d_im + q_im * d_re)
    for s in range(SETS):
        for offset in range(1, gx):
            v_copy(s, offset).wait_send()
        for offset in range(1, count):
            g_copy(s, lax.rem(me + offset, count)).wait_send()
        for offset in range(1, gy):
            f_copy(s, offset).wait_send()


def far(sd, freqs, grid_rows, grid_cols):
    gx, gy = lax.axis_size("gx"), lax.axis_size("gy")
    count = gx * gy
    nu, vb, nper = NA // gx, NA // gy, NA // count
    wide = sd[0].shape[2]
    bf16 = jnp.bfloat16
    turn_re, turn_im = jnp.cos(1.5 * freqs), jnp.sin(1.5 * freqs)
    half_re, half_im = jnp.cos(0.5 * freqs), jnp.sin(0.5 * freqs)
    mix = jnp.stack(
        [turn_re * half_re, turn_im * half_re, -turn_im * half_im, turn_re * half_im], 1
    ) * (1.0 / math.sqrt(grid_rows * grid_cols))
    dma = pltpu.SemaphoreType.DMA
    done = pl.pallas_call(
        functools.partial(far_kernel, grid_rows, grid_cols),
        out_shape=jax.ShapeDtypeStruct((NF * 4, 2, nu, vb), jnp.float32),
        in_specs=[SM] + [ANY] * SETS,
        out_specs=VM,
        scratch_shapes=[
            pltpu.VMEM((count, 2 * nper, grid_rows), bf16),
            pltpu.VMEM((2, grid_cols, NA), bf16),
            pltpu.VMEM((SETS, grid_rows, wide), bf16),
            pltpu.VMEM((SETS, wide // LANES, 2 * NA, LANES), bf16),
            pltpu.VMEM((SETS, 2 * EACH, 2 * nper, grid_cols), bf16),
            pltpu.VMEM((SETS, gy, 2 * EACH, 2, nper, vb), bf16),
            pltpu.VMEM((SETS, gy, 2 * EACH, 2, nper, vb), bf16),
            dma((SETS, gx)),
            dma((SETS, gx)),
            dma((SETS, count)),
            dma((SETS, count)),
            dma((SETS, gy)),
            dma((SETS, gy)),
        ],
        compiler_params=pltpu.CompilerParams(
            vmem_limit_bytes=BIG, collective_id=1, has_side_effects=True
        ),
        name="far",
    )(mix, *sd)
    return jnp.transpose(done, (2, 0, 1, 3))


def on_device(e_field, h_field, material, eps_table, src_pos, src_amp, freqs):
    rows, cols = material.shape[1:]
    grid_rows, grid_cols = rows * lax.axis_size("gx"), cols * lax.axis_size("gy")
    e_new, h_new, *sd = yee(e_field, h_field, material, eps_table, src_pos, src_amp)
    shape = e_field.shape
    return (e_new.reshape(shape), h_new.reshape(shape), far(sd, freqs, grid_rows, grid_cols))


def solution(mesh):
    placed = (
        P(None, None, "gx", "gy"),
        P(None, None, "gx", "gy"),
        P(None, "gx", "gy"),
        P(),
        P(),
        P(),
        P(),
    )
    return jax.shard_map(
        on_device,
        mesh=mesh,
        in_specs=placed,
        out_specs=(P(None, None, "gx", "gy"), P(None, None, "gx", "gy"), P("gx", None, None, "gy")),
        check_vma=False,
    )
```

```python
import functools
import math

import jax
import jax.numpy as jnp
from jax import lax
from jax.experimental import pallas as pl
from jax.experimental.pallas import tpu as pltpu
from jax.sharding import PartitionSpec as P

LZ = 3
FACE = 1
STEPS = 2
NF = 2
NA = 1024
NMAT = 8

courant = 0.5
source_rate = 0.7
zoom_factor = 4

BASE = 32
CHUNK = 16
SETS = 2
EACH = 4 // SETS
LANES = 128
PAD = 128
ANY = pl.BlockSpec(memory_space=pl.ANY)
VM = pl.BlockSpec(memory_space=pltpu.VMEM)
SM = pl.BlockSpec(memory_space=pltpu.SMEM)
BIG = 60 * 1024 * 1024


def halo_kernel(
    e, h, m, col_rim, corner, rim_f, rim_m,
    edge_f, edge_m, packed, got_col, got_corner, got_f, got_m, load, send, recv,
):
    gx, gy = lax.axis_size("gx"), lax.axis_size("gy")
    i, z = lax.axis_index("gx"), lax.axis_index("gy")
    planes, rows, cols = e.shape
    around = [(a, b) for a in (-1, 0, 1) for b in (-1, 0, 1) if (a, b) != (0, 0)]

    def exists(step):
        row, col = i + step[0], z + step[1]
        return (row >= 0) & (row < gx) & (col >= 0) & (col < gy)

    loads = []
    for side, lane in enumerate((0, cols - LANES)):
        at = pl.ds(lane, LANES)
        loads.append(pltpu.make_async_copy(e.at[:, :, at], edge_f.at[side, pl.ds(0, planes)], load.at[3 * side]))
        loads.append(pltpu.make_async_copy(h.at[:, :, at], edge_f.at[side, pl.ds(planes, planes)], load.at[3 * side + 1]))
        loads.append(pltpu.make_async_copy(m.at[:, :, at], edge_m.at[side], load.at[3 * side + 2]))
    for copy in loads:
        copy.start()
    barrier = pltpu.get_barrier_semaphore()
    total = jnp.int32(0)
    for step in around:
        total += exists(step).astype(jnp.int32)

        @pl.when(exists(step))
        def _():
            pl.semaphore_signal(
                barrier, inc=1, device_id=(i + step[0], z + step[1]), device_id_type=pl.DeviceIdType.MESH
            )

    pl.semaphore_wait(barrier, total)

    def remote(step, src, dst, index):
        copy = pltpu.make_async_remote_copy(
            src_ref=src, dst_ref=dst, send_sem=send.at[index], recv_sem=recv.at[index],
            device_id=(i + step[0], z + step[1]), device_id_type=pl.DeviceIdType.MESH,
        )
        return step, copy

    rows_out, cols_out = [], []
    for side, low in enumerate((0, rows - 8)):
        step = (2 * side - 1, 0)
        at = pl.ds(low, 8)
        rows_out.append(remote(step, e.at[:, at, :], got_f.at[side, pl.ds(0, planes)], 3 * side))
        rows_out.append(remote(step, h.at[:, at, :], got_f.at[side, pl.ds(planes, planes)], 3 * side + 1))
        rows_out.append(remote(step, m.at[:, at, :], got_m.at[side], 3 * side + 2))
    for side in range(2):
        cols_out.append(remote((0, 2 * side - 1), packed.at[side], got_col.at[side], 6 + side))
        for end, low in enumerate((0, rows - 8)):
            step = (2 * end - 1, 2 * side - 1)
            src = packed.at[side, pl.ds(low, 8)]
            cols_out.append(remote(step, src, got_corner.at[end, side], 8 + 2 * side + end))

    def start(copies):
        for step, copy in copies:

            @pl.when(exists(step))
            def _():
                copy.start()

    start(rows_out)
    for copy in loads:
        copy.wait()
    tall = 32
    lane = lax.broadcasted_iota(jnp.int32, (tall, LANES), 1)

    def pack(c, carry):
        at = pl.ds(pl.multiple_of(c * tall, tall), tall)
        for side in range(2):
            place = ((lane + 2 * side) & (LANES - 1)) >> 2
            block = jnp.zeros((tall, LANES), jnp.float32)
            for p in range(2 * planes + LZ):
                if p < 2 * planes:
                    piece = edge_f[side, p, at, :]
                else:
                    piece = edge_m[side, p - 2 * planes, at, :].astype(jnp.float32)
                block = jnp.where(place == p, pltpu.roll(piece, 4 * p, 1), block)
            packed[side, at, :] = block
        return carry

    lax.fori_loop(0, rows // tall, pack, 0)
    start(cols_out)
    for step, copy in rows_out + cols_out:

        @pl.when(exists((-step[0], -step[1])))
        def _():
            copy.wait_recv()

    last = (lane & 2) == 0
    after, before = exists((0, 1)), exists((0, -1))

    def merge(c, carry):
        at = pl.ds(pl.multiple_of(c * tall, tall), tall)
        right = jnp.where(after, got_col[0, at, :], 0.0)
        left = jnp.where(before, got_col[1, at, :], 0.0)
        col_rim[at, :] = jnp.where(last, right, left)
        return carry

    lax.fori_loop(0, rows // tall, merge, 0)
    for side in range(2):
        there = exists((1 - 2 * side, 0))
        rim_f[side] = jnp.where(there, got_f[side], 0.0)
        rim_m[side] = jnp.where(there, got_m[side], 0)
        right = jnp.where(there & after, got_corner[side, 0], 0.0)
        left = jnp.where(there & before, got_corner[side, 1], 0.0)
        corner[side] = jnp.where(last[:8], right, left)
    for step, copy in rows_out + cols_out:

        @pl.when(exists(step))
        def _():
            copy.wait_send()


def halo(e, h, m):
    planes, rows, cols = e.shape
    f32, i32 = jnp.float32, jnp.int32
    dma = pltpu.SemaphoreType.DMA
    return pl.pallas_call(
        halo_kernel,
        out_shape=(
            jax.ShapeDtypeStruct((rows, LANES), f32),
            jax.ShapeDtypeStruct((2, 8, LANES), f32),
            jax.ShapeDtypeStruct((2, 2 * planes, 8, cols), f32),
            jax.ShapeDtypeStruct((2, LZ, 8, cols), i32),
        ),
        in_specs=[ANY] * 3,
        out_specs=(VM,) * 4,
        scratch_shapes=[
            pltpu.VMEM((2, 2 * planes, rows, LANES), f32),
            pltpu.VMEM((2, LZ, rows, LANES), i32),
            pltpu.VMEM((2, rows, LANES), f32),
            pltpu.VMEM((2, rows, LANES), f32),
            pltpu.VMEM((2, 2, 8, LANES), f32),
            pltpu.VMEM((2, 2 * planes, 8, cols), f32),
            pltpu.VMEM((2, LZ, 8, cols), i32),
            dma((6,)),
            dma((12,)),
            dma((12,)),
        ],
        compiler_params=pltpu.CompilerParams(collective_id=0, has_side_effects=True),
        name="halo",
    )(e, h, m)


def fields_per_device(gx, cols):
    return 2 * EACH * cols // (gx * LANES)


def yee_kernel(
    grid_rows, grid_cols, per,
    e_hbm, h_hbm, m_hbm, col_rim, corner, rim_f, rim_m, eps, pos, amp,
    e_out, h_out, *rest,
):
    sd_outs, (e_ext, h_ext, m_main, scale, src, first, sems) = rest[:SETS], rest[SETS:]
    rows, cols = m_main.shape[1:]
    width = cols + PAD
    high = e_ext.shape[1]
    row0 = lax.axis_index("gx") * rows
    col0 = lax.axis_index("gy") * cols
    main_r = pl.ds(BASE, rows)
    copies = [
        pltpu.make_async_copy(e_hbm, e_ext.at[:, main_r, pl.ds(0, cols)], sems.at[0]),
        pltpu.make_async_copy(h_hbm, h_ext.at[:, main_r, pl.ds(0, cols)], sems.at[1]),
        pltpu.make_async_copy(m_hbm, m_main, sems.at[2]),
    ]
    for copy in copies:
        copy.start()
    count = amp.shape[1]
    step = min(count, 1024)
    used = high - 2 * CHUNK
    row_at = row0 + lax.broadcasted_iota(jnp.int32, (used, step), 0) + (CHUNK - BASE)
    lane = lax.broadcasted_iota(jnp.int32, (width, step), 0)
    col_at = col0 + jnp.where(lane < cols + PAD // 2, lane, lane - width)
    for start in range(0, count, step):
        at = pl.ds(start, step)
        amp_now = amp[:, at]
        hi = amp_now.astype(jnp.bfloat16).astype(jnp.float32)
        mid = (amp_now - hi).astype(jnp.bfloat16).astype(jnp.float32)
        low = amp_now - hi - mid
        hit_col = jnp.where(col_at == pos[2:3, at], 1.0, 0.0).astype(jnp.bfloat16)
        hit_row = row_at == pos[1:2, at]
        for layer in range(LZ):
            hit = hit_row & (pos[0:1, at] == layer)
            total = None
            for piece in (hi, mid, low):
                left = jnp.where(hit, piece, 0.0).astype(jnp.bfloat16)
                term = lax.dot_general(
                    left, hit_col, (((1,), (1,)), ((), ())), preferred_element_type=jnp.float32
                )
                total = term if total is None else total + term
            if start == 0:
                src[layer, CHUNK : CHUNK + used, :] = total
            else:
                src[layer, CHUNK : CHUNK + used, :] += total
    copies[2].wait()

    def scale_of(index, row, col):
        value = jnp.full(index.shape, eps[0], jnp.float32)
        for material in range(1, NMAT):
            value = jnp.where(index == material, eps[material], value)
        inside = (row >= 0) & (row < grid_rows) & (col >= 0) & (col < grid_cols)
        return jnp.where(inside, courant / value, 0.0)

    col_main = col0 + lax.broadcasted_iota(jnp.int32, (CHUNK, cols), 1)
    lane_pad = lax.broadcasted_iota(jnp.int32, (CHUNK, PAD), 1)
    col_pad = col0 + jnp.where(lane_pad < PAD // 2, cols + lane_pad, lane_pad - PAD)
    row_chunk = row0 + lax.broadcasted_iota(jnp.int32, (CHUNK, cols), 0)

    def shown(block, plane):
        return pltpu.roll(block, PAD - 4 * plane, 1) if plane else block

    def fill(step_index, carry):
        r = pl.multiple_of(step_index * CHUNK, CHUNK)
        near = pl.ds(r, CHUNK)
        far = pl.ds(BASE + r, CHUNK)
        block = col_rim[near, :]
        for layer in range(LZ):
            scale[layer, far, :cols] = scale_of(m_main[layer, near, :], row_chunk + r, col_main)
            scale[layer, far, cols:] = scale_of(
                shown(block, 6 * LZ + layer), row_chunk[:, :PAD] + r, col_pad
            )
        for plane in range(3 * LZ):
            e_ext[plane, far, cols:] = shown(block, plane)
            h_ext[plane, far, cols:] = shown(block, 3 * LZ + plane)
        return carry

    lax.fori_loop(0, rows // CHUNK, fill, 0)
    row_eight = row0 + lax.broadcasted_iota(jnp.int32, (8, cols), 0)
    blank = jnp.zeros((8, width), jnp.float32)
    for side, target, offset, spare in (
        (0, BASE + rows, rows, BASE + rows + 8),
        (1, BASE - 8, -8, BASE - 16),
    ):
        here = slice(target, target + 8)
        block = corner[side]
        for layer in range(LZ):
            scale[layer, here, :cols] = scale_of(
                rim_m[side, layer], row_eight + offset, col_main[:8]
            )
            scale[layer, here, cols:] = scale_of(
                shown(block, 6 * LZ + layer), row_eight[:, :PAD] + offset, col_pad[:8]
            )
            scale[layer, spare : spare + 8, :] = blank
        for plane in range(3 * LZ):
            e_ext[plane, here, :cols] = rim_f[side, plane]
            h_ext[plane, here, :cols] = rim_f[side, 3 * LZ + plane]
            e_ext[plane, here, cols:] = shown(block, plane)
            h_ext[plane, here, cols:] = shown(block, 3 * LZ + plane)
            e_ext[plane, spare : spare + 8, :] = blank
            h_ext[plane, spare : spare + 8, :] = blank
    for plane in range(3 * LZ):
        e_ext[plane, high - 16 : high, :] = jnp.zeros((16, width), jnp.float32)
        h_ext[plane, 0:16, :] = jnp.zeros((16, width), jnp.float32)
    lane_c = lax.broadcasted_iota(jnp.int32, (CHUNK, width), 1)
    col_c = col0 + jnp.where(lane_c < cols + PAD // 2, lane_c, lane_c - width)
    weight = jnp.where(col_c >= 0, courant, 0.0)
    top = lax.axis_index("gx") == 0
    copies[0].wait()
    copies[1].wait()

    def magnetic_pass(index, carry):
        r = pl.multiple_of(index * CHUNK, CHUNK)
        now = pl.ds(r, CHUNK)
        more = pl.ds(r, CHUNK + 8)
        factor = weight * jnp.where(top & (index * CHUNK < BASE), 0.0, 1.0)
        zero = jnp.zeros((CHUNK, width), jnp.float32)
        ex = [e_ext[layer, now, :] for layer in range(LZ)] + [zero]
        ey = [e_ext[LZ + layer, now, :] for layer in range(LZ)] + [zero]
        for layer in range(LZ):
            ez = e_ext[2 * LZ + layer, now, :]
            ez_row = pltpu.roll(e_ext[2 * LZ + layer, more, :], CHUNK + 7, 0)[:CHUNK]
            ey_row = pltpu.roll(e_ext[LZ + layer, more, :], CHUNK + 7, 0)[:CHUNK]
            ez_col = pltpu.roll(ez, width - 1, 1)
            ex_col = pltpu.roll(ex[layer], width - 1, 1)
            curl_x = ez_col - ez - (ey[layer + 1] - ey[layer])
            curl_y = ex[layer + 1] - ex[layer] - (ez_row - ez)
            curl_z = ey_row - ey[layer] - (ex_col - ex[layer])
            for part, curl in enumerate((curl_x, curl_y, curl_z)):
                plane = part * LZ + layer
                h_ext[plane, now, :] = h_ext[plane, now, :] - factor * curl
        return carry

    def electric_pass(moment, last, index, carry):
        r = pl.multiple_of(index * CHUNK, CHUNK)
        now = pl.ds(r, CHUNK)
        more = pl.ds(pl.multiple_of(r - 8, 8), CHUNK + 8)
        drive = math.sin(source_rate * moment)
        zero = jnp.zeros((CHUNK, width), jnp.float32)
        hx = [zero] + [h_ext[layer, now, :] for layer in range(LZ)]
        hy = [zero] + [h_ext[LZ + layer, now, :] for layer in range(LZ)]
        for layer in range(LZ):
            hz = h_ext[2 * LZ + layer, now, :]
            hz_row = pltpu.roll(h_ext[2 * LZ + layer, more, :], 1, 0)[8:]
            hy_row = pltpu.roll(h_ext[LZ + layer, more, :], 1, 0)[8:]
            hx_now, hy_now = hx[layer + 1], hy[layer + 1]
            hz_col = pltpu.roll(hz, 1, 1)
            hx_col = pltpu.roll(hx_now, 1, 1)
            curl_x = hz - hz_col - (hy_now - hy[layer])
            curl_y = hx_now - hx[layer] - (hz - hz_row)
            curl_z = hy_now - hy_row - (hx_now - hx_col)
            factor = scale[layer, now, :]
            new_x = e_ext[layer, now, :] + factor * curl_x
            new_y = e_ext[LZ + layer, now, :] + factor * curl_y
            new_z = e_ext[2 * LZ + layer, now, :] + factor * curl_z + drive * src[layer, now, :]
            e_ext[layer, now, :] = new_x
            e_ext[LZ + layer, now, :] = new_y
            e_ext[2 * LZ + layer, now, :] = new_z
            if layer == FACE:
                faces = (-hy_now, hx_now, new_y, -new_x)
                for item, face in enumerate(faces):
                    if last:
                        old = first[item, now, :]
                        here = pl.ds(r - BASE, CHUNK)
                        for which, value in enumerate((old + face, face - old)):
                            share, place = divmod(which * EACH + item % EACH, per)
                            for q in range(cols // LANES):
                                piece = value[:, q * LANES : (q + 1) * LANES].astype(jnp.bfloat16)
                                lanes = pl.ds(place * LANES, LANES)
                                sd_outs[item // EACH][q * (2 * EACH // per) + share, here, lanes] = piece
                    else:
                        first[item, now, :] = face
        return carry

    chunks = high // CHUNK
    main0 = BASE // CHUNK
    main1 = main0 + rows // CHUNK
    lax.fori_loop(1, chunks - 1, magnetic_pass, 0)
    lax.fori_loop(1, chunks - 1, functools.partial(electric_pass, 1.0, False), 0)
    lax.fori_loop(1, main1, magnetic_pass, 0)
    out_h = pltpu.make_async_copy(h_ext.at[:, main_r, pl.ds(0, cols)], h_out, sems.at[3])
    out_h.start()
    lax.fori_loop(main0, main1, functools.partial(electric_pass, 2.0, True), 0)
    out_e = pltpu.make_async_copy(e_ext.at[:, main_r, pl.ds(0, cols)], e_out, sems.at[4])
    out_e.start()
    out_h.wait()
    out_e.wait()


def yee(e_field, h_field, material, eps_table, src_pos, src_amp):
    rows, cols = material.shape[1:]
    gx = lax.axis_size("gx")
    per = fields_per_device(gx, cols)
    grid_rows = rows * gx
    grid_cols = cols * lax.axis_size("gy")
    planes = 3 * LZ
    e = e_field.reshape(planes, rows, cols)
    h = h_field.reshape(planes, rows, cols)

    high = rows + 2 * BASE
    width = cols + PAD
    f32 = jnp.float32
    out = pl.pallas_call(
        functools.partial(yee_kernel, grid_rows, grid_cols, per),
        out_shape=(
            jax.ShapeDtypeStruct((planes, rows, cols), f32),
            jax.ShapeDtypeStruct((planes, rows, cols), f32),
        )
        + (jax.ShapeDtypeStruct((gx, rows, per * LANES), jnp.bfloat16),) * SETS,
        in_specs=[ANY, ANY, ANY, VM, VM, VM, VM, SM, VM, VM],
        out_specs=(ANY, ANY) + (VM,) * SETS,
        scratch_shapes=[
            pltpu.VMEM((planes, high, width), f32),
            pltpu.VMEM((planes, high, width), f32),
            pltpu.VMEM((LZ, rows, cols), jnp.int32),
            pltpu.VMEM((LZ, high, width), f32),
            pltpu.VMEM((LZ, high, width), f32),
            pltpu.VMEM((4, high, width), f32),
            pltpu.SemaphoreType.DMA((5,)),
        ],
        compiler_params=pltpu.CompilerParams(vmem_limit_bytes=BIG),
        name="yee",
    )(
        e, h, material, *halo(e, h, material),
        eps_table, jnp.swapaxes(src_pos, 0, 1), src_amp[None, :],
    )
    return out


SIN = (-1.0 / 6.0, 1.0 / 120.0, -1.0 / 5040.0, 1.0 / 362880.0)
COS = (-0.5, 1.0 / 24.0, -1.0 / 720.0, 1.0 / 40320.0, -1.0 / 3628800.0)


def unit(phase, period):
    eighth = period // 8
    turn = phase & (period - 1)
    quarter = (turn + eighth) // (2 * eighth)
    x = (turn - quarter * (2 * eighth)).astype(jnp.float32) * (2.0 * math.pi / period)
    square = x * x
    sine = jnp.full_like(x, SIN[-1])
    for factor in SIN[-2::-1]:
        sine = sine * square + factor
    sine = x + x * (square * sine)
    cosine = jnp.full_like(x, COS[-1])
    for factor in COS[-2::-1]:
        cosine = cosine * square + factor
    cosine = 1.0 + square * cosine
    odd = (quarter & 1) == 1
    re = jnp.where(odd, sine, cosine)
    im = jnp.where(odd, cosine, sine)
    re = jnp.where(((quarter + 1) & 2) == 2, -re, re)
    im = jnp.where((quarter & 2) == 2, im, -im)
    return re, im


def far_kernel(grid_rows, grid_cols, mix, *rest):
    sd, out, rest = rest[:SETS], rest[SETS], rest[SETS + 1 :]
    x_tab, y_tab, v, g, left, held, got, *sems = rest
    send_v, recv_v, send_g, recv_g, send_f, recv_f = sems
    gx, gy = lax.axis_size("gx"), lax.axis_size("gy")
    i, z = lax.axis_index("gx"), lax.axis_index("gy")
    me = i * gy + z
    count = gx * gy
    rows = grid_rows // gx
    cols = grid_cols // gy
    per = v.shape[2] // LANES
    split = 2 * EACH // per
    slabs = cols // LANES
    own = x_tab.shape[1]
    nper = own // 2
    vb = NA // gy
    mesh_id = pl.DeviceIdType.MESH

    barrier = pltpu.get_barrier_semaphore()
    for offset in range(1, count):
        peer = lax.rem(me + offset, count)
        pl.semaphore_signal(
            barrier, inc=1, device_id=(lax.div(peer, gy), lax.rem(peer, gy)), device_id_type=mesh_id
        )
    pl.semaphore_wait(barrier, count - 1)

    def v_copy(s, offset):
        peer = lax.rem(i + offset, gx)
        here = pl.ds(pl.multiple_of(i * rows, rows), rows)
        return pltpu.make_async_remote_copy(
            src_ref=sd[s].at[peer],
            dst_ref=v.at[s, here],
            send_sem=send_v.at[s, offset],
            recv_sem=recv_v.at[s, offset],
            device_id=(peer, z),
            device_id_type=mesh_id,
        )

    def v_own(s):
        here = pl.ds(pl.multiple_of(i * rows, rows), rows)
        return pltpu.make_async_copy(sd[s].at[i], v.at[s, here], recv_v.at[s, 0])

    def g_place(s):
        share = lax.rem(i, split) * per
        lane = (z * slabs + lax.div(i, split)) * LANES
        return left.at[s, pl.ds(share, per), :, pl.ds(pl.multiple_of(lane, LANES), LANES)]

    def g_part(s, peer):
        return g.at[s, :, pl.ds(pl.multiple_of(peer * own, own), own), :]

    def g_copy(s, peer):
        offset = lax.rem(peer - me + count, count)
        return pltpu.make_async_remote_copy(
            src_ref=g_part(s, peer),
            dst_ref=g_place(s),
            send_sem=send_g.at[s, offset],
            recv_sem=recv_g.at[s, offset],
            device_id=(lax.div(peer, gy), lax.rem(peer, gy)),
            device_id_type=mesh_id,
        )

    def g_own(s):
        return pltpu.make_async_copy(g_part(s, me), g_place(s), recv_g.at[s, 0])

    def f_copy(s, offset):
        peer = lax.rem(z + offset, gy)
        return pltpu.make_async_remote_copy(
            src_ref=held.at[s, peer],
            dst_ref=got.at[s, z],
            send_sem=send_f.at[s, offset],
            recv_sem=recv_f.at[s, offset],
            device_id=(i, peer),
            device_id_type=mesh_id,
        )

    def build_x():
        low = lax.broadcasted_iota(jnp.int32, (nper, LANES), 1)
        row = lax.broadcasted_iota(jnp.int32, (nper, LANES), 0) - NA // 2

        def body(d, carry):
            u = row + d * nper
            a_re, a_im = unit(u * (low * LANES), zoom_factor * grid_rows)
            b_re, b_im = unit(u * low, zoom_factor * grid_rows)
            for block in range(grid_rows // LANES):
                h_re, h_im = a_re[:, block : block + 1], a_im[:, block : block + 1]
                re = h_re * b_re - h_im * b_im
                im = h_re * b_im + h_im * b_re
                both = jnp.concatenate([re, im], 0).astype(jnp.bfloat16)
                x_tab[d, :, block * LANES : (block + 1) * LANES] = both
            return carry

        lax.fori_loop(0, count, body, 0)

    def build_y():
        tall = 32
        low = lax.broadcasted_iota(jnp.int32, (tall, LANES), 1)
        row = lax.broadcasted_iota(jnp.int32, (tall, LANES), 0)

        def body(d, carry):
            start = pl.multiple_of(d * tall, tall)
            y = row + start
            a_re, a_im = unit(y * (low * LANES + NA // 4), zoom_factor * grid_cols)
            b_re, b_im = unit(y * low, zoom_factor * grid_cols)
            for block in range(NA // LANES):
                h_re, h_im = a_re[:, block : block + 1], a_im[:, block : block + 1]
                at = slice(block * LANES, (block + 1) * LANES)
                y_tab[0, pl.ds(start, tall), at] = (h_re * b_re - h_im * b_im).astype(jnp.bfloat16)
                y_tab[1, pl.ds(start, tall), at] = (h_re * b_im + h_im * b_re).astype(jnp.bfloat16)
            return carry

        lax.fori_loop(0, grid_cols // tall, body, 0)

    dot = functools.partial(jnp.dot, preferred_element_type=jnp.float32)
    group = 2 * gy
    parts = count // group

    def transform_rows(s):
        v_own(s).wait()
        for offset in range(1, gx):
            v_copy(s, offset).wait_recv()

        def body(c, carry):
            chunk = lax.rem(lax.div(me, group) + 1 + c, parts)
            block = x_tab[pl.ds(chunk * group, group)].reshape(group * own, grid_rows)
            both = dot(block, v[s]).astype(jnp.bfloat16)
            here = pl.ds(pl.multiple_of(chunk * (group * own), group * own), group * own)
            for f in range(per):
                g[s, f, here, :] = both[:, f * LANES : (f + 1) * LANES]
            for e in range(group):
                peer = chunk * group + e

                @pl.when(peer != me)
                def _():
                    g_copy(s, peer).start()

                @pl.when(peer == me)
                def _():
                    g_own(s).start()

            return carry

        lax.fori_loop(0, parts, body, 0)

    def transform_cols(s):
        g_own(s).wait()
        for offset in range(1, count):
            g_copy(s, lax.rem(me + offset, count)).wait_recv()
        lhs = left[s].reshape(2 * EACH * own, grid_cols)
        for step in range(1, gy + 1):
            peer = lax.rem(z + step, gy)
            at = pl.ds(pl.multiple_of(peer * vb, vb), vb)
            p_re = dot(lhs, y_tab[0, :, at])
            p_im = dot(lhs, y_tab[1, :, at])
            for f in range(2 * EACH):
                top = slice(f * own, f * own + nper)
                low = slice(f * own + nper, (f + 1) * own)
                re = (p_re[top] - p_im[low]).astype(jnp.bfloat16)
                im = (p_im[top] + p_re[low]).astype(jnp.bfloat16)
                if step < gy:
                    held[s, peer, f, 0] = re
                    held[s, peer, f, 1] = im
                else:
                    got[s, z, f, 0] = re
                    got[s, z, f, 1] = im
            if step < gy:
                f_copy(s, step).start()

    for s in range(SETS):
        v_own(s).start()
        for offset in range(1, gx):
            v_copy(s, offset).start()
    build_x()
    transform_rows(0)
    build_y()
    for s in range(1, SETS):
        transform_rows(s)
    for s in range(SETS):
        transform_cols(s)
    for s in range(SETS):
        for offset in range(1, gy):
            f_copy(s, offset).wait_recv()
        for src in range(gy):
            at = slice(src * nper, (src + 1) * nper)
            for k in range(EACH):
                s_re = got[s, src, k, 0].astype(jnp.float32)
                s_im = got[s, src, k, 1].astype(jnp.float32)
                d_re = got[s, src, EACH + k, 0].astype(jnp.float32)
                d_im = got[s, src, EACH + k, 1].astype(jnp.float32)
                for f in range(NF):
                    p_re, p_im, q_re, q_im = (mix[f, t] for t in range(4))
                    item = f * 4 + s * EACH + k
                    out[item, 0, at, :] = p_re * s_re - p_im * s_im + (q_re * d_re - q_im * d_im)
                    out[item, 1, at, :] = p_re * s_im + p_im * s_re + (q_re * d_im + q_im * d_re)
    for s in range(SETS):
        for offset in range(1, gx):
            v_copy(s, offset).wait_send()
        for offset in range(1, count):
            g_copy(s, lax.rem(me + offset, count)).wait_send()
        for offset in range(1, gy):
            f_copy(s, offset).wait_send()


def far(sd, freqs, grid_rows, grid_cols):
    gx, gy = lax.axis_size("gx"), lax.axis_size("gy")
    count = gx * gy
    nu, vb, nper = NA // gx, NA // gy, NA // count
    wide = sd[0].shape[2]
    bf16 = jnp.bfloat16
    turn_re, turn_im = jnp.cos(1.5 * freqs), jnp.sin(1.5 * freqs)
    half_re, half_im = jnp.cos(0.5 * freqs), jnp.sin(0.5 * freqs)
    mix = jnp.stack(
        [turn_re * half_re, turn_im * half_re, -turn_im * half_im, turn_re * half_im], 1
    ) * (1.0 / math.sqrt(grid_rows * grid_cols))
    dma = pltpu.SemaphoreType.DMA
    done = pl.pallas_call(
        functools.partial(far_kernel, grid_rows, grid_cols),
        out_shape=jax.ShapeDtypeStruct((NF * 4, 2, nu, vb), jnp.float32),
        in_specs=[SM] + [ANY] * SETS,
        out_specs=VM,
        scratch_shapes=[
            pltpu.VMEM((count, 2 * nper, grid_rows), bf16),
            pltpu.VMEM((2, grid_cols, NA), bf16),
            pltpu.VMEM((SETS, grid_rows, wide), bf16),
            pltpu.VMEM((SETS, wide // LANES, 2 * NA, LANES), bf16),
            pltpu.VMEM((SETS, 2 * EACH, 2 * nper, grid_cols), bf16),
            pltpu.VMEM((SETS, gy, 2 * EACH, 2, nper, vb), bf16),
            pltpu.VMEM((SETS, gy, 2 * EACH, 2, nper, vb), bf16),
            dma((SETS, gx)),
            dma((SETS, gx)),
            dma((SETS, count)),
            dma((SETS, count)),
            dma((SETS, gy)),
            dma((SETS, gy)),
        ],
        compiler_params=pltpu.CompilerParams(
            vmem_limit_bytes=BIG, collective_id=1, has_side_effects=True
        ),
        name="far",
    )(mix, *sd)
    return jnp.transpose(done, (2, 0, 1, 3))


def on_device(e_field, h_field, material, eps_table, src_pos, src_amp, freqs):
    rows, cols = material.shape[1:]
    grid_rows, grid_cols = rows * lax.axis_size("gx"), cols * lax.axis_size("gy")
    e_new, h_new, *sd = yee(e_field, h_field, material, eps_table, src_pos, src_amp)
    shape = e_field.shape
    return (e_new.reshape(shape), h_new.reshape(shape), far(sd, freqs, grid_rows, grid_cols))


def solution(mesh):
    placed = (
        P(None, None, "gx", "gy"),
        P(None, None, "gx", "gy"),
        P(None, "gx", "gy"),
        P(),
        P(),
        P(),
        P(),
    )
    return jax.shard_map(
        on_device,
        mesh=mesh,
        in_specs=placed,
        out_specs=(P(None, None, "gx", "gy"), P(None, None, "gx", "gy"), P("gx", None, None, "gy")),
        check_vma=False,
    )
```

```python
import functools
import math

import jax
import jax.numpy as jnp
from jax import lax
from jax.experimental import pallas as pl
from jax.experimental.pallas import tpu as pltpu
from jax.sharding import PartitionSpec as P

LZ = 3
FACE = 1
STEPS = 2
NF = 2
NA = 1024
NMAT = 8

courant = 0.5
source_rate = 0.7
zoom_factor = 4

BASE = 32
CHUNK = 16
SETS = 2
EACH = 4 // SETS
LANES = 128
PAD = 128
ANY = pl.BlockSpec(memory_space=pl.ANY)
VM = pl.BlockSpec(memory_space=pltpu.VMEM)
SM = pl.BlockSpec(memory_space=pltpu.SMEM)
BIG = 60 * 1024 * 1024


def halo_kernel(
    e, h, m, col_rim, corner, rim_f, rim_m,
    edge_f, edge_m, packed, got_col, got_corner, got_f, got_m, load, send, recv,
):
    gx, gy = lax.axis_size("gx"), lax.axis_size("gy")
    i, z = lax.axis_index("gx"), lax.axis_index("gy")
    planes, rows, cols = e.shape
    around = [(a, b) for a in (-1, 0, 1) for b in (-1, 0, 1) if (a, b) != (0, 0)]

    def exists(step):
        row, col = i + step[0], z + step[1]
        return (row >= 0) & (row < gx) & (col >= 0) & (col < gy)

    loads = []
    for side, lane in enumerate((0, cols - LANES)):
        at = pl.ds(lane, LANES)
        loads.append(pltpu.make_async_copy(e.at[:, :, at], edge_f.at[side, pl.ds(0, planes)], load.at[3 * side]))
        loads.append(pltpu.make_async_copy(h.at[:, :, at], edge_f.at[side, pl.ds(planes, planes)], load.at[3 * side + 1]))
        loads.append(pltpu.make_async_copy(m.at[:, :, at], edge_m.at[side], load.at[3 * side + 2]))
    for copy in loads:
        copy.start()
    barrier = pltpu.get_barrier_semaphore()
    total = jnp.int32(0)
    for step in around:
        total += exists(step).astype(jnp.int32)

        @pl.when(exists(step))
        def _():
            pl.semaphore_signal(
                barrier, inc=1, device_id=(i + step[0], z + step[1]), device_id_type=pl.DeviceIdType.MESH
            )

    pl.semaphore_wait(barrier, total)

    def remote(step, src, dst, index):
        copy = pltpu.make_async_remote_copy(
            src_ref=src, dst_ref=dst, send_sem=send.at[index], recv_sem=recv.at[index],
            device_id=(i + step[0], z + step[1]), device_id_type=pl.DeviceIdType.MESH,
        )
        return step, copy

    rows_out, cols_out = [], []
    for side, low in enumerate((0, rows - 8)):
        step = (2 * side - 1, 0)
        at = pl.ds(low, 8)
        rows_out.append(remote(step, e.at[:, at, :], got_f.at[side, pl.ds(0, planes)], 3 * side))
        rows_out.append(remote(step, h.at[:, at, :], got_f.at[side, pl.ds(planes, planes)], 3 * side + 1))
        rows_out.append(remote(step, m.at[:, at, :], got_m.at[side], 3 * side + 2))
    for side in range(2):
        cols_out.append(remote((0, 2 * side - 1), packed.at[side], got_col.at[side], 6 + side))
        for end, low in enumerate((0, rows - 8)):
            step = (2 * end - 1, 2 * side - 1)
            src = packed.at[side, pl.ds(low, 8)]
            cols_out.append(remote(step, src, got_corner.at[end, side], 8 + 2 * side + end))

    def start(copies):
        for step, copy in copies:

            @pl.when(exists(step))
            def _():
                copy.start()

    start(rows_out)
    for copy in loads:
        copy.wait()
    tall = 32
    lane = lax.broadcasted_iota(jnp.int32, (tall, LANES), 1)

    def pack(c, carry):
        at = pl.ds(pl.multiple_of(c * tall, tall), tall)
        for side in range(2):
            place = ((lane + 2 * side) & (LANES - 1)) >> 2
            block = jnp.zeros((tall, LANES), jnp.float32)
            for p in range(2 * planes + LZ):
                if p < 2 * planes:
                    piece = edge_f[side, p, at, :]
                else:
                    piece = edge_m[side, p - 2 * planes, at, :].astype(jnp.float32)
                block = jnp.where(place == p, pltpu.roll(piece, 4 * p, 1), block)
            packed[side, at, :] = block
        return carry

    lax.fori_loop(0, rows // tall, pack, 0)
    start(cols_out)
    for step, copy in rows_out + cols_out:

        @pl.when(exists((-step[0], -step[1])))
        def _():
            copy.wait_recv()

    last = (lane & 2) == 0
    after, before = exists((0, 1)), exists((0, -1))

    def merge(c, carry):
        at = pl.ds(pl.multiple_of(c * tall, tall), tall)
        right = jnp.where(after, got_col[0, at, :], 0.0)
        left = jnp.where(before, got_col[1, at, :], 0.0)
        col_rim[at, :] = jnp.where(last, right, left)
        return carry

    lax.fori_loop(0, rows // tall, merge, 0)
    for side in range(2):
        there = exists((1 - 2 * side, 0))
        rim_f[side] = jnp.where(there, got_f[side], 0.0)
        rim_m[side] = jnp.where(there, got_m[side], 0)
        right = jnp.where(there & after, got_corner[side, 0], 0.0)
        left = jnp.where(there & before, got_corner[side, 1], 0.0)
        corner[side] = jnp.where(last[:8], right, left)
    for step, copy in rows_out + cols_out:

        @pl.when(exists(step))
        def _():
            copy.wait_send()


def halo(e, h, m):
    planes, rows, cols = e.shape
    f32, i32 = jnp.float32, jnp.int32
    dma = pltpu.SemaphoreType.DMA
    return pl.pallas_call(
        halo_kernel,
        out_shape=(
            jax.ShapeDtypeStruct((rows, LANES), f32),
            jax.ShapeDtypeStruct((2, 8, LANES), f32),
            jax.ShapeDtypeStruct((2, 2 * planes, 8, cols), f32),
            jax.ShapeDtypeStruct((2, LZ, 8, cols), i32),
        ),
        in_specs=[ANY] * 3,
        out_specs=(VM,) * 4,
        scratch_shapes=[
            pltpu.VMEM((2, 2 * planes, rows, LANES), f32),
            pltpu.VMEM((2, LZ, rows, LANES), i32),
            pltpu.VMEM((2, rows, LANES), f32),
            pltpu.VMEM((2, rows, LANES), f32),
            pltpu.VMEM((2, 2, 8, LANES), f32),
            pltpu.VMEM((2, 2 * planes, 8, cols), f32),
            pltpu.VMEM((2, LZ, 8, cols), i32),
            dma((6,)),
            dma((12,)),
            dma((12,)),
        ],
        compiler_params=pltpu.CompilerParams(collective_id=0, has_side_effects=True),
        name="halo",
    )(e, h, m)


def fields_per_device(gx, cols):
    return 2 * EACH * cols // (gx * LANES)


def yee_kernel(
    grid_rows, grid_cols, per,
    e_hbm, h_hbm, m_hbm, col_rim, corner, rim_f, rim_m, eps, pos, amp,
    e_out, h_out, *rest,
):
    sd_outs, (e_ext, h_ext, m_main, scale, src, first, sems) = rest[:SETS], rest[SETS:]
    rows, cols = m_main.shape[1:]
    width = cols + PAD
    high = e_ext.shape[1]
    row0 = lax.axis_index("gx") * rows
    col0 = lax.axis_index("gy") * cols
    main_r = pl.ds(BASE, rows)
    copies = [
        pltpu.make_async_copy(e_hbm, e_ext.at[:, main_r, pl.ds(0, cols)], sems.at[0]),
        pltpu.make_async_copy(h_hbm, h_ext.at[:, main_r, pl.ds(0, cols)], sems.at[1]),
        pltpu.make_async_copy(m_hbm, m_main, sems.at[2]),
    ]
    for copy in copies:
        copy.start()
    count = amp.shape[1]
    step = min(count, 1024)
    used = high - 2 * CHUNK
    row_at = row0 + lax.broadcasted_iota(jnp.int32, (used, step), 0) + (CHUNK - BASE)
    lane = lax.broadcasted_iota(jnp.int32, (width, step), 0)
    col_at = col0 + jnp.where(lane < cols + PAD // 2, lane, lane - width)
    for start in range(0, count, step):
        at = pl.ds(start, step)
        amp_now = amp[:, at]
        hi = amp_now.astype(jnp.bfloat16).astype(jnp.float32)
        mid = (amp_now - hi).astype(jnp.bfloat16).astype(jnp.float32)
        low = amp_now - hi - mid
        hit_col = jnp.where(col_at == pos[2:3, at], 1.0, 0.0).astype(jnp.bfloat16)
        hit_row = row_at == pos[1:2, at]
        for layer in range(LZ):
            hit = hit_row & (pos[0:1, at] == layer)
            total = None
            for piece in (hi, mid, low):
                left = jnp.where(hit, piece, 0.0).astype(jnp.bfloat16)
                term = lax.dot_general(
                    left, hit_col, (((1,), (1,)), ((), ())), preferred_element_type=jnp.float32
                )
                total = term if total is None else total + term
            if start == 0:
                src[layer, CHUNK : CHUNK + used, :] = total
            else:
                src[layer, CHUNK : CHUNK + used, :] += total
    copies[2].wait()

    def scale_of(index, row, col):
        value = jnp.full(index.shape, eps[0], jnp.float32)
        for material in range(1, NMAT):
            value = jnp.where(index == material, eps[material], value)
        inside = (row >= 0) & (row < grid_rows) & (col >= 0) & (col < grid_cols)
        return jnp.where(inside, courant / value, 0.0)

    col_main = col0 + lax.broadcasted_iota(jnp.int32, (CHUNK, cols), 1)
    lane_pad = lax.broadcasted_iota(jnp.int32, (CHUNK, PAD), 1)
    col_pad = col0 + jnp.where(lane_pad < PAD // 2, cols + lane_pad, lane_pad - PAD)
    row_chunk = row0 + lax.broadcasted_iota(jnp.int32, (CHUNK, cols), 0)

    def shown(block, plane):
        return pltpu.roll(block, PAD - 4 * plane, 1) if plane else block

    def fill(step_index, carry):
        r = pl.multiple_of(step_index * CHUNK, CHUNK)
        near = pl.ds(r, CHUNK)
        far = pl.ds(BASE + r, CHUNK)
        block = col_rim[near, :]
        for layer in range(LZ):
            scale[layer, far, :cols] = scale_of(m_main[layer, near, :], row_chunk + r, col_main)
            scale[layer, far, cols:] = scale_of(
                shown(block, 6 * LZ + layer), row_chunk[:, :PAD] + r, col_pad
            )
        for plane in range(3 * LZ):
            e_ext[plane, far, cols:] = shown(block, plane)
            h_ext[plane, far, cols:] = shown(block, 3 * LZ + plane)
        return carry

    lax.fori_loop(0, rows // CHUNK, fill, 0)
    row_eight = row0 + lax.broadcasted_iota(jnp.int32, (8, cols), 0)
    blank = jnp.zeros((8, width), jnp.float32)
    for side, target, offset, spare in (
        (0, BASE + rows, rows, BASE + rows + 8),
        (1, BASE - 8, -8, BASE - 16),
    ):
        here = slice(target, target + 8)
        block = corner[side]
        for layer in range(LZ):
            scale[layer, here, :cols] = scale_of(
                rim_m[side, layer], row_eight + offset, col_main[:8]
            )
            scale[layer, here, cols:] = scale_of(
                shown(block, 6 * LZ + layer), row_eight[:, :PAD] + offset, col_pad[:8]
            )
            scale[layer, spare : spare + 8, :] = blank
        for plane in range(3 * LZ):
            e_ext[plane, here, :cols] = rim_f[side, plane]
            h_ext[plane, here, :cols] = rim_f[side, 3 * LZ + plane]
            e_ext[plane, here, cols:] = shown(block, plane)
            h_ext[plane, here, cols:] = shown(block, 3 * LZ + plane)
            e_ext[plane, spare : spare + 8, :] = blank
            h_ext[plane, spare : spare + 8, :] = blank
    for plane in range(3 * LZ):
        e_ext[plane, high - 16 : high, :] = jnp.zeros((16, width), jnp.float32)
        h_ext[plane, 0:16, :] = jnp.zeros((16, width), jnp.float32)
    lane_c = lax.broadcasted_iota(jnp.int32, (CHUNK, width), 1)
    col_c = col0 + jnp.where(lane_c < cols + PAD // 2, lane_c, lane_c - width)
    weight = jnp.where(col_c >= 0, courant, 0.0)
    top = lax.axis_index("gx") == 0
    copies[0].wait()
    copies[1].wait()

    def magnetic_pass(index, carry):
        r = pl.multiple_of(index * CHUNK, CHUNK)
        now = pl.ds(r, CHUNK)
        more = pl.ds(r, CHUNK + 8)
        factor = weight * jnp.where(top & (index * CHUNK < BASE), 0.0, 1.0)
        zero = jnp.zeros((CHUNK, width), jnp.float32)
        ex = [e_ext[layer, now, :] for layer in range(LZ)] + [zero]
        ey = [e_ext[LZ + layer, now, :] for layer in range(LZ)] + [zero]
        for layer in range(LZ):
            ez = e_ext[2 * LZ + layer, now, :]
            ez_row = pltpu.roll(e_ext[2 * LZ + layer, more, :], CHUNK + 7, 0)[:CHUNK]
            ey_row = pltpu.roll(e_ext[LZ + layer, more, :], CHUNK + 7, 0)[:CHUNK]
            ez_col = pltpu.roll(ez, width - 1, 1)
            ex_col = pltpu.roll(ex[layer], width - 1, 1)
            curl_x = ez_col - ez - (ey[layer + 1] - ey[layer])
            curl_y = ex[layer + 1] - ex[layer] - (ez_row - ez)
            curl_z = ey_row - ey[layer] - (ex_col - ex[layer])
            for part, curl in enumerate((curl_x, curl_y, curl_z)):
                plane = part * LZ + layer
                h_ext[plane, now, :] = h_ext[plane, now, :] - factor * curl
        return carry

    def electric_pass(moment, last, index, carry):
        r = pl.multiple_of(index * CHUNK, CHUNK)
        now = pl.ds(r, CHUNK)
        more = pl.ds(pl.multiple_of(r - 8, 8), CHUNK + 8)
        drive = math.sin(source_rate * moment)
        zero = jnp.zeros((CHUNK, width), jnp.float32)
        hx = [zero] + [h_ext[layer, now, :] for layer in range(LZ)]
        hy = [zero] + [h_ext[LZ + layer, now, :] for layer in range(LZ)]
        for layer in range(LZ):
            hz = h_ext[2 * LZ + layer, now, :]
            hz_row = pltpu.roll(h_ext[2 * LZ + layer, more, :], 1, 0)[8:]
            hy_row = pltpu.roll(h_ext[LZ + layer, more, :], 1, 0)[8:]
            hx_now, hy_now = hx[layer + 1], hy[layer + 1]
            hz_col = pltpu.roll(hz, 1, 1)
            hx_col = pltpu.roll(hx_now, 1, 1)
            curl_x = hz - hz_col - (hy_now - hy[layer])
            curl_y = hx_now - hx[layer] - (hz - hz_row)
            curl_z = hy_now - hy_row - (hx_now - hx_col)
            factor = scale[layer, now, :]
            new_x = e_ext[layer, now, :] + factor * curl_x
            new_y = e_ext[LZ + layer, now, :] + factor * curl_y
            new_z = e_ext[2 * LZ + layer, now, :] + factor * curl_z + drive * src[layer, now, :]
            e_ext[layer, now, :] = new_x
            e_ext[LZ + layer, now, :] = new_y
            e_ext[2 * LZ + layer, now, :] = new_z
            if layer == FACE:
                faces = (-hy_now, hx_now, new_y, -new_x)
                for item, face in enumerate(faces):
                    if last:
                        old = first[item, now, :]
                        here = pl.ds(r - BASE, CHUNK)
                        for which, value in enumerate((old + face, face - old)):
                            share, place = divmod(which * EACH + item % EACH, per)
                            for q in range(cols // LANES):
                                piece = value[:, q * LANES : (q + 1) * LANES].astype(jnp.bfloat16)
                                lanes = pl.ds(place * LANES, LANES)
                                sd_outs[item // EACH][q * (2 * EACH // per) + share, here, lanes] = piece
                    else:
                        first[item, now, :] = face
        return carry

    chunks = high // CHUNK
    main0 = BASE // CHUNK
    main1 = main0 + rows // CHUNK
    lax.fori_loop(1, chunks - 1, magnetic_pass, 0)
    lax.fori_loop(1, chunks - 1, functools.partial(electric_pass, 1.0, False), 0)
    lax.fori_loop(1, main1, magnetic_pass, 0)
    out_h = pltpu.make_async_copy(h_ext.at[:, main_r, pl.ds(0, cols)], h_out, sems.at[3])
    out_h.start()
    lax.fori_loop(main0, main1, functools.partial(electric_pass, 2.0, True), 0)
    out_e = pltpu.make_async_copy(e_ext.at[:, main_r, pl.ds(0, cols)], e_out, sems.at[4])
    out_e.start()
    out_h.wait()
    out_e.wait()


def yee(e_field, h_field, material, eps_table, src_pos, src_amp):
    rows, cols = material.shape[1:]
    gx = lax.axis_size("gx")
    per = fields_per_device(gx, cols)
    grid_rows = rows * gx
    grid_cols = cols * lax.axis_size("gy")
    planes = 3 * LZ
    e = e_field.reshape(planes, rows, cols)
    h = h_field.reshape(planes, rows, cols)

    high = rows + 2 * BASE
    width = cols + PAD
    f32 = jnp.float32
    out = pl.pallas_call(
        functools.partial(yee_kernel, grid_rows, grid_cols, per),
        out_shape=(
            jax.ShapeDtypeStruct((planes, rows, cols), f32),
            jax.ShapeDtypeStruct((planes, rows, cols), f32),
        )
        + (jax.ShapeDtypeStruct((gx, rows, per * LANES), jnp.bfloat16),) * SETS,
        in_specs=[ANY, ANY, ANY, VM, VM, VM, VM, SM, VM, VM],
        out_specs=(ANY, ANY) + (VM,) * SETS,
        scratch_shapes=[
            pltpu.VMEM((planes, high, width), f32),
            pltpu.VMEM((planes, high, width), f32),
            pltpu.VMEM((LZ, rows, cols), jnp.int32),
            pltpu.VMEM((LZ, high, width), f32),
            pltpu.VMEM((LZ, high, width), f32),
            pltpu.VMEM((4, high, width), f32),
            pltpu.SemaphoreType.DMA((5,)),
        ],
        compiler_params=pltpu.CompilerParams(vmem_limit_bytes=BIG),
        name="yee",
    )(
        e, h, material, *halo(e, h, material),
        eps_table, jnp.swapaxes(src_pos, 0, 1), src_amp[None, :],
    )
    return out


SIN = (-1.0 / 6.0, 1.0 / 120.0, -1.0 / 5040.0, 1.0 / 362880.0)
COS = (-0.5, 1.0 / 24.0, -1.0 / 720.0, 1.0 / 40320.0, -1.0 / 3628800.0)


def unit(phase, period):
    eighth = period // 8
    turn = phase & (period - 1)
    quarter = (turn + eighth) // (2 * eighth)
    x = (turn - quarter * (2 * eighth)).astype(jnp.float32) * (2.0 * math.pi / period)
    square = x * x
    sine = jnp.full_like(x, SIN[-1])
    for factor in SIN[-2::-1]:
        sine = sine * square + factor
    sine = x + x * (square * sine)
    cosine = jnp.full_like(x, COS[-1])
    for factor in COS[-2::-1]:
        cosine = cosine * square + factor
    cosine = 1.0 + square * cosine
    odd = (quarter & 1) == 1
    re = jnp.where(odd, sine, cosine)
    im = jnp.where(odd, cosine, sine)
    re = jnp.where(((quarter + 1) & 2) == 2, -re, re)
    im = jnp.where((quarter & 2) == 2, im, -im)
    return re, im


def layout(gx, gy):
    mper = max(8, NA // 2 // (gx * gy))
    return mper, NA // 2 // mper, NA // gx // mper


def far_kernel(grid_rows, grid_cols, mix, *rest):
    sd, outs, rest = rest[:SETS], rest[SETS : 2 * SETS], rest[2 * SETS :]
    x_tab, y_tab, v, g, left, left_x, held, held_x, *sems = rest
    send_v, recv_v, send_g, recv_g, send_x, recv_x, send_f, recv_f, send_1, recv_1, send_e = sems
    gx, gy = lax.axis_size("gx"), lax.axis_size("gy")
    i, z = lax.axis_index("gx"), lax.axis_index("gy")
    me = i * gy + z
    count = gx * gy
    rows = grid_rows // gx
    cols = grid_cols // gy
    per = v.shape[2] // LANES
    split = 2 * EACH // per
    slabs = cols // LANES
    mper, owners, near = layout(gx, gy)
    own = 2 * mper
    vb = NA // gy
    wide = NF * EACH * 2
    half = gx // 2
    mesh_id = pl.DeviceIdType.MESH

    upper = i >= half
    plane = jnp.where(upper, i - half, half - 1 - i)
    turn = jnp.where(upper, 0, gy) + z
    block_id = plane * near + turn

    def owner(t):
        c, r = lax.div(t, near), lax.rem(t, near)
        return jnp.where(r < gy, half + c, half - 1 - c), lax.rem(r, gy)

    end_i, end_z = owner(jnp.int32(owners - 1))

    def ship(src, dst, where, send_sem, recv_sem, start):
        here = (where[0] == i) & (where[1] == z)

        @pl.when(~here)
        def _():
            copy = pltpu.make_async_remote_copy(
                src_ref=src, dst_ref=dst, send_sem=send_sem, recv_sem=recv_sem,
                device_id=where, device_id_type=mesh_id,
            )
            if start:
                copy.start()
            else:
                copy.wait_send()

        if start:

            @pl.when(here)
            def _():
                pltpu.make_async_copy(src, dst, recv_sem).start()

    def arrived(ref, sem):
        pltpu.make_async_copy(ref, ref, sem).wait()

    barrier = pltpu.get_barrier_semaphore()
    for offset in range(1, count):
        peer = lax.rem(me + offset, count)
        pl.semaphore_signal(
            barrier, inc=1, device_id=(lax.div(peer, gy), lax.rem(peer, gy)), device_id_type=mesh_id
        )
    pl.semaphore_wait(barrier, count - 1)

    def v_ship(s, offset, start):
        peer = lax.rem(i + offset, gx)
        here = pl.ds(pl.multiple_of(i * rows, rows), rows)
        ship(sd[s].at[peer], v.at[s, here], (peer, z), send_v.at[s, offset], recv_v.at[s, i], start)

    def g_ship(s, t, start):
        lane = pl.multiple_of((z * slabs + lax.div(i, split)) * LANES, LANES)
        to = (pl.ds(lax.rem(i, split) * per, per), slice(None), pl.ds(lane, LANES))
        part = g.at[s, :, pl.ds(pl.multiple_of(t * own, own), own), :]
        ship(part, left.at[(s, *to)], owner(t), send_g.at[s, t], recv_g.at[s, me], start)

    def x_ship(s, start):
        lane = pl.multiple_of((z * slabs + lax.div(i, split)) * LANES, LANES)
        to = (pl.ds(lax.rem(i, split) * per, per), slice(None), pl.ds(lane, LANES))
        part = g.at[s, :, pl.ds(owners * own, 16), :]
        ship(part, left_x.at[(s, *to)], (end_i, end_z), send_x.at[s], recv_x.at[s, me], start)

    def f_ship(s, step, start):
        peer = lax.rem(z + step, gy)
        at = pl.ds(pl.multiple_of(turn * mper, mper), mper)
        ship(
            held.at[s, peer, 0], outs[s].at[at], (half + plane, peer),
            send_f.at[s, 0, step - 1], recv_f.at[s, turn], start,
        )
        mirror = near - 1 - turn
        at = pl.ds(mirror * mper + 1, mper - 1)
        ship(
            held.at[s, peer, 1, pl.ds(0, mper - 1)], outs[s].at[at], (half - 1 - plane, peer),
            send_f.at[s, 1, step - 1], recv_f.at[s, mirror], start,
        )
        first = turn == 0
        to = jnp.where(first, half - plane, half - 1 - plane)
        slot = jnp.where(first, 0, near - turn)

        @pl.when(block_id > 0)
        def _():
            ship(
                held.at[s, peer, 1, pl.ds(mper - 1, 1)], outs[s].at[pl.ds(slot * mper, 1)], (to, peer),
                send_1.at[s, step - 1], recv_1.at[s, slot], start,
            )

    def e_ship(s, step, start):
        peer = lax.rem(z + step, gy)
        ship(
            held_x.at[s, peer], outs[s].at[pl.ds(0, 1)], (0, peer),
            send_e.at[s, step - 1], recv_1.at[s, 0], start,
        )

    def fill_x(m, row):
        low = lax.broadcasted_iota(jnp.int32, m.shape, 1)
        a_re, a_im = unit(m * (low * LANES), zoom_factor * grid_rows)
        b_re, b_im = unit(m * low, zoom_factor * grid_rows)
        for block in range(grid_rows // LANES):
            h_re, h_im = a_re[:, block : block + 1], a_im[:, block : block + 1]
            re = h_re * b_re - h_im * b_im
            im = h_re * b_im + h_im * b_re
            both = jnp.concatenate([re, im], 0).astype(jnp.bfloat16)
            x_tab[pl.ds(row, 2 * m.shape[0]), block * LANES : (block + 1) * LANES] = both

    def build_x():
        row = lax.broadcasted_iota(jnp.int32, (mper, LANES), 0)

        def body(t, carry):
            fill_x(row + t * mper, pl.multiple_of(t * own, own))
            return carry

        lax.fori_loop(0, owners, body, 0)
        fill_x(jnp.full((8, LANES), NA // 2, jnp.int32), owners * own)

    def build_y():
        tall = 32
        low = lax.broadcasted_iota(jnp.int32, (tall, LANES), 1)
        row = lax.broadcasted_iota(jnp.int32, (tall, LANES), 0)

        def body(d, carry):
            start = pl.multiple_of(d * tall, tall)
            y = row + start
            a_re, a_im = unit(y * (low * LANES + NA // 4), zoom_factor * grid_cols)
            b_re, b_im = unit(y * low, zoom_factor * grid_cols)
            for block in range(NA // LANES):
                h_re, h_im = a_re[:, block : block + 1], a_im[:, block : block + 1]
                at = slice(block * LANES, (block + 1) * LANES)
                y_tab[0, pl.ds(start, tall), at] = (h_re * b_re - h_im * b_im).astype(jnp.bfloat16)
                y_tab[1, pl.ds(start, tall), at] = (h_re * b_im + h_im * b_re).astype(jnp.bfloat16)
            return carry

        lax.fori_loop(0, grid_cols // tall, body, 0)

    dot = functools.partial(jnp.dot, preferred_element_type=jnp.float32)
    parts = 2
    group = owners // parts

    def transform_rows(s):
        for src in range(gx):
            arrived(v.at[s, pl.ds(src * rows, rows)], recv_v.at[s, src])

        def body(c, carry):
            chunk = lax.rem(lax.div(block_id, group) + 1 + c, parts)
            tall = group * own
            start = pl.multiple_of(chunk * tall, tall)
            both = dot(x_tab[pl.ds(start, tall + 16), :], v[s]).astype(jnp.bfloat16)
            for f in range(per):
                g[s, f, pl.ds(start, tall), :] = both[:tall, f * LANES : (f + 1) * LANES]

            @pl.when(chunk == parts - 1)
            def _():
                for f in range(per):
                    g[s, f, owners * own :, :] = both[tall:, f * LANES : (f + 1) * LANES]
                x_ship(s, True)

            for e in range(group):
                g_ship(s, chunk * group + e, True)
            return carry

        lax.fori_loop(0, parts, body, 0)

    def one_hot(shape, source):
        row = lax.broadcasted_iota(jnp.int32, shape, 0)
        col = lax.broadcasted_iota(jnp.int32, shape, 1)
        return jnp.where(col == source(row), 1.0, 0.0).astype(jnp.bfloat16)

    size = (wide * mper, wide * mper)
    forth = one_hot(size, lambda row: lax.rem(row, wide) * mper + lax.div(row, wide))
    back = one_hot(size, lambda row: lax.rem(row, wide) * mper + mper - 1 - lax.div(row, wide))
    only = one_hot((wide, wide * 8), lambda row: row * 8)

    def finish(lhs, count_m, peer):
        at = pl.ds(pl.multiple_of(peer * vb, vb), vb)
        p_re, p_im = dot(lhs, y_tab[0, :, at]), dot(lhs, y_tab[1, :, at])
        plus, minus = [], []

        def both_signs(f):
            top = slice(2 * f * count_m, (2 * f + 1) * count_m)
            low = slice((2 * f + 1) * count_m, (2 * f + 2) * count_m)
            a_re, a_im, b_re, b_im = p_re[top], p_im[top], p_re[low], p_im[low]
            return (a_re - b_im, a_im + b_re), (a_re + b_im, a_im - b_re)

        fields = [both_signs(f) for f in range(2 * EACH)]
        for f in range(NF):
            p0, p1, q0, q1 = (mix[f, t] for t in range(4))
            for k in range(EACH):
                for sign, result in enumerate((plus, minus)):
                    s_re, s_im = fields[k][sign]
                    d_re, d_im = fields[EACH + k][sign]
                    result.append(p0 * s_re - p1 * s_im + (q0 * d_re - q1 * d_im))
                    result.append(p0 * s_im + p1 * s_re + (q0 * d_im + q1 * d_re))
        pack = lambda result: jnp.concatenate(result, 0).astype(jnp.bfloat16)
        return pack(plus), pack(minus)

    def transform_cols(s):
        for src in range(count):
            src_i, src_z = divmod(src, gy)
            lane = (src_z * slabs + src_i // split) * LANES
            region = left.at[s, pl.ds(src_i % split * per, per), :, pl.ds(lane, LANES)]
            arrived(region, recv_g.at[s, src])
        lhs = left[s].reshape(2 * EACH * own, grid_cols)
        for step in range(1, gy + 1):
            peer = lax.rem(z + step, gy)
            plus, minus = finish(lhs, mper, peer)
            held[s, peer, 0] = dot(forth, plus).reshape(mper, wide, vb).astype(jnp.bfloat16)
            held[s, peer, 1] = dot(back, minus).reshape(mper, wide, vb).astype(jnp.bfloat16)
            f_ship(s, step, True)

    at_end = (i == end_i) & (z == end_z)

    def transform_end(s):
        for src in range(count):
            src_i, src_z = divmod(src, gy)
            lane = (src_z * slabs + src_i // split) * LANES
            region = left_x.at[s, pl.ds(src_i % split * per, per), :, pl.ds(lane, LANES)]
            arrived(region, recv_x.at[s, src])
        lhs = left_x[s].reshape(2 * EACH * 16, grid_cols)
        for step in range(1, gy + 1):
            peer = lax.rem(z + step, gy)
            _, minus = finish(lhs, 8, peer)
            held_x[s, peer] = dot(only, minus).reshape(1, wide, vb).astype(jnp.bfloat16)
            e_ship(s, step, True)

    def owned(body):
        if near == 2 * gy:
            body()
        else:
            pl.when(turn < near)(body)

    for s in range(SETS):
        for offset in range(gx):
            v_ship(s, offset, True)
    build_x()
    transform_rows(0)
    build_y()
    for s in range(1, SETS):
        transform_rows(s)
    for s in range(SETS):
        owned(functools.partial(transform_cols, s))
        pl.when(at_end)(functools.partial(transform_end, s))
    for s in range(SETS):

        @pl.when(upper)
        def _():
            for slot in range(near):
                arrived(outs[s].at[pl.ds(slot * mper, mper)], recv_f.at[s, slot])

        @pl.when(~upper)
        def _():
            for slot in range(near):
                arrived(outs[s].at[pl.ds(slot * mper + 1, mper - 1)], recv_f.at[s, slot])
                arrived(outs[s].at[pl.ds(slot * mper, 1)], recv_1.at[s, slot])

    for s in range(SETS):
        for offset in range(gx):
            v_ship(s, offset, False)
        x_ship(s, False)
        for t in range(owners):
            g_ship(s, jnp.int32(t), False)

        def sent():
            for step in range(1, gy + 1):
                f_ship(s, step, False)

        owned(sent)

        @pl.when(at_end)
        def _():
            for step in range(1, gy + 1):
                e_ship(s, step, False)


def far(sd, freqs, grid_rows, grid_cols):
    gx, gy = lax.axis_size("gx"), lax.axis_size("gy")
    count = gx * gy
    nu, vb = NA // gx, NA // gy
    mper, owners, near = layout(gx, gy)
    lanes = sd[0].shape[2]
    wide = NF * EACH * 2
    bf16 = jnp.bfloat16
    turn_re, turn_im = jnp.cos(1.5 * freqs), jnp.sin(1.5 * freqs)
    half_re, half_im = jnp.cos(0.5 * freqs), jnp.sin(0.5 * freqs)
    mix = jnp.stack(
        [turn_re * half_re, turn_im * half_re, -turn_im * half_im, turn_re * half_im], 1
    ) * (1.0 / math.sqrt(grid_rows * grid_cols))
    dma = pltpu.SemaphoreType.DMA
    done = pl.pallas_call(
        functools.partial(far_kernel, grid_rows, grid_cols),
        out_shape=(jax.ShapeDtypeStruct((nu, wide, vb), bf16),) * SETS,
        in_specs=[SM] + [ANY] * SETS,
        out_specs=(ANY,) * SETS,
        scratch_shapes=[
            pltpu.VMEM((NA + 16, grid_rows), bf16),
            pltpu.VMEM((2, grid_cols, NA), bf16),
            pltpu.VMEM((SETS, grid_rows, lanes), bf16),
            pltpu.VMEM((SETS, lanes // LANES, NA + 16, LANES), bf16),
            pltpu.VMEM((SETS, 2 * EACH, 2 * mper, grid_cols), bf16),
            pltpu.VMEM((SETS, 2 * EACH, 16, grid_cols), bf16),
            pltpu.VMEM((SETS, gy, 2, mper, wide, vb), bf16),
            pltpu.VMEM((SETS, gy, 1, wide, vb), bf16),
            dma((SETS, gx)),
            dma((SETS, gx)),
            dma((SETS, owners)),
            dma((SETS, count)),
            dma((SETS,)),
            dma((SETS, count)),
            dma((SETS, 2, gy)),
            dma((SETS, near)),
            dma((SETS, gy)),
            dma((SETS, near)),
            dma((SETS, gy)),
        ],
        compiler_params=pltpu.CompilerParams(
            vmem_limit_bytes=BIG, collective_id=1, has_side_effects=True
        ),
        name="far",
    )(mix, *sd)
    done = [part.astype(jnp.float32).reshape(nu, NF, EACH, 2, vb) for part in done]
    return jnp.concatenate(done, 2).reshape(nu, NF * 4, 2, vb)


def on_device(e_field, h_field, material, eps_table, src_pos, src_amp, freqs):
    rows, cols = material.shape[1:]
    grid_rows, grid_cols = rows * lax.axis_size("gx"), cols * lax.axis_size("gy")
    e_new, h_new, *sd = yee(e_field, h_field, material, eps_table, src_pos, src_amp)
    shape = e_field.shape
    return (e_new.reshape(shape), h_new.reshape(shape), far(sd, freqs, grid_rows, grid_cols))


def solution(mesh):
    placed = (
        P(None, None, "gx", "gy"),
        P(None, None, "gx", "gy"),
        P(None, "gx", "gy"),
        P(),
        P(),
        P(),
        P(),
    )
    return jax.shard_map(
        on_device,
        mesh=mesh,
        in_specs=placed,
        out_specs=(P(None, None, "gx", "gy"), P(None, None, "gx", "gy"), P("gx", None, None, "gy")),
        check_vma=False,
    )
```

```python
import functools
import math

import jax
import jax.numpy as jnp
from jax import lax
from jax.experimental import pallas as pl
from jax.experimental.pallas import tpu as pltpu
from jax.sharding import PartitionSpec as P

LZ = 3
FACE = 1
STEPS = 2
NF = 2
NA = 1024
NMAT = 8

courant = 0.5
source_rate = 0.7
zoom_factor = 4

BASE = 32
CHUNK = 16
SETS = 2
EACH = 4 // SETS
LANES = 128
PAD = 128
ANY = pl.BlockSpec(memory_space=pl.ANY)
VM = pl.BlockSpec(memory_space=pltpu.VMEM)
SM = pl.BlockSpec(memory_space=pltpu.SMEM)
BIG = 60 * 1024 * 1024


def halo_kernel(
    e, h, m, col_rim, corner, rim_f, rim_m,
    edge_f, edge_m, packed, got_col, got_corner, got_f, got_m, load, send, recv,
):
    gx, gy = lax.axis_size("gx"), lax.axis_size("gy")
    i, z = lax.axis_index("gx"), lax.axis_index("gy")
    planes, rows, cols = e.shape
    around = [(a, b) for a in (-1, 0, 1) for b in (-1, 0, 1) if (a, b) != (0, 0)]

    def exists(step):
        row, col = i + step[0], z + step[1]
        return (row >= 0) & (row < gx) & (col >= 0) & (col < gy)

    loads = []
    for side, lane in enumerate((0, cols - LANES)):
        at = pl.ds(lane, LANES)
        loads.append(pltpu.make_async_copy(e.at[:, :, at], edge_f.at[side, pl.ds(0, planes)], load.at[3 * side]))
        loads.append(pltpu.make_async_copy(h.at[:, :, at], edge_f.at[side, pl.ds(planes, planes)], load.at[3 * side + 1]))
        loads.append(pltpu.make_async_copy(m.at[:, :, at], edge_m.at[side], load.at[3 * side + 2]))
    for copy in loads:
        copy.start()
    barrier = pltpu.get_barrier_semaphore()
    total = jnp.int32(0)
    for step in around:
        total += exists(step).astype(jnp.int32)

        @pl.when(exists(step))
        def _():
            pl.semaphore_signal(
                barrier, inc=1, device_id=(i + step[0], z + step[1]), device_id_type=pl.DeviceIdType.MESH
            )

    pl.semaphore_wait(barrier, total)

    def remote(step, src, dst, index):
        copy = pltpu.make_async_remote_copy(
            src_ref=src, dst_ref=dst, send_sem=send.at[index], recv_sem=recv.at[index],
            device_id=(i + step[0], z + step[1]), device_id_type=pl.DeviceIdType.MESH,
        )
        return step, copy

    rows_out, cols_out = [], []
    for side, low in enumerate((0, rows - 8)):
        step = (2 * side - 1, 0)
        at = pl.ds(low, 8)
        rows_out.append(remote(step, e.at[:, at, :], got_f.at[side, pl.ds(0, planes)], 3 * side))
        rows_out.append(remote(step, h.at[:, at, :], got_f.at[side, pl.ds(planes, planes)], 3 * side + 1))
        rows_out.append(remote(step, m.at[:, at, :], got_m.at[side], 3 * side + 2))
    for side in range(2):
        cols_out.append(remote((0, 2 * side - 1), packed.at[side], got_col.at[side], 6 + side))
        for end, low in enumerate((0, rows - 8)):
            step = (2 * end - 1, 2 * side - 1)
            src = packed.at[side, pl.ds(low, 8)]
            cols_out.append(remote(step, src, got_corner.at[end, side], 8 + 2 * side + end))

    def start(copies):
        for step, copy in copies:

            @pl.when(exists(step))
            def _():
                copy.start()

    start(rows_out)
    for copy in loads:
        copy.wait()
    tall = 32
    lane = lax.broadcasted_iota(jnp.int32, (tall, LANES), 1)

    def pack(c, carry):
        at = pl.ds(pl.multiple_of(c * tall, tall), tall)
        for side in range(2):
            place = ((lane + 2 * side) & (LANES - 1)) >> 2
            block = jnp.zeros((tall, LANES), jnp.float32)
            for p in range(2 * planes + LZ):
                if p < 2 * planes:
                    piece = edge_f[side, p, at, :]
                else:
                    piece = edge_m[side, p - 2 * planes, at, :].astype(jnp.float32)
                block = jnp.where(place == p, pltpu.roll(piece, 4 * p, 1), block)
            packed[side, at, :] = block
        return carry

    lax.fori_loop(0, rows // tall, pack, 0)
    start(cols_out)
    for step, copy in rows_out + cols_out:

        @pl.when(exists((-step[0], -step[1])))
        def _():
            copy.wait_recv()

    last = (lane & 2) == 0
    after, before = exists((0, 1)), exists((0, -1))

    def merge(c, carry):
        at = pl.ds(pl.multiple_of(c * tall, tall), tall)
        right = jnp.where(after, got_col[0, at, :], 0.0)
        left = jnp.where(before, got_col[1, at, :], 0.0)
        col_rim[at, :] = jnp.where(last, right, left)
        return carry

    lax.fori_loop(0, rows // tall, merge, 0)
    for side in range(2):
        there = exists((1 - 2 * side, 0))
        rim_f[side] = jnp.where(there, got_f[side], 0.0)
        rim_m[side] = jnp.where(there, got_m[side], 0)
        right = jnp.where(there & after, got_corner[side, 0], 0.0)
        left = jnp.where(there & before, got_corner[side, 1], 0.0)
        corner[side] = jnp.where(last[:8], right, left)
    for step, copy in rows_out + cols_out:

        @pl.when(exists(step))
        def _():
            copy.wait_send()


def halo(e, h, m):
    planes, rows, cols = e.shape
    f32, i32 = jnp.float32, jnp.int32
    dma = pltpu.SemaphoreType.DMA
    return pl.pallas_call(
        halo_kernel,
        out_shape=(
            jax.ShapeDtypeStruct((rows, LANES), f32),
            jax.ShapeDtypeStruct((2, 8, LANES), f32),
            jax.ShapeDtypeStruct((2, 2 * planes, 8, cols), f32),
            jax.ShapeDtypeStruct((2, LZ, 8, cols), i32),
        ),
        in_specs=[ANY] * 3,
        out_specs=(VM,) * 4,
        scratch_shapes=[
            pltpu.VMEM((2, 2 * planes, rows, LANES), f32),
            pltpu.VMEM((2, LZ, rows, LANES), i32),
            pltpu.VMEM((2, rows, LANES), f32),
            pltpu.VMEM((2, rows, LANES), f32),
            pltpu.VMEM((2, 2, 8, LANES), f32),
            pltpu.VMEM((2, 2 * planes, 8, cols), f32),
            pltpu.VMEM((2, LZ, 8, cols), i32),
            dma((6,)),
            dma((12,)),
            dma((12,)),
        ],
        compiler_params=pltpu.CompilerParams(collective_id=0, has_side_effects=True),
        name="halo",
    )(e, h, m)


def fields_per_device(gx, cols):
    return 2 * EACH * cols // (gx * LANES)


def yee_kernel(
    grid_rows, grid_cols, per,
    e_hbm, h_hbm, m_hbm, col_rim, corner, rim_f, rim_m, eps, pos, amp,
    e_out, h_out, *rest,
):
    sd_outs, (e_ext, h_ext, m_main, scale, src, first, sems) = rest[:SETS], rest[SETS:]
    rows, cols = m_main.shape[1:]
    width = cols + PAD
    high = e_ext.shape[1]
    row0 = lax.axis_index("gx") * rows
    col0 = lax.axis_index("gy") * cols
    main_r = pl.ds(BASE, rows)
    copies = [
        pltpu.make_async_copy(e_hbm, e_ext.at[:, main_r, pl.ds(0, cols)], sems.at[0]),
        pltpu.make_async_copy(h_hbm, h_ext.at[:, main_r, pl.ds(0, cols)], sems.at[1]),
        pltpu.make_async_copy(m_hbm, m_main, sems.at[2]),
    ]
    for copy in copies:
        copy.start()
    count = amp.shape[1]
    used = high - 2 * CHUNK
    bf16 = jnp.bfloat16
    gather = functools.partial(
        lax.dot_general, dimension_numbers=(((1,), (1,)), ((), ())), preferred_element_type=jnp.float32
    )
    tall_at = lambda shape: row0 + lax.broadcasted_iota(jnp.int32, shape, 0) + (CHUNK - BASE)
    lane = lax.broadcasted_iota(jnp.int32, (width, LANES), 0)
    col_at = (col0 + jnp.where(lane < cols + PAD // 2, lane, lane - width)).astype(jnp.float32)
    row_at = tall_at((used, LANES)).astype(jnp.float32)
    row_s = jnp.broadcast_to(pos[1:2, :], (8, count))
    col_s = jnp.broadcast_to(pos[2:3, :], (8, count))
    inside = (row_s >= row0 - (BASE - CHUNK)) & (row_s < row0 + used - (BASE - CHUNK))
    inside &= (col_s >= col0 - PAD // 2) & (col_s < col0 + cols + PAD // 2)
    rank = jnp.where(inside, 1.0, 0.0)
    at_lane = lax.broadcasted_iota(jnp.int32, (8, count), 1)
    reach = 1
    while reach < count:
        rank = rank + jnp.where(at_lane >= reach, pltpu.roll(rank, reach, 1), 0.0)
        reach *= 2
    found = jnp.max(rank).astype(jnp.int32)
    rank = jnp.where(inside, rank, 0.0)[:1]
    hi = amp[...].astype(bf16).astype(jnp.float32)
    mid = (amp[...] - hi).astype(bf16).astype(jnp.float32)
    low = amp[...] - hi - mid
    parts = [
        (pos[1:2, :] >> 6).astype(jnp.float32), (pos[1:2, :] & 63).astype(jnp.float32),
        (pos[2:3, :] >> 6).astype(jnp.float32), (pos[2:3, :] & 63).astype(jnp.float32),
        pos[0:1, :].astype(jnp.float32), hi, mid, low,
    ]
    parts = jnp.concatenate(parts, 0).astype(bf16)
    for layer in range(LZ):
        src[layer] = jnp.zeros((high, width), jnp.float32)
    slot = lax.broadcasted_iota(jnp.int32, (LANES, count), 0).astype(jnp.float32)

    def place(group, carry):
        pick = jnp.where(slot + (group * LANES + 1).astype(jnp.float32) == rank, 1.0, 0.0)
        some = gather(parts, pick.astype(bf16))
        row, col = some[0:1] * 64.0 + some[1:2], some[2:3] * 64.0 + some[3:4]
        hit_col = jnp.where(col_at == col, 1.0, 0.0).astype(bf16)
        hit_col = jnp.concatenate([hit_col] * 3, 1)
        hit_row = row_at == row
        for layer in range(LZ):
            hit = hit_row & (some[4:5] == float(layer))
            left = [jnp.where(hit, some[p : p + 1], 0.0).astype(bf16) for p in (5, 6, 7)]
            src[layer, CHUNK : CHUNK + used, :] += gather(jnp.concatenate(left, 1), hit_col)
        return carry

    lax.fori_loop(0, lax.div(found + (LANES - 1), LANES), place, 0)
    copies[2].wait()

    def scale_of(index, row, col):
        value = jnp.full(index.shape, eps[0], jnp.float32)
        for material in range(1, NMAT):
            value = jnp.where(index == material, eps[material], value)
        inside = (row >= 0) & (row < grid_rows) & (col >= 0) & (col < grid_cols)
        return jnp.where(inside, courant / value, 0.0)

    col_main = col0 + lax.broadcasted_iota(jnp.int32, (CHUNK, cols), 1)
    lane_pad = lax.broadcasted_iota(jnp.int32, (CHUNK, PAD), 1)
    col_pad = col0 + jnp.where(lane_pad < PAD // 2, cols + lane_pad, lane_pad - PAD)
    row_chunk = row0 + lax.broadcasted_iota(jnp.int32, (CHUNK, cols), 0)

    def shown(block, plane):
        return pltpu.roll(block, PAD - 4 * plane, 1) if plane else block

    def fill(step_index, carry):
        r = pl.multiple_of(step_index * CHUNK, CHUNK)
        near = pl.ds(r, CHUNK)
        far = pl.ds(BASE + r, CHUNK)
        block = col_rim[near, :]
        for layer in range(LZ):
            scale[layer, far, :cols] = scale_of(m_main[layer, near, :], row_chunk + r, col_main)
            scale[layer, far, cols:] = scale_of(
                shown(block, 6 * LZ + layer), row_chunk[:, :PAD] + r, col_pad
            )
        for plane in range(3 * LZ):
            e_ext[plane, far, cols:] = shown(block, plane)
            h_ext[plane, far, cols:] = shown(block, 3 * LZ + plane)
        return carry

    lax.fori_loop(0, rows // CHUNK, fill, 0)
    row_eight = row0 + lax.broadcasted_iota(jnp.int32, (8, cols), 0)
    blank = jnp.zeros((8, width), jnp.float32)
    for side, target, offset, spare in (
        (0, BASE + rows, rows, BASE + rows + 8),
        (1, BASE - 8, -8, BASE - 16),
    ):
        here = slice(target, target + 8)
        block = corner[side]
        for layer in range(LZ):
            scale[layer, here, :cols] = scale_of(
                rim_m[side, layer], row_eight + offset, col_main[:8]
            )
            scale[layer, here, cols:] = scale_of(
                shown(block, 6 * LZ + layer), row_eight[:, :PAD] + offset, col_pad[:8]
            )
            scale[layer, spare : spare + 8, :] = blank
        for plane in range(3 * LZ):
            e_ext[plane, here, :cols] = rim_f[side, plane]
            h_ext[plane, here, :cols] = rim_f[side, 3 * LZ + plane]
            e_ext[plane, here, cols:] = shown(block, plane)
            h_ext[plane, here, cols:] = shown(block, 3 * LZ + plane)
            e_ext[plane, spare : spare + 8, :] = blank
            h_ext[plane, spare : spare + 8, :] = blank
    for plane in range(3 * LZ):
        e_ext[plane, high - 16 : high, :] = jnp.zeros((16, width), jnp.float32)
        h_ext[plane, 0:16, :] = jnp.zeros((16, width), jnp.float32)
    lane_c = lax.broadcasted_iota(jnp.int32, (CHUNK, width), 1)
    col_c = col0 + jnp.where(lane_c < cols + PAD // 2, lane_c, lane_c - width)
    weight = jnp.where(col_c >= 0, courant, 0.0)
    top = lax.axis_index("gx") == 0
    copies[0].wait()
    copies[1].wait()

    def magnetic_pass(index, carry):
        r = pl.multiple_of(index * CHUNK, CHUNK)
        now = pl.ds(r, CHUNK)
        more = pl.ds(r, CHUNK + 8)
        factor = weight * jnp.where(top & (index * CHUNK < BASE), 0.0, 1.0)
        zero = jnp.zeros((CHUNK, width), jnp.float32)
        ex = [e_ext[layer, now, :] for layer in range(LZ)] + [zero]
        ey = [e_ext[LZ + layer, now, :] for layer in range(LZ)] + [zero]
        for layer in range(LZ):
            ez = e_ext[2 * LZ + layer, now, :]
            ez_row = pltpu.roll(e_ext[2 * LZ + layer, more, :], CHUNK + 7, 0)[:CHUNK]
            ey_row = pltpu.roll(e_ext[LZ + layer, more, :], CHUNK + 7, 0)[:CHUNK]
            ez_col = pltpu.roll(ez, width - 1, 1)
            ex_col = pltpu.roll(ex[layer], width - 1, 1)
            curl_x = ez_col - ez - (ey[layer + 1] - ey[layer])
            curl_y = ex[layer + 1] - ex[layer] - (ez_row - ez)
            curl_z = ey_row - ey[layer] - (ex_col - ex[layer])
            for part, curl in enumerate((curl_x, curl_y, curl_z)):
                plane = part * LZ + layer
                h_ext[plane, now, :] = h_ext[plane, now, :] - factor * curl
        return carry

    def electric_pass(moment, last, index, carry):
        r = pl.multiple_of(index * CHUNK, CHUNK)
        now = pl.ds(r, CHUNK)
        more = pl.ds(pl.multiple_of(r - 8, 8), CHUNK + 8)
        drive = math.sin(source_rate * moment)
        zero = jnp.zeros((CHUNK, width), jnp.float32)
        hx = [zero] + [h_ext[layer, now, :] for layer in range(LZ)]
        hy = [zero] + [h_ext[LZ + layer, now, :] for layer in range(LZ)]
        for layer in range(LZ):
            hz = h_ext[2 * LZ + layer, now, :]
            hz_row = pltpu.roll(h_ext[2 * LZ + layer, more, :], 1, 0)[8:]
            hy_row = pltpu.roll(h_ext[LZ + layer, more, :], 1, 0)[8:]
            hx_now, hy_now = hx[layer + 1], hy[layer + 1]
            hz_col = pltpu.roll(hz, 1, 1)
            hx_col = pltpu.roll(hx_now, 1, 1)
            curl_x = hz - hz_col - (hy_now - hy[layer])
            curl_y = hx_now - hx[layer] - (hz - hz_row)
            curl_z = hy_now - hy_row - (hx_now - hx_col)
            factor = scale[layer, now, :]
            new_x = e_ext[layer, now, :] + factor * curl_x
            new_y = e_ext[LZ + layer, now, :] + factor * curl_y
            new_z = e_ext[2 * LZ + layer, now, :] + factor * curl_z + drive * src[layer, now, :]
            e_ext[layer, now, :] = new_x
            e_ext[LZ + layer, now, :] = new_y
            e_ext[2 * LZ + layer, now, :] = new_z
            if layer == FACE:
                faces = (-hy_now, hx_now, new_y, -new_x)
                for item, face in enumerate(faces):
                    if last:
                        old = first[item, now, :]
                        here = pl.ds(r - BASE, CHUNK)
                        for which, value in enumerate((old + face, face - old)):
                            share, place = divmod(which * EACH + item % EACH, per)
                            for q in range(cols // LANES):
                                piece = value[:, q * LANES : (q + 1) * LANES].astype(jnp.bfloat16)
                                lanes = pl.ds(place * LANES, LANES)
                                sd_outs[item // EACH][q * (2 * EACH // per) + share, here, lanes] = piece
                    else:
                        first[item, now, :] = face
        return carry

    chunks = high // CHUNK
    main0 = BASE // CHUNK
    main1 = main0 + rows // CHUNK
    lax.fori_loop(1, chunks - 1, magnetic_pass, 0)
    lax.fori_loop(1, chunks - 1, functools.partial(electric_pass, 1.0, False), 0)
    lax.fori_loop(1, main1, magnetic_pass, 0)
    out_h = pltpu.make_async_copy(h_ext.at[:, main_r, pl.ds(0, cols)], h_out, sems.at[3])
    out_h.start()
    lax.fori_loop(main0, main1, functools.partial(electric_pass, 2.0, True), 0)
    out_e = pltpu.make_async_copy(e_ext.at[:, main_r, pl.ds(0, cols)], e_out, sems.at[4])
    out_e.start()
    out_h.wait()
    out_e.wait()


def yee(e_field, h_field, material, eps_table, src_pos, src_amp):
    rows, cols = material.shape[1:]
    gx = lax.axis_size("gx")
    per = fields_per_device(gx, cols)
    grid_rows = rows * gx
    grid_cols = cols * lax.axis_size("gy")
    planes = 3 * LZ
    e = e_field.reshape(planes, rows, cols)
    h = h_field.reshape(planes, rows, cols)

    high = rows + 2 * BASE
    width = cols + PAD
    f32 = jnp.float32
    out = pl.pallas_call(
        functools.partial(yee_kernel, grid_rows, grid_cols, per),
        out_shape=(
            jax.ShapeDtypeStruct((planes, rows, cols), f32),
            jax.ShapeDtypeStruct((planes, rows, cols), f32),
        )
        + (jax.ShapeDtypeStruct((gx, rows, per * LANES), jnp.bfloat16),) * SETS,
        in_specs=[ANY, ANY, ANY, VM, VM, VM, VM, SM, VM, VM],
        out_specs=(ANY, ANY) + (VM,) * SETS,
        scratch_shapes=[
            pltpu.VMEM((planes, high, width), f32),
            pltpu.VMEM((planes, high, width), f32),
            pltpu.VMEM((LZ, rows, cols), jnp.int32),
            pltpu.VMEM((LZ, high, width), f32),
            pltpu.VMEM((LZ, high, width), f32),
            pltpu.VMEM((4, high, width), f32),
            pltpu.SemaphoreType.DMA((5,)),
        ],
        compiler_params=pltpu.CompilerParams(vmem_limit_bytes=BIG),
        name="yee",
    )(
        e, h, material, *halo(e, h, material),
        eps_table, jnp.swapaxes(src_pos, 0, 1), src_amp[None, :],
    )
    return out


SIN = (-1.0 / 6.0, 1.0 / 120.0, -1.0 / 5040.0, 1.0 / 362880.0)
COS = (-0.5, 1.0 / 24.0, -1.0 / 720.0, 1.0 / 40320.0, -1.0 / 3628800.0)


def unit(phase, period):
    eighth = period // 8
    turn = phase & (period - 1)
    quarter = (turn + eighth) // (2 * eighth)
    x = (turn - quarter * (2 * eighth)).astype(jnp.float32) * (2.0 * math.pi / period)
    square = x * x
    sine = jnp.full_like(x, SIN[-1])
    for factor in SIN[-2::-1]:
        sine = sine * square + factor
    sine = x + x * (square * sine)
    cosine = jnp.full_like(x, COS[-1])
    for factor in COS[-2::-1]:
        cosine = cosine * square + factor
    cosine = 1.0 + square * cosine
    odd = (quarter & 1) == 1
    re = jnp.where(odd, sine, cosine)
    im = jnp.where(odd, cosine, sine)
    re = jnp.where(((quarter + 1) & 2) == 2, -re, re)
    im = jnp.where((quarter & 2) == 2, im, -im)
    return re, im


def layout(gx, gy):
    mper = max(8, NA // 2 // (gx * gy))
    return mper, NA // 2 // mper, NA // gx // mper


def far_kernel(grid_rows, grid_cols, freqs, *rest):
    sd, outs, rest = rest[:SETS], rest[SETS : 2 * SETS], rest[2 * SETS :]
    x_tab, y_tab, v, g, left, left_x, held, held_x, *sems = rest
    send_v, recv_v, send_g, recv_g, send_x, recv_x, send_f, recv_f, send_1, recv_1, send_e = sems
    gx, gy = lax.axis_size("gx"), lax.axis_size("gy")
    i, z = lax.axis_index("gx"), lax.axis_index("gy")
    me = i * gy + z
    count = gx * gy
    rows = grid_rows // gx
    cols = grid_cols // gy
    per = v.shape[2] // LANES
    split = 2 * EACH // per
    slabs = cols // LANES
    mper, owners, near = layout(gx, gy)
    own = 2 * mper
    vb = NA // gy
    wide = NF * EACH * 2
    half = gx // 2
    mesh_id = pl.DeviceIdType.MESH

    upper = i >= half
    plane = jnp.where(upper, i - half, half - 1 - i)
    turn = jnp.where(upper, 0, gy) + z
    block_id = plane * near + turn

    def owner(t):
        c, r = lax.div(t, near), lax.rem(t, near)
        return jnp.where(r < gy, half + c, half - 1 - c), lax.rem(r, gy)

    end_i, end_z = owner(jnp.int32(owners - 1))

    def ship(src, dst, where, send_sem, recv_sem, start):
        here = (where[0] == i) & (where[1] == z)

        @pl.when(~here)
        def _():
            copy = pltpu.make_async_remote_copy(
                src_ref=src, dst_ref=dst, send_sem=send_sem, recv_sem=recv_sem,
                device_id=where, device_id_type=mesh_id,
            )
            if start:
                copy.start()
            else:
                copy.wait_send()

        if start:

            @pl.when(here)
            def _():
                pltpu.make_async_copy(src, dst, recv_sem).start()

    def arrived(ref, sem):
        pltpu.make_async_copy(ref, ref, sem).wait()

    barrier = pltpu.get_barrier_semaphore()
    for offset in range(1, count):
        peer = lax.rem(me + offset, count)
        pl.semaphore_signal(
            barrier, inc=1, device_id=(lax.div(peer, gy), lax.rem(peer, gy)), device_id_type=mesh_id
        )
    pl.semaphore_wait(barrier, count - 1)

    def v_ship(s, offset, start):
        peer = lax.rem(i + offset, gx)
        here = pl.ds(pl.multiple_of(i * rows, rows), rows)
        ship(sd[s].at[peer], v.at[s, here], (peer, z), send_v.at[s, offset], recv_v.at[s, i], start)

    def g_ship(s, t, start):
        lane = pl.multiple_of((z * slabs + lax.div(i, split)) * LANES, LANES)
        to = (pl.ds(lax.rem(i, split) * per, per), slice(None), pl.ds(lane, LANES))
        part = g.at[s, :, pl.ds(pl.multiple_of(t * own, own), own), :]
        ship(part, left.at[(s, *to)], owner(t), send_g.at[s, t], recv_g.at[s, me], start)

    def x_ship(s, start):
        lane = pl.multiple_of((z * slabs + lax.div(i, split)) * LANES, LANES)
        to = (pl.ds(lax.rem(i, split) * per, per), slice(None), pl.ds(lane, LANES))
        part = g.at[s, :, pl.ds(owners * own, 16), :]
        ship(part, left_x.at[(s, *to)], (end_i, end_z), send_x.at[s], recv_x.at[s, me], start)

    def f_ship(s, step, start):
        peer = lax.rem(z + step, gy)
        at = pl.ds(pl.multiple_of(turn * mper, mper), mper)
        ship(
            held.at[s, peer, 0], outs[s].at[at], (half + plane, peer),
            send_f.at[s, 0, step - 1], recv_f.at[s, turn], start,
        )
        mirror = near - 1 - turn
        at = pl.ds(mirror * mper + 1, mper - 1)
        ship(
            held.at[s, peer, 1, pl.ds(0, mper - 1)], outs[s].at[at], (half - 1 - plane, peer),
            send_f.at[s, 1, step - 1], recv_f.at[s, mirror], start,
        )
        first = turn == 0
        to = jnp.where(first, half - plane, half - 1 - plane)
        slot = jnp.where(first, 0, near - turn)

        @pl.when(block_id > 0)
        def _():
            ship(
                held.at[s, peer, 1, pl.ds(mper - 1, 1)], outs[s].at[pl.ds(slot * mper, 1)], (to, peer),
                send_1.at[s, step - 1], recv_1.at[s, slot], start,
            )

    def e_ship(s, step, start):
        peer = lax.rem(z + step, gy)
        ship(
            held_x.at[s, peer], outs[s].at[pl.ds(0, 1)], (0, peer),
            send_e.at[s, step - 1], recv_1.at[s, 0], start,
        )

    def fill_x(m, row):
        low = lax.broadcasted_iota(jnp.int32, m.shape, 1)
        a_re, a_im = unit(m * (low * LANES), zoom_factor * grid_rows)
        b_re, b_im = unit(m * low, zoom_factor * grid_rows)
        for block in range(grid_rows // LANES):
            h_re, h_im = a_re[:, block : block + 1], a_im[:, block : block + 1]
            re = h_re * b_re - h_im * b_im
            im = h_re * b_im + h_im * b_re
            both = jnp.concatenate([re, im], 0).astype(jnp.bfloat16)
            x_tab[pl.ds(row, 2 * m.shape[0]), block * LANES : (block + 1) * LANES] = both

    def build_x():
        row = lax.broadcasted_iota(jnp.int32, (mper, LANES), 0)

        def body(t, carry):
            fill_x(row + t * mper, pl.multiple_of(t * own, own))
            return carry

        lax.fori_loop(0, owners, body, 0)
        fill_x(jnp.full((8, LANES), NA // 2, jnp.int32), owners * own)

    def build_y():
        tall = 32
        low = lax.broadcasted_iota(jnp.int32, (tall, LANES), 1)
        row = lax.broadcasted_iota(jnp.int32, (tall, LANES), 0)

        def body(d, carry):
            start = pl.multiple_of(d * tall, tall)
            y = row + start
            a_re, a_im = unit(y * (low * LANES + NA // 4), zoom_factor * grid_cols)
            b_re, b_im = unit(y * low, zoom_factor * grid_cols)
            for block in range(NA // LANES):
                h_re, h_im = a_re[:, block : block + 1], a_im[:, block : block + 1]
                at = slice(block * LANES, (block + 1) * LANES)
                y_tab[0, pl.ds(start, tall), at] = (h_re * b_re - h_im * b_im).astype(jnp.bfloat16)
                y_tab[1, pl.ds(start, tall), at] = (h_re * b_im + h_im * b_re).astype(jnp.bfloat16)
            return carry

        lax.fori_loop(0, grid_cols // tall, body, 0)

    inv_norm = 1.0 / math.sqrt(grid_rows * grid_cols)
    mix = []
    for f in range(NF):
        angle = jnp.full((8, LANES), 0.5 * freqs[f], jnp.float32)
        half_re, half_im = jnp.cos(angle), jnp.sin(angle)
        turn_re, turn_im = jnp.cos(3.0 * angle) * inv_norm, jnp.sin(3.0 * angle) * inv_norm
        four = (turn_re * half_re, turn_im * half_re, -turn_im * half_im, turn_re * half_im)
        mix.append([value[:1, :1] for value in four])

    dot = functools.partial(jnp.dot, preferred_element_type=jnp.float32)
    parts = 2
    group = owners // parts

    def transform_rows(s):
        for src in range(gx):
            arrived(v.at[s, pl.ds(src * rows, rows)], recv_v.at[s, src])

        def body(c, carry):
            chunk = lax.rem(lax.div(block_id, group) + 1 + c, parts)
            tall = group * own
            start = pl.multiple_of(chunk * tall, tall)
            both = dot(x_tab[pl.ds(start, tall + 16), :], v[s]).astype(jnp.bfloat16)
            for f in range(per):
                g[s, f, pl.ds(start, tall), :] = both[:tall, f * LANES : (f + 1) * LANES]

            @pl.when(chunk == parts - 1)
            def _():
                for f in range(per):
                    g[s, f, owners * own :, :] = both[tall:, f * LANES : (f + 1) * LANES]
                x_ship(s, True)

            for e in range(group):
                g_ship(s, chunk * group + e, True)
            return carry

        lax.fori_loop(0, parts, body, 0)

    def one_hot(shape, source):
        row = lax.broadcasted_iota(jnp.int32, shape, 0)
        col = lax.broadcasted_iota(jnp.int32, shape, 1)
        return jnp.where(col == source(row), 1.0, 0.0).astype(jnp.bfloat16)

    size = (wide * mper, wide * mper)
    forth = one_hot(size, lambda row: lax.rem(row, wide) * mper + lax.div(row, wide))
    back = one_hot(size, lambda row: lax.rem(row, wide) * mper + mper - 1 - lax.div(row, wide))
    only = one_hot((wide, wide * 8), lambda row: row * 8)

    def finish(lhs, count_m, peer):
        at = pl.ds(pl.multiple_of(peer * vb, vb), vb)
        p_re, p_im = dot(lhs, y_tab[0, :, at]), dot(lhs, y_tab[1, :, at])
        plus, minus = [], []

        def both_signs(f):
            top = slice(2 * f * count_m, (2 * f + 1) * count_m)
            low = slice((2 * f + 1) * count_m, (2 * f + 2) * count_m)
            a_re, a_im, b_re, b_im = p_re[top], p_im[top], p_re[low], p_im[low]
            return (a_re - b_im, a_im + b_re), (a_re + b_im, a_im - b_re)

        fields = [both_signs(f) for f in range(2 * EACH)]
        for f in range(NF):
            p0, p1, q0, q1 = mix[f]
            for k in range(EACH):
                for sign, result in enumerate((plus, minus)):
                    s_re, s_im = fields[k][sign]
                    d_re, d_im = fields[EACH + k][sign]
                    result.append(p0 * s_re - p1 * s_im + (q0 * d_re - q1 * d_im))
                    result.append(p0 * s_im + p1 * s_re + (q0 * d_im + q1 * d_re))
        pack = lambda result: jnp.concatenate(result, 0).astype(jnp.bfloat16)
        return pack(plus), pack(minus)

    def transform_cols(s):
        for src in range(count):
            src_i, src_z = divmod(src, gy)
            lane = (src_z * slabs + src_i // split) * LANES
            region = left.at[s, pl.ds(src_i % split * per, per), :, pl.ds(lane, LANES)]
            arrived(region, recv_g.at[s, src])
        lhs = left[s].reshape(2 * EACH * own, grid_cols)
        for step in range(1, gy + 1):
            peer = lax.rem(z + step, gy)
            plus, minus = finish(lhs, mper, peer)
            held[s, peer, 0] = dot(forth, plus).reshape(mper, wide, vb).astype(jnp.bfloat16)
            held[s, peer, 1] = dot(back, minus).reshape(mper, wide, vb).astype(jnp.bfloat16)
            f_ship(s, step, True)

    at_end = (i == end_i) & (z == end_z)

    def transform_end(s):
        for src in range(count):
            src_i, src_z = divmod(src, gy)
            lane = (src_z * slabs + src_i // split) * LANES
            region = left_x.at[s, pl.ds(src_i % split * per, per), :, pl.ds(lane, LANES)]
            arrived(region, recv_x.at[s, src])
        lhs = left_x[s].reshape(2 * EACH * 16, grid_cols)
        for step in range(1, gy + 1):
            peer = lax.rem(z + step, gy)
            _, minus = finish(lhs, 8, peer)
            held_x[s, peer] = dot(only, minus).reshape(1, wide, vb).astype(jnp.bfloat16)
            e_ship(s, step, True)

    def owned(body):
        if near == 2 * gy:
            body()
        else:
            pl.when(turn < near)(body)

    for s in range(SETS):
        for offset in range(gx):
            v_ship(s, offset, True)
    build_x()
    transform_rows(0)
    build_y()
    for s in range(1, SETS):
        transform_rows(s)
    for s in range(SETS):
        owned(functools.partial(transform_cols, s))
        pl.when(at_end)(functools.partial(transform_end, s))
    for s in range(SETS):

        @pl.when(upper)
        def _():
            for slot in range(near):
                arrived(outs[s].at[pl.ds(slot * mper, mper)], recv_f.at[s, slot])

        @pl.when(~upper)
        def _():
            for slot in range(near):
                arrived(outs[s].at[pl.ds(slot * mper + 1, mper - 1)], recv_f.at[s, slot])
                arrived(outs[s].at[pl.ds(slot * mper, 1)], recv_1.at[s, slot])

    for s in range(SETS):
        for offset in range(gx):
            v_ship(s, offset, False)
        x_ship(s, False)
        for t in range(owners):
            g_ship(s, jnp.int32(t), False)

        def sent():
            for step in range(1, gy + 1):
                f_ship(s, step, False)

        owned(sent)

        @pl.when(at_end)
        def _():
            for step in range(1, gy + 1):
                e_ship(s, step, False)


def order_kernel(*refs):
    *parts, out = refs
    for s, part in enumerate(parts):
        block = part[...].astype(jnp.float32)
        for f in range(NF):
            for k in range(EACH):
                at = 2 * (f * EACH + k)
                out[:, f * 4 + s * EACH + k] = block[:, at : at + 2]


def far(sd, freqs, grid_rows, grid_cols):
    gx, gy = lax.axis_size("gx"), lax.axis_size("gy")
    count = gx * gy
    nu, vb = NA // gx, NA // gy
    mper, owners, near = layout(gx, gy)
    lanes = sd[0].shape[2]
    wide = NF * EACH * 2
    bf16 = jnp.bfloat16
    dma = pltpu.SemaphoreType.DMA
    done = pl.pallas_call(
        functools.partial(far_kernel, grid_rows, grid_cols),
        out_shape=(jax.ShapeDtypeStruct((nu, wide, vb), bf16),) * SETS,
        in_specs=[SM] + [ANY] * SETS,
        out_specs=(ANY,) * SETS,
        scratch_shapes=[
            pltpu.VMEM((NA + 16, grid_rows), bf16),
            pltpu.VMEM((2, grid_cols, NA), bf16),
            pltpu.VMEM((SETS, grid_rows, lanes), bf16),
            pltpu.VMEM((SETS, lanes // LANES, NA + 16, LANES), bf16),
            pltpu.VMEM((SETS, 2 * EACH, 2 * mper, grid_cols), bf16),
            pltpu.VMEM((SETS, 2 * EACH, 16, grid_cols), bf16),
            pltpu.VMEM((SETS, gy, 2, mper, wide, vb), bf16),
            pltpu.VMEM((SETS, gy, 1, wide, vb), bf16),
            dma((SETS, gx)),
            dma((SETS, gx)),
            dma((SETS, owners)),
            dma((SETS, count)),
            dma((SETS,)),
            dma((SETS, count)),
            dma((SETS, 2, gy)),
            dma((SETS, near)),
            dma((SETS, gy)),
            dma((SETS, near)),
            dma((SETS, gy)),
        ],
        compiler_params=pltpu.CompilerParams(
            vmem_limit_bytes=BIG, collective_id=1, has_side_effects=True
        ),
        name="far",
    )(freqs, *sd)
    block = nu // 4
    return pl.pallas_call(
        order_kernel,
        grid=(4,),
        out_shape=jax.ShapeDtypeStruct((nu, NF * 4, 2, vb), jnp.float32),
        in_specs=[pl.BlockSpec((block, wide, vb), lambda n: (n, 0, 0))] * SETS,
        out_specs=pl.BlockSpec((block, NF * 4, 2, vb), lambda n: (n, 0, 0, 0)),
        name="order",
    )(*done)


def on_device(e_field, h_field, material, eps_table, src_pos, src_amp, freqs):
    rows, cols = material.shape[1:]
    grid_rows, grid_cols = rows * lax.axis_size("gx"), cols * lax.axis_size("gy")
    e_new, h_new, *sd = yee(e_field, h_field, material, eps_table, src_pos, src_amp)
    shape = e_field.shape
    return (e_new.reshape(shape), h_new.reshape(shape), far(sd, freqs, grid_rows, grid_cols))


def solution(mesh):
    placed = (
        P(None, None, "gx", "gy"),
        P(None, None, "gx", "gy"),
        P(None, "gx", "gy"),
        P(),
        P(),
        P(),
        P(),
    )
    return jax.shard_map(
        on_device,
        mesh=mesh,
        in_specs=placed,
        out_specs=(P(None, None, "gx", "gy"), P(None, None, "gx", "gy"), P("gx", None, None, "gy")),
        check_vma=False,
    )
```

```python
import functools
import math

import jax
import jax.numpy as jnp
from jax import lax
from jax.experimental import pallas as pl
from jax.experimental.pallas import tpu as pltpu
from jax.sharding import PartitionSpec as P

LZ = 3
FACE = 1
STEPS = 2
NF = 2
NA = 1024
NMAT = 8

courant = 0.5
source_rate = 0.7
zoom_factor = 4

BASE = 32
CHUNK = 16
PAIR = 32
SETS = 2
EACH = 4 // SETS
LANES = 128
PAD = 128
ANY = pl.BlockSpec(memory_space=pl.ANY)
VM = pl.BlockSpec(memory_space=pltpu.VMEM)
SM = pl.BlockSpec(memory_space=pltpu.SMEM)
BIG = 60 * 1024 * 1024


def halo_kernel(
    e, h, m, col_rim, corner, rim_f, rim_m,
    edge_f, edge_m, packed, got_col, got_corner, got_f, got_m, load, send, recv,
):
    gx, gy = lax.axis_size("gx"), lax.axis_size("gy")
    i, z = lax.axis_index("gx"), lax.axis_index("gy")
    planes, rows, cols = e.shape
    around = [(a, b) for a in (-1, 0, 1) for b in (-1, 0, 1) if (a, b) != (0, 0)]

    def exists(step):
        row, col = i + step[0], z + step[1]
        return (row >= 0) & (row < gx) & (col >= 0) & (col < gy)

    loads = []
    for side, lane in enumerate((0, cols - LANES)):
        at = pl.ds(lane, LANES)
        loads.append(pltpu.make_async_copy(e.at[:, :, at], edge_f.at[side, pl.ds(0, planes)], load.at[3 * side]))
        loads.append(pltpu.make_async_copy(h.at[:, :, at], edge_f.at[side, pl.ds(planes, planes)], load.at[3 * side + 1]))
        loads.append(pltpu.make_async_copy(m.at[:, :, at], edge_m.at[side], load.at[3 * side + 2]))
    for copy in loads:
        copy.start()
    barrier = pltpu.get_barrier_semaphore()
    total = jnp.int32(0)
    for step in around:
        total += exists(step).astype(jnp.int32)

        @pl.when(exists(step))
        def _():
            pl.semaphore_signal(
                barrier, inc=1, device_id=(i + step[0], z + step[1]), device_id_type=pl.DeviceIdType.MESH
            )

    pl.semaphore_wait(barrier, total)

    def remote(step, src, dst, index):
        copy = pltpu.make_async_remote_copy(
            src_ref=src, dst_ref=dst, send_sem=send.at[index], recv_sem=recv.at[index],
            device_id=(i + step[0], z + step[1]), device_id_type=pl.DeviceIdType.MESH,
        )
        return step, copy

    rows_out, cols_out = [], []
    for side, low in enumerate((0, rows - 8)):
        step = (2 * side - 1, 0)
        at = pl.ds(low, 8)
        rows_out.append(remote(step, e.at[:, at, :], got_f.at[side, pl.ds(0, planes)], 3 * side))
        rows_out.append(remote(step, h.at[:, at, :], got_f.at[side, pl.ds(planes, planes)], 3 * side + 1))
        rows_out.append(remote(step, m.at[:, at, :], got_m.at[side], 3 * side + 2))
    for side in range(2):
        cols_out.append(remote((0, 2 * side - 1), packed.at[side], got_col.at[side], 6 + side))
        for end, low in enumerate((0, rows - 8)):
            step = (2 * end - 1, 2 * side - 1)
            src = packed.at[side, pl.ds(low, 8)]
            cols_out.append(remote(step, src, got_corner.at[end, side], 8 + 2 * side + end))

    def start(copies):
        for step, copy in copies:

            @pl.when(exists(step))
            def _():
                copy.start()

    start(rows_out)
    for copy in loads:
        copy.wait()
    tall = 32
    lane = lax.broadcasted_iota(jnp.int32, (tall, LANES), 1)

    def pack(c, carry):
        at = pl.ds(pl.multiple_of(c * tall, tall), tall)
        for side in range(2):
            place = ((lane + 2 * side) & (LANES - 1)) >> 2
            block = jnp.zeros((tall, LANES), jnp.float32)
            for p in range(2 * planes + LZ):
                if p < 2 * planes:
                    piece = edge_f[side, p, at, :]
                else:
                    piece = edge_m[side, p - 2 * planes, at, :].astype(jnp.float32)
                block = jnp.where(place == p, pltpu.roll(piece, 4 * p, 1), block)
            packed[side, at, :] = block
        return carry

    lax.fori_loop(0, rows // tall, pack, 0)
    start(cols_out)
    for step, copy in rows_out + cols_out:

        @pl.when(exists((-step[0], -step[1])))
        def _():
            copy.wait_recv()

    last = (lane & 2) == 0
    after, before = exists((0, 1)), exists((0, -1))

    def merge(c, carry):
        at = pl.ds(pl.multiple_of(c * tall, tall), tall)
        right = jnp.where(after, got_col[0, at, :], 0.0)
        left = jnp.where(before, got_col[1, at, :], 0.0)
        col_rim[at, :] = jnp.where(last, right, left)
        return carry

    lax.fori_loop(0, rows // tall, merge, 0)
    for side in range(2):
        there = exists((1 - 2 * side, 0))
        rim_f[side] = jnp.where(there, got_f[side], 0.0)
        rim_m[side] = jnp.where(there, got_m[side], 0)
        right = jnp.where(there & after, got_corner[side, 0], 0.0)
        left = jnp.where(there & before, got_corner[side, 1], 0.0)
        corner[side] = jnp.where(last[:8], right, left)
    for step, copy in rows_out + cols_out:

        @pl.when(exists(step))
        def _():
            copy.wait_send()


def halo(e, h, m):
    planes, rows, cols = e.shape
    f32, i32 = jnp.float32, jnp.int32
    dma = pltpu.SemaphoreType.DMA
    return pl.pallas_call(
        halo_kernel,
        out_shape=(
            jax.ShapeDtypeStruct((rows, LANES), f32),
            jax.ShapeDtypeStruct((2, 8, LANES), f32),
            jax.ShapeDtypeStruct((2, 2 * planes, 8, cols), f32),
            jax.ShapeDtypeStruct((2, LZ, 8, cols), i32),
        ),
        in_specs=[ANY] * 3,
        out_specs=(VM,) * 4,
        scratch_shapes=[
            pltpu.VMEM((2, 2 * planes, rows, LANES), f32),
            pltpu.VMEM((2, LZ, rows, LANES), i32),
            pltpu.VMEM((2, rows, LANES), f32),
            pltpu.VMEM((2, rows, LANES), f32),
            pltpu.VMEM((2, 2, 8, LANES), f32),
            pltpu.VMEM((2, 2 * planes, 8, cols), f32),
            pltpu.VMEM((2, LZ, 8, cols), i32),
            dma((6,)),
            dma((12,)),
            dma((12,)),
        ],
        compiler_params=pltpu.CompilerParams(collective_id=0, has_side_effects=True),
        name="halo",
    )(e, h, m)


def fields_per_device(gx, cols):
    return 2 * EACH * cols // (gx * LANES)


def yee_kernel(
    grid_rows, grid_cols, per,
    e_hbm, h_hbm, m_hbm, col_rim, corner, rim_f, rim_m, eps, pos, amp,
    e_out, h_out, *rest,
):
    sd_outs, (e_ext, h_ext, m_main, scale, src, first, *sd, sems) = rest[:SETS], rest[SETS:]
    rows, cols = m_main.shape[1:]
    width = cols + PAD
    high = e_ext.shape[1]
    row0 = lax.axis_index("gx") * rows
    col0 = lax.axis_index("gy") * cols
    pairs = rows // PAIR

    def load(q):
        here, there = pl.ds(PAIR * q, PAIR), pl.ds(BASE + PAIR * q, PAIR)
        return [
            pltpu.make_async_copy(e_hbm.at[:, here, :], e_ext.at[:, there, pl.ds(0, cols)], sems.at[0, q]),
            pltpu.make_async_copy(h_hbm.at[:, here, :], h_ext.at[:, there, pl.ds(0, cols)], sems.at[1, q]),
            pltpu.make_async_copy(m_hbm.at[:, here, :], m_main.at[:, here, :], sems.at[2, q]),
        ]

    def store(q):
        here, there = pl.ds(PAIR * q, PAIR), pl.ds(BASE + PAIR * q, PAIR)
        return [
            pltpu.make_async_copy(e_ext.at[:, there, pl.ds(0, cols)], e_out.at[:, here, :], sems.at[3, q]),
            pltpu.make_async_copy(h_ext.at[:, there, pl.ds(0, cols)], h_out.at[:, here, :], sems.at[4, q]),
        ] + [
            pltpu.make_async_copy(sd[s].at[:, here, :], sd_outs[s].at[:, here, :], sems.at[5 + s, q])
            for s in range(SETS)
        ]

    for q in range(pairs):
        for copy in load(q):
            copy.start()
    count = amp.shape[1]
    used = high - 2 * CHUNK
    bf16 = jnp.bfloat16
    gather = functools.partial(
        lax.dot_general, dimension_numbers=(((1,), (1,)), ((), ())), preferred_element_type=jnp.float32
    )
    tall_at = lambda shape: row0 + lax.broadcasted_iota(jnp.int32, shape, 0) + (CHUNK - BASE)
    lane = lax.broadcasted_iota(jnp.int32, (width, LANES), 0)
    col_at = (col0 + jnp.where(lane < cols + PAD // 2, lane, lane - width)).astype(jnp.float32)
    row_at = tall_at((used, LANES)).astype(jnp.float32)
    row_s = jnp.broadcast_to(pos[1:2, :], (8, count))
    col_s = jnp.broadcast_to(pos[2:3, :], (8, count))
    inside = (row_s >= row0 - (BASE - CHUNK)) & (row_s < row0 + used - (BASE - CHUNK))
    inside &= (col_s >= col0 - PAD // 2) & (col_s < col0 + cols + PAD // 2)
    rank = jnp.where(inside, 1.0, 0.0)
    at_lane = lax.broadcasted_iota(jnp.int32, (8, count), 1)
    reach = 1
    while reach < count:
        rank = rank + jnp.where(at_lane >= reach, pltpu.roll(rank, reach, 1), 0.0)
        reach *= 2
    found = jnp.max(rank).astype(jnp.int32)
    rank = jnp.where(inside, rank, 0.0)[:1]
    hi = amp[...].astype(bf16).astype(jnp.float32)
    mid = (amp[...] - hi).astype(bf16).astype(jnp.float32)
    low = amp[...] - hi - mid
    parts = [
        (pos[1:2, :] >> 6).astype(jnp.float32), (pos[1:2, :] & 63).astype(jnp.float32),
        (pos[2:3, :] >> 6).astype(jnp.float32), (pos[2:3, :] & 63).astype(jnp.float32),
        pos[0:1, :].astype(jnp.float32), hi, mid, low,
    ]
    parts = jnp.concatenate(parts, 0).astype(bf16)
    for layer in range(LZ):
        src[layer] = jnp.zeros((high, width), jnp.float32)
    slot = lax.broadcasted_iota(jnp.int32, (LANES, count), 0).astype(jnp.float32)

    def place(group, carry):
        pick = jnp.where(slot + (group * LANES + 1).astype(jnp.float32) == rank, 1.0, 0.0)
        some = gather(parts, pick.astype(bf16))
        row, col = some[0:1] * 64.0 + some[1:2], some[2:3] * 64.0 + some[3:4]
        hit_col = jnp.where(col_at == col, 1.0, 0.0).astype(bf16)
        hit_col = jnp.concatenate([hit_col] * 3, 1)
        hit_row = row_at == row
        for layer in range(LZ):
            hit = hit_row & (some[4:5] == float(layer))
            left = [jnp.where(hit, some[p : p + 1], 0.0).astype(bf16) for p in (5, 6, 7)]
            src[layer, CHUNK : CHUNK + used, :] += gather(jnp.concatenate(left, 1), hit_col)
        return carry

    lax.fori_loop(0, lax.div(found + (LANES - 1), LANES), place, 0)

    def scale_of(index, row, col):
        value = jnp.full(index.shape, eps[0], jnp.float32)
        for material in range(1, NMAT):
            value = jnp.where(index == material, eps[material], value)
        inside = (row >= 0) & (row < grid_rows) & (col >= 0) & (col < grid_cols)
        return jnp.where(inside, courant / value, 0.0)

    col_main = col0 + lax.broadcasted_iota(jnp.int32, (CHUNK, cols), 1)
    lane_pad = lax.broadcasted_iota(jnp.int32, (CHUNK, PAD), 1)
    col_pad = col0 + jnp.where(lane_pad < PAD // 2, cols + lane_pad, lane_pad - PAD)
    row_chunk = row0 + lax.broadcasted_iota(jnp.int32, (CHUNK, cols), 0)

    def shown(block, plane):
        return pltpu.roll(block, PAD - 4 * plane, 1) if plane else block

    def fill(step_index, carry):
        r = pl.multiple_of(step_index * CHUNK, CHUNK)
        near = pl.ds(r, CHUNK)
        far = pl.ds(BASE + r, CHUNK)
        block = col_rim[near, :]
        for layer in range(LZ):
            scale[layer, far, :cols] = scale_of(m_main[layer, near, :], row_chunk + r, col_main)
            scale[layer, far, cols:] = scale_of(
                shown(block, 6 * LZ + layer), row_chunk[:, :PAD] + r, col_pad
            )
        for plane in range(3 * LZ):
            e_ext[plane, far, cols:] = shown(block, plane)
            h_ext[plane, far, cols:] = shown(block, 3 * LZ + plane)
        return carry

    row_eight = row0 + lax.broadcasted_iota(jnp.int32, (8, cols), 0)
    blank = jnp.zeros((8, width), jnp.float32)
    for side, target, offset, spare in (
        (0, BASE + rows, rows, BASE + rows + 8),
        (1, BASE - 8, -8, BASE - 16),
    ):
        here = slice(target, target + 8)
        block = corner[side]
        for layer in range(LZ):
            scale[layer, here, :cols] = scale_of(
                rim_m[side, layer], row_eight + offset, col_main[:8]
            )
            scale[layer, here, cols:] = scale_of(
                shown(block, 6 * LZ + layer), row_eight[:, :PAD] + offset, col_pad[:8]
            )
            scale[layer, spare : spare + 8, :] = blank
        for plane in range(3 * LZ):
            e_ext[plane, here, :cols] = rim_f[side, plane]
            h_ext[plane, here, :cols] = rim_f[side, 3 * LZ + plane]
            e_ext[plane, here, cols:] = shown(block, plane)
            h_ext[plane, here, cols:] = shown(block, 3 * LZ + plane)
            e_ext[plane, spare : spare + 8, :] = blank
            h_ext[plane, spare : spare + 8, :] = blank
    for plane in range(3 * LZ):
        e_ext[plane, high - 16 : high, :] = jnp.zeros((16, width), jnp.float32)
        h_ext[plane, 0:16, :] = jnp.zeros((16, width), jnp.float32)
    lane_c = lax.broadcasted_iota(jnp.int32, (CHUNK, width), 1)
    col_c = col0 + jnp.where(lane_c < cols + PAD // 2, lane_c, lane_c - width)
    weight = jnp.where(col_c >= 0, courant, 0.0)
    top = lax.axis_index("gx") == 0

    def magnetic_pass(index, carry):
        r = pl.multiple_of(index * CHUNK, CHUNK)
        now = pl.ds(r, CHUNK)
        more = pl.ds(r, CHUNK + 8)
        factor = weight * jnp.where(top & (index * CHUNK < BASE), 0.0, 1.0)
        zero = jnp.zeros((CHUNK, width), jnp.float32)
        ex = [e_ext[layer, now, :] for layer in range(LZ)] + [zero]
        ey = [e_ext[LZ + layer, now, :] for layer in range(LZ)] + [zero]
        for layer in range(LZ):
            ez = e_ext[2 * LZ + layer, now, :]
            ez_row = pltpu.roll(e_ext[2 * LZ + layer, more, :], CHUNK + 7, 0)[:CHUNK]
            ey_row = pltpu.roll(e_ext[LZ + layer, more, :], CHUNK + 7, 0)[:CHUNK]
            ez_col = pltpu.roll(ez, width - 1, 1)
            ex_col = pltpu.roll(ex[layer], width - 1, 1)
            curl_x = ez_col - ez - (ey[layer + 1] - ey[layer])
            curl_y = ex[layer + 1] - ex[layer] - (ez_row - ez)
            curl_z = ey_row - ey[layer] - (ex_col - ex[layer])
            for part, curl in enumerate((curl_x, curl_y, curl_z)):
                plane = part * LZ + layer
                h_ext[plane, now, :] = h_ext[plane, now, :] - factor * curl
        return carry

    def electric_pass(moment, last, index, carry):
        r = pl.multiple_of(index * CHUNK, CHUNK)
        now = pl.ds(r, CHUNK)
        more = pl.ds(pl.multiple_of(r - 8, 8), CHUNK + 8)
        drive = math.sin(source_rate * moment)
        zero = jnp.zeros((CHUNK, width), jnp.float32)
        hx = [zero] + [h_ext[layer, now, :] for layer in range(LZ)]
        hy = [zero] + [h_ext[LZ + layer, now, :] for layer in range(LZ)]
        for layer in range(LZ):
            hz = h_ext[2 * LZ + layer, now, :]
            hz_row = pltpu.roll(h_ext[2 * LZ + layer, more, :], 1, 0)[8:]
            hy_row = pltpu.roll(h_ext[LZ + layer, more, :], 1, 0)[8:]
            hx_now, hy_now = hx[layer + 1], hy[layer + 1]
            hz_col = pltpu.roll(hz, 1, 1)
            hx_col = pltpu.roll(hx_now, 1, 1)
            curl_x = hz - hz_col - (hy_now - hy[layer])
            curl_y = hx_now - hx[layer] - (hz - hz_row)
            curl_z = hy_now - hy_row - (hx_now - hx_col)
            factor = scale[layer, now, :]
            new_x = e_ext[layer, now, :] + factor * curl_x
            new_y = e_ext[LZ + layer, now, :] + factor * curl_y
            new_z = e_ext[2 * LZ + layer, now, :] + factor * curl_z + drive * src[layer, now, :]
            e_ext[layer, now, :] = new_x
            e_ext[LZ + layer, now, :] = new_y
            e_ext[2 * LZ + layer, now, :] = new_z
            if layer == FACE:
                faces = (-hy_now, hx_now, new_y, -new_x)
                for item, face in enumerate(faces):
                    if last:
                        old = first[item, now, :]
                        here = pl.ds(r - BASE, CHUNK)
                        for which, value in enumerate((old + face, face - old)):
                            share, place = divmod(which * EACH + item % EACH, per)
                            for q in range(cols // LANES):
                                piece = value[:, q * LANES : (q + 1) * LANES].astype(jnp.bfloat16)
                                lanes = pl.ds(place * LANES, LANES)
                                sd[item // EACH][q * (2 * EACH // per) + share, here, lanes] = piece
                    else:
                        first[item, now, :] = face
        return carry

    def arrive(q):
        for copy in load(q):
            copy.wait()
        for part in range(PAIR // CHUNK):
            fill(q * (PAIR // CHUNK) + part, 0)

    def advance(n, second):
        magnetic_pass(n, 0)
        electric_pass(1.0, False, n, 0)
        magnetic_pass(n - 1, 0)
        if second:
            electric_pass(2.0, True, n - 1, 0)

    start = BASE // CHUNK
    arrive(0)
    magnetic_pass(start - 1, 0)
    electric_pass(1.0, False, start - 1, 0)
    advance(start, False)

    def wave(q, carry):
        @pl.when(q < pairs - 1)
        def _():
            arrive(q + 1)

        for part in range(PAIR // CHUNK):
            advance(start + 1 + q * (PAIR // CHUNK) + part, True)
        for copy in store(q):
            copy.start()
        return carry

    lax.fori_loop(0, pairs, wave, 0)
    for q in range(pairs):
        for copy in store(q):
            copy.wait()


def yee(e_field, h_field, material, eps_table, src_pos, src_amp):
    rows, cols = material.shape[1:]
    gx = lax.axis_size("gx")
    per = fields_per_device(gx, cols)
    grid_rows = rows * gx
    grid_cols = cols * lax.axis_size("gy")
    planes = 3 * LZ
    e = e_field.reshape(planes, rows, cols)
    h = h_field.reshape(planes, rows, cols)

    high = rows + 2 * BASE
    width = cols + PAD
    f32 = jnp.float32
    out = pl.pallas_call(
        functools.partial(yee_kernel, grid_rows, grid_cols, per),
        out_shape=(
            jax.ShapeDtypeStruct((planes, rows, cols), f32),
            jax.ShapeDtypeStruct((planes, rows, cols), f32),
        )
        + (jax.ShapeDtypeStruct((gx, rows, per * LANES), jnp.bfloat16),) * SETS,
        in_specs=[ANY, ANY, ANY, VM, VM, VM, VM, SM, VM, VM],
        out_specs=(ANY,) * (2 + SETS),
        scratch_shapes=[
            pltpu.VMEM((planes, high, width), f32),
            pltpu.VMEM((planes, high, width), f32),
            pltpu.VMEM((LZ, rows, cols), jnp.int32),
            pltpu.VMEM((LZ, high, width), f32),
            pltpu.VMEM((LZ, high, width), f32),
            pltpu.VMEM((4, high, width), f32),
        ]
        + [pltpu.VMEM((gx, rows, per * LANES), jnp.bfloat16)] * SETS
        + [
            pltpu.SemaphoreType.DMA((5 + SETS, rows // PAIR)),
        ],
        compiler_params=pltpu.CompilerParams(vmem_limit_bytes=BIG),
        name="yee",
    )(
        e, h, material, *halo(e, h, material),
        eps_table, jnp.swapaxes(src_pos, 0, 1), src_amp[None, :],
    )
    return out


SIN = (-1.0 / 6.0, 1.0 / 120.0, -1.0 / 5040.0, 1.0 / 362880.0)
COS = (-0.5, 1.0 / 24.0, -1.0 / 720.0, 1.0 / 40320.0, -1.0 / 3628800.0)


def unit(phase, period):
    eighth = period // 8
    turn = phase & (period - 1)
    quarter = (turn + eighth) // (2 * eighth)
    x = (turn - quarter * (2 * eighth)).astype(jnp.float32) * (2.0 * math.pi / period)
    square = x * x
    sine = jnp.full_like(x, SIN[-1])
    for factor in SIN[-2::-1]:
        sine = sine * square + factor
    sine = x + x * (square * sine)
    cosine = jnp.full_like(x, COS[-1])
    for factor in COS[-2::-1]:
        cosine = cosine * square + factor
    cosine = 1.0 + square * cosine
    odd = (quarter & 1) == 1
    re = jnp.where(odd, sine, cosine)
    im = jnp.where(odd, cosine, sine)
    re = jnp.where(((quarter + 1) & 2) == 2, -re, re)
    im = jnp.where((quarter & 2) == 2, im, -im)
    return re, im


def layout(gx, gy):
    mper = max(8, NA // 2 // (gx * gy))
    return mper, NA // 2 // mper, NA // gx // mper


def far_kernel(grid_rows, grid_cols, freqs, *rest):
    sd, outs, rest = rest[:SETS], rest[SETS : 2 * SETS], rest[2 * SETS :]
    x_tab, y_tab, v, g, left, left_x, held, held_x, *sems = rest
    send_v, recv_v, send_g, recv_g, send_x, recv_x, send_f, recv_f, send_1, recv_1, send_e = sems
    gx, gy = lax.axis_size("gx"), lax.axis_size("gy")
    i, z = lax.axis_index("gx"), lax.axis_index("gy")
    me = i * gy + z
    count = gx * gy
    rows = grid_rows // gx
    cols = grid_cols // gy
    per = v.shape[2] // LANES
    split = 2 * EACH // per
    slabs = cols // LANES
    mper, owners, near = layout(gx, gy)
    own = 2 * mper
    vb = NA // gy
    wide = NF * EACH * 2
    half = gx // 2
    mesh_id = pl.DeviceIdType.MESH

    upper = i >= half
    plane = jnp.where(upper, i - half, half - 1 - i)
    turn = jnp.where(upper, 0, gy) + z
    block_id = plane * near + turn

    def owner(t):
        c, r = lax.div(t, near), lax.rem(t, near)
        return jnp.where(r < gy, half + c, half - 1 - c), lax.rem(r, gy)

    end_i, end_z = owner(jnp.int32(owners - 1))

    def ship(src, dst, where, send_sem, recv_sem, start):
        here = (where[0] == i) & (where[1] == z)

        @pl.when(~here)
        def _():
            copy = pltpu.make_async_remote_copy(
                src_ref=src, dst_ref=dst, send_sem=send_sem, recv_sem=recv_sem,
                device_id=where, device_id_type=mesh_id,
            )
            if start:
                copy.start()
            else:
                copy.wait_send()

        if start:

            @pl.when(here)
            def _():
                pltpu.make_async_copy(src, dst, recv_sem).start()

    def arrived(ref, sem):
        pltpu.make_async_copy(ref, ref, sem).wait()

    barrier = pltpu.get_barrier_semaphore()
    for offset in range(1, count):
        peer = lax.rem(me + offset, count)
        pl.semaphore_signal(
            barrier, inc=1, device_id=(lax.div(peer, gy), lax.rem(peer, gy)), device_id_type=mesh_id
        )
    pl.semaphore_wait(barrier, count - 1)

    def v_ship(s, offset, start):
        peer = lax.rem(i + offset, gx)
        here = pl.ds(pl.multiple_of(i * rows, rows), rows)
        ship(sd[s].at[peer], v.at[s, here], (peer, z), send_v.at[s, offset], recv_v.at[s, i], start)

    def g_ship(s, t, start):
        lane = pl.multiple_of((z * slabs + lax.div(i, split)) * LANES, LANES)
        to = (pl.ds(lax.rem(i, split) * per, per), slice(None), pl.ds(lane, LANES))
        part = g.at[s, :, pl.ds(pl.multiple_of(t * own, own), own), :]
        ship(part, left.at[(s, *to)], owner(t), send_g.at[s, t], recv_g.at[s, me], start)

    def x_ship(s, start):
        lane = pl.multiple_of((z * slabs + lax.div(i, split)) * LANES, LANES)
        to = (pl.ds(lax.rem(i, split) * per, per), slice(None), pl.ds(lane, LANES))
        part = g.at[s, :, pl.ds(owners * own, 16), :]
        ship(part, left_x.at[(s, *to)], (end_i, end_z), send_x.at[s], recv_x.at[s, me], start)

    def f_ship(s, step, start):
        peer = lax.rem(z + step, gy)
        at = pl.ds(pl.multiple_of(turn * mper, mper), mper)
        ship(
            held.at[s, peer, 0], outs[s].at[at], (half + plane, peer),
            send_f.at[s, 0, step - 1], recv_f.at[s, turn], start,
        )
        mirror = near - 1 - turn
        at = pl.ds(mirror * mper + 1, mper - 1)
        ship(
            held.at[s, peer, 1, pl.ds(0, mper - 1)], outs[s].at[at], (half - 1 - plane, peer),
            send_f.at[s, 1, step - 1], recv_f.at[s, mirror], start,
        )
        first = turn == 0
        to = jnp.where(first, half - plane, half - 1 - plane)
        slot = jnp.where(first, 0, near - turn)

        @pl.when(block_id > 0)
        def _():
            ship(
                held.at[s, peer, 1, pl.ds(mper - 1, 1)], outs[s].at[pl.ds(slot * mper, 1)], (to, peer),
                send_1.at[s, step - 1], recv_1.at[s, slot], start,
            )

    def e_ship(s, step, start):
        peer = lax.rem(z + step, gy)
        ship(
            held_x.at[s, peer], outs[s].at[pl.ds(0, 1)], (0, peer),
            send_e.at[s, step - 1], recv_1.at[s, 0], start,
        )

    def fill_x(m, row):
        low = lax.broadcasted_iota(jnp.int32, m.shape, 1)
        a_re, a_im = unit(m * (low * LANES), zoom_factor * grid_rows)
        b_re, b_im = unit(m * low, zoom_factor * grid_rows)
        for block in range(grid_rows // LANES):
            h_re, h_im = a_re[:, block : block + 1], a_im[:, block : block + 1]
            re = h_re * b_re - h_im * b_im
            im = h_re * b_im + h_im * b_re
            both = jnp.concatenate([re, im], 0).astype(jnp.bfloat16)
            x_tab[pl.ds(row, 2 * m.shape[0]), block * LANES : (block + 1) * LANES] = both

    def build_x():
        row = lax.broadcasted_iota(jnp.int32, (mper, LANES), 0)

        def body(t, carry):
            fill_x(row + t * mper, pl.multiple_of(t * own, own))
            return carry

        lax.fori_loop(0, owners, body, 0)
        fill_x(jnp.full((8, LANES), NA // 2, jnp.int32), owners * own)

    def build_y():
        tall = 32
        low = lax.broadcasted_iota(jnp.int32, (tall, LANES), 1)
        row = lax.broadcasted_iota(jnp.int32, (tall, LANES), 0)

        def body(d, carry):
            start = pl.multiple_of(d * tall, tall)
            y = row + start
            a_re, a_im = unit(y * (low * LANES + NA // 4), zoom_factor * grid_cols)
            b_re, b_im = unit(y * low, zoom_factor * grid_cols)
            for block in range(NA // LANES):
                h_re, h_im = a_re[:, block : block + 1], a_im[:, block : block + 1]
                at = slice(block * LANES, (block + 1) * LANES)
                y_tab[0, pl.ds(start, tall), at] = (h_re * b_re - h_im * b_im).astype(jnp.bfloat16)
                y_tab[1, pl.ds(start, tall), at] = (h_re * b_im + h_im * b_re).astype(jnp.bfloat16)
            return carry

        lax.fori_loop(0, grid_cols // tall, body, 0)

    inv_norm = 1.0 / math.sqrt(grid_rows * grid_cols)
    mix = []
    for f in range(NF):
        angle = jnp.full((8, LANES), 0.5 * freqs[f], jnp.float32)
        half_re, half_im = jnp.cos(angle), jnp.sin(angle)
        turn_re, turn_im = jnp.cos(3.0 * angle) * inv_norm, jnp.sin(3.0 * angle) * inv_norm
        four = (turn_re * half_re, turn_im * half_re, -turn_im * half_im, turn_re * half_im)
        mix.append([value[:1, :1] for value in four])

    dot = functools.partial(jnp.dot, preferred_element_type=jnp.float32)
    parts = 2
    group = owners // parts

    def transform_rows(s):
        for src in range(gx):
            arrived(v.at[s, pl.ds(src * rows, rows)], recv_v.at[s, src])

        def body(c, carry):
            chunk = lax.rem(lax.div(block_id, group) + 1 + c, parts)
            tall = group * own
            start = pl.multiple_of(chunk * tall, tall)
            both = dot(x_tab[pl.ds(start, tall + 16), :], v[s]).astype(jnp.bfloat16)
            for f in range(per):
                g[s, f, pl.ds(start, tall), :] = both[:tall, f * LANES : (f + 1) * LANES]

            @pl.when(chunk == parts - 1)
            def _():
                for f in range(per):
                    g[s, f, owners * own :, :] = both[tall:, f * LANES : (f + 1) * LANES]
                x_ship(s, True)

            for e in range(group):
                g_ship(s, chunk * group + e, True)
            return carry

        lax.fori_loop(0, parts, body, 0)

    def one_hot(shape, source):
        row = lax.broadcasted_iota(jnp.int32, shape, 0)
        col = lax.broadcasted_iota(jnp.int32, shape, 1)
        return jnp.where(col == source(row), 1.0, 0.0).astype(jnp.bfloat16)

    size = (wide * mper, wide * mper)
    forth = one_hot(size, lambda row: lax.rem(row, wide) * mper + lax.div(row, wide))
    back = one_hot(size, lambda row: lax.rem(row, wide) * mper + mper - 1 - lax.div(row, wide))
    only = one_hot((wide, wide * 8), lambda row: row * 8)

    def finish(lhs, count_m, peer):
        at = pl.ds(pl.multiple_of(peer * vb, vb), vb)
        p_re, p_im = dot(lhs, y_tab[0, :, at]), dot(lhs, y_tab[1, :, at])
        plus, minus = [], []

        def both_signs(f):
            top = slice(2 * f * count_m, (2 * f + 1) * count_m)
            low = slice((2 * f + 1) * count_m, (2 * f + 2) * count_m)
            a_re, a_im, b_re, b_im = p_re[top], p_im[top], p_re[low], p_im[low]
            return (a_re - b_im, a_im + b_re), (a_re + b_im, a_im - b_re)

        fields = [both_signs(f) for f in range(2 * EACH)]
        for f in range(NF):
            p0, p1, q0, q1 = mix[f]
            for k in range(EACH):
                for sign, result in enumerate((plus, minus)):
                    s_re, s_im = fields[k][sign]
                    d_re, d_im = fields[EACH + k][sign]
                    result.append(p0 * s_re - p1 * s_im + (q0 * d_re - q1 * d_im))
                    result.append(p0 * s_im + p1 * s_re + (q0 * d_im + q1 * d_re))
        pack = lambda result: jnp.concatenate(result, 0).astype(jnp.bfloat16)
        return pack(plus), pack(minus)

    def transform_cols(s):
        for src in range(count):
            src_i, src_z = divmod(src, gy)
            lane = (src_z * slabs + src_i // split) * LANES
            region = left.at[s, pl.ds(src_i % split * per, per), :, pl.ds(lane, LANES)]
            arrived(region, recv_g.at[s, src])
        lhs = left[s].reshape(2 * EACH * own, grid_cols)
        for step in range(1, gy + 1):
            peer = lax.rem(z + step, gy)
            plus, minus = finish(lhs, mper, peer)
            held[s, peer, 0] = dot(forth, plus).reshape(mper, wide, vb).astype(jnp.bfloat16)
            held[s, peer, 1] = dot(back, minus).reshape(mper, wide, vb).astype(jnp.bfloat16)
            f_ship(s, step, True)

    at_end = (i == end_i) & (z == end_z)

    def transform_end(s):
        for src in range(count):
            src_i, src_z = divmod(src, gy)
            lane = (src_z * slabs + src_i // split) * LANES
            region = left_x.at[s, pl.ds(src_i % split * per, per), :, pl.ds(lane, LANES)]
            arrived(region, recv_x.at[s, src])
        lhs = left_x[s].reshape(2 * EACH * 16, grid_cols)
        for step in range(1, gy + 1):
            peer = lax.rem(z + step, gy)
            _, minus = finish(lhs, 8, peer)
            held_x[s, peer] = dot(only, minus).reshape(1, wide, vb).astype(jnp.bfloat16)
            e_ship(s, step, True)

    def owned(body):
        if near == 2 * gy:
            body()
        else:
            pl.when(turn < near)(body)

    for s in range(SETS):
        for offset in range(gx):
            v_ship(s, offset, True)
    build_x()
    transform_rows(0)
    build_y()
    for s in range(1, SETS):
        transform_rows(s)
    for s in range(SETS):
        owned(functools.partial(transform_cols, s))
        pl.when(at_end)(functools.partial(transform_end, s))
    for s in range(SETS):

        @pl.when(upper)
        def _():
            for slot in range(near):
                arrived(outs[s].at[pl.ds(slot * mper, mper)], recv_f.at[s, slot])

        @pl.when(~upper)
        def _():
            for slot in range(near):
                arrived(outs[s].at[pl.ds(slot * mper + 1, mper - 1)], recv_f.at[s, slot])
                arrived(outs[s].at[pl.ds(slot * mper, 1)], recv_1.at[s, slot])

    for s in range(SETS):
        for offset in range(gx):
            v_ship(s, offset, False)
        x_ship(s, False)
        for t in range(owners):
            g_ship(s, jnp.int32(t), False)

        def sent():
            for step in range(1, gy + 1):
                f_ship(s, step, False)

        owned(sent)

        @pl.when(at_end)
        def _():
            for step in range(1, gy + 1):
                e_ship(s, step, False)


def order_kernel(*refs):
    *parts, out = refs
    for s, part in enumerate(parts):
        block = part[...].astype(jnp.float32)
        for f in range(NF):
            for k in range(EACH):
                at = 2 * (f * EACH + k)
                out[:, f * 4 + s * EACH + k] = block[:, at : at + 2]


def far(sd, freqs, grid_rows, grid_cols):
    gx, gy = lax.axis_size("gx"), lax.axis_size("gy")
    count = gx * gy
    nu, vb = NA // gx, NA // gy
    mper, owners, near = layout(gx, gy)
    lanes = sd[0].shape[2]
    wide = NF * EACH * 2
    bf16 = jnp.bfloat16
    dma = pltpu.SemaphoreType.DMA
    done = pl.pallas_call(
        functools.partial(far_kernel, grid_rows, grid_cols),
        out_shape=(jax.ShapeDtypeStruct((nu, wide, vb), bf16),) * SETS,
        in_specs=[SM] + [ANY] * SETS,
        out_specs=(ANY,) * SETS,
        scratch_shapes=[
            pltpu.VMEM((NA + 16, grid_rows), bf16),
            pltpu.VMEM((2, grid_cols, NA), bf16),
            pltpu.VMEM((SETS, grid_rows, lanes), bf16),
            pltpu.VMEM((SETS, lanes // LANES, NA + 16, LANES), bf16),
            pltpu.VMEM((SETS, 2 * EACH, 2 * mper, grid_cols), bf16),
            pltpu.VMEM((SETS, 2 * EACH, 16, grid_cols), bf16),
            pltpu.VMEM((SETS, gy, 2, mper, wide, vb), bf16),
            pltpu.VMEM((SETS, gy, 1, wide, vb), bf16),
            dma((SETS, gx)),
            dma((SETS, gx)),
            dma((SETS, owners)),
            dma((SETS, count)),
            dma((SETS,)),
            dma((SETS, count)),
            dma((SETS, 2, gy)),
            dma((SETS, near)),
            dma((SETS, gy)),
            dma((SETS, near)),
            dma((SETS, gy)),
        ],
        compiler_params=pltpu.CompilerParams(
            vmem_limit_bytes=BIG, collective_id=1, has_side_effects=True
        ),
        name="far",
    )(freqs, *sd)
    block = nu // 4
    return pl.pallas_call(
        order_kernel,
        grid=(4,),
        out_shape=jax.ShapeDtypeStruct((nu, NF * 4, 2, vb), jnp.float32),
        in_specs=[pl.BlockSpec((block, wide, vb), lambda n: (n, 0, 0))] * SETS,
        out_specs=pl.BlockSpec((block, NF * 4, 2, vb), lambda n: (n, 0, 0, 0)),
        name="order",
    )(*done)


def on_device(e_field, h_field, material, eps_table, src_pos, src_amp, freqs):
    rows, cols = material.shape[1:]
    grid_rows, grid_cols = rows * lax.axis_size("gx"), cols * lax.axis_size("gy")
    e_new, h_new, *sd = yee(e_field, h_field, material, eps_table, src_pos, src_amp)
    shape = e_field.shape
    return (e_new.reshape(shape), h_new.reshape(shape), far(sd, freqs, grid_rows, grid_cols))


def solution(mesh):
    placed = (
        P(None, None, "gx", "gy"),
        P(None, None, "gx", "gy"),
        P(None, "gx", "gy"),
        P(),
        P(),
        P(),
        P(),
    )
    return jax.shard_map(
        on_device,
        mesh=mesh,
        in_specs=placed,
        out_specs=(P(None, None, "gx", "gy"), P(None, None, "gx", "gy"), P("gx", None, None, "gy")),
        check_vma=False,
    )
```

```python
import functools
import math

import jax
import jax.numpy as jnp
from jax import lax
from jax.experimental import pallas as pl
from jax.experimental.pallas import tpu as pltpu
from jax.sharding import PartitionSpec as P

LZ = 3
FACE = 1
STEPS = 2
NF = 2
NA = 1024
NMAT = 8

courant = 0.5
source_rate = 0.7
zoom_factor = 4

BASE = 32
CHUNK = 16
PAIR = 32
LANES = 128
Y_STEPS = 8
Y_EARLY = 2
ORDER = {
    2: ("a0", "a1", "x0", "r0", "y2", "y3", "y4", "y5", "y6", "y7", "r1", "c0", "c1"),
    4: (
        "a0", "a1", "x0", "r0", "a2", "y2", "y3", "r1", "a3", "y4",
        "y5", "y6", "y7", "c0", "r2", "c1", "r3", "c2", "c3",
    ),
}
PAD = 128
ANY = pl.BlockSpec(memory_space=pl.ANY)
VM = pl.BlockSpec(memory_space=pltpu.VMEM)
SM = pl.BlockSpec(memory_space=pltpu.SMEM)
BIG = 60 * 1024 * 1024


def halo_kernel(
    e, h, m, col_rim, corner, rim_f, rim_m,
    edge_f, edge_m, packed, got_col, got_corner, got_f, got_m, load, send, recv,
):
    gx, gy = lax.axis_size("gx"), lax.axis_size("gy")
    i, z = lax.axis_index("gx"), lax.axis_index("gy")
    planes, rows, cols = e.shape
    around = [(a, b) for a in (-1, 0, 1) for b in (-1, 0, 1) if (a, b) != (0, 0)]

    def exists(step):
        row, col = i + step[0], z + step[1]
        return (row >= 0) & (row < gx) & (col >= 0) & (col < gy)

    loads = []
    for side, lane in enumerate((0, cols - LANES)):
        at = pl.ds(lane, LANES)
        loads.append(pltpu.make_async_copy(e.at[:, :, at], edge_f.at[side, pl.ds(0, planes)], load.at[3 * side]))
        loads.append(pltpu.make_async_copy(h.at[:, :, at], edge_f.at[side, pl.ds(planes, planes)], load.at[3 * side + 1]))
        loads.append(pltpu.make_async_copy(m.at[:, :, at], edge_m.at[side], load.at[3 * side + 2]))
    for copy in loads:
        copy.start()
    barrier = pltpu.get_barrier_semaphore()
    total = jnp.int32(0)
    for step in around:
        total += exists(step).astype(jnp.int32)

        @pl.when(exists(step))
        def _():
            pl.semaphore_signal(
                barrier, inc=1, device_id=(i + step[0], z + step[1]), device_id_type=pl.DeviceIdType.MESH
            )

    pl.semaphore_wait(barrier, total)

    def remote(step, src, dst, index):
        copy = pltpu.make_async_remote_copy(
            src_ref=src, dst_ref=dst, send_sem=send.at[index], recv_sem=recv.at[index],
            device_id=(i + step[0], z + step[1]), device_id_type=pl.DeviceIdType.MESH,
        )
        return step, copy

    rows_out, cols_out = [], []
    for side, low in enumerate((0, rows - 2)):
        step = (2 * side - 1, 0)
        at, to = pl.ds(low, 2), pl.ds(6 * side, 2)
        rows_out.append(remote(step, e.at[:, at, :], got_f.at[side, pl.ds(0, planes), to], 3 * side))
        rows_out.append(remote(step, h.at[:, at, :], got_f.at[side, pl.ds(planes, planes), to], 3 * side + 1))
        rows_out.append(remote(step, m.at[:, at, :], got_m.at[side, :, to], 3 * side + 2))
    for side in range(2):
        cols_out.append(remote((0, 2 * side - 1), packed.at[side], got_col.at[side], 6 + side))
        for end, low in enumerate((0, rows - 8)):
            step = (2 * end - 1, 2 * side - 1)
            src = packed.at[side, pl.ds(low, 8)]
            cols_out.append(remote(step, src, got_corner.at[end, side], 8 + 2 * side + end))

    def start(copies):
        for step, copy in copies:

            @pl.when(exists(step))
            def _():
                copy.start()

    start(rows_out)
    for copy in loads:
        copy.wait()
    tall = 32
    lane = lax.broadcasted_iota(jnp.int32, (tall, LANES), 1)

    def pack(c, carry):
        at = pl.ds(pl.multiple_of(c * tall, tall), tall)
        for side in range(2):
            place = ((lane + 2 * side) & (LANES - 1)) >> 2
            block = jnp.zeros((tall, LANES), jnp.float32)
            for p in range(2 * planes + LZ):
                if p < 2 * planes:
                    piece = edge_f[side, p, at, :]
                else:
                    piece = edge_m[side, p - 2 * planes, at, :].astype(jnp.float32)
                block = jnp.where(place == p, pltpu.roll(piece, 4 * p, 1), block)
            packed[side, at, :] = block
        return carry

    lax.fori_loop(0, rows // tall, pack, 0)
    start(cols_out)
    for step, copy in rows_out + cols_out:

        @pl.when(exists((-step[0], -step[1])))
        def _():
            copy.wait_recv()

    last = (lane & 2) == 0
    after, before = exists((0, 1)), exists((0, -1))

    def merge(c, carry):
        at = pl.ds(pl.multiple_of(c * tall, tall), tall)
        right = jnp.where(after, got_col[0, at, :], 0.0)
        left = jnp.where(before, got_col[1, at, :], 0.0)
        col_rim[at, :] = jnp.where(last, right, left)
        return carry

    lax.fori_loop(0, rows // tall, merge, 0)
    for side in range(2):
        there = exists((1 - 2 * side, 0))
        row = lax.broadcasted_iota(jnp.int32, (8, cols), 0)
        kept = there & ((row >= 6) if side else (row < 2))
        rim_f[side] = jnp.where(kept[None], got_f[side], 0.0)
        rim_m[side] = jnp.where(kept[None], got_m[side], 0)
        right = jnp.where(there & after, got_corner[side, 0], 0.0)
        left = jnp.where(there & before, got_corner[side, 1], 0.0)
        corner[side] = jnp.where(last[:8], right, left)
    for step, copy in rows_out + cols_out:

        @pl.when(exists(step))
        def _():
            copy.wait_send()


def halo(e, h, m):
    planes, rows, cols = e.shape
    f32, i32 = jnp.float32, jnp.int32
    dma = pltpu.SemaphoreType.DMA
    return pl.pallas_call(
        halo_kernel,
        out_shape=(
            jax.ShapeDtypeStruct((rows, LANES), f32),
            jax.ShapeDtypeStruct((2, 8, LANES), f32),
            jax.ShapeDtypeStruct((2, 2 * planes, 8, cols), f32),
            jax.ShapeDtypeStruct((2, LZ, 8, cols), i32),
        ),
        in_specs=[ANY] * 3,
        out_specs=(VM,) * 4,
        scratch_shapes=[
            pltpu.VMEM((2, 2 * planes, rows, LANES), f32),
            pltpu.VMEM((2, LZ, rows, LANES), i32),
            pltpu.VMEM((2, rows, LANES), f32),
            pltpu.VMEM((2, rows, LANES), f32),
            pltpu.VMEM((2, 2, 8, LANES), f32),
            pltpu.VMEM((2, 2 * planes, 8, cols), f32),
            pltpu.VMEM((2, LZ, 8, cols), i32),
            dma((6,)),
            dma((12,)),
            dma((12,)),
        ],
        compiler_params=pltpu.CompilerParams(collective_id=0, has_side_effects=True),
        name="halo",
    )(e, h, m)


def split_sets(gx, cols):
    sets = 4 if 2 * cols >= gx * LANES else 2
    each = 4 // sets
    return sets, each, 2 * each * cols // (gx * LANES)


def yee_kernel(
    grid_rows, grid_cols, plan,
    e_hbm, h_hbm, m_hbm, col_rim, corner, rim_f, rim_m, eps, pos, amp,
    e_out, h_out, *rest,
):
    sets, each, per = plan
    sd_outs, (e_ext, h_ext, m_main, scale, src, first, *sd, sems) = rest[:sets], rest[sets:]
    rows, cols = m_main.shape[1:]
    width = cols + PAD
    high = e_ext.shape[1]
    row0 = lax.axis_index("gx") * rows
    col0 = lax.axis_index("gy") * cols
    pairs = rows // PAIR

    def load(q):
        here, there = pl.ds(PAIR * q, PAIR), pl.ds(BASE + PAIR * q, PAIR)
        return [
            pltpu.make_async_copy(e_hbm.at[:, here, :], e_ext.at[:, there, pl.ds(0, cols)], sems.at[0, q]),
            pltpu.make_async_copy(h_hbm.at[:, here, :], h_ext.at[:, there, pl.ds(0, cols)], sems.at[1, q]),
            pltpu.make_async_copy(m_hbm.at[:, here, :], m_main.at[:, here, :], sems.at[2, q]),
        ]

    def store(q):
        here, there = pl.ds(PAIR * q, PAIR), pl.ds(BASE + PAIR * q, PAIR)
        return [
            pltpu.make_async_copy(e_ext.at[:, there, pl.ds(0, cols)], e_out.at[:, here, :], sems.at[3, q]),
            pltpu.make_async_copy(h_ext.at[:, there, pl.ds(0, cols)], h_out.at[:, here, :], sems.at[4, q]),
        ] + [
            pltpu.make_async_copy(sd[s].at[:, here, :], sd_outs[s].at[:, here, :], sems.at[5 + s, q])
            for s in range(sets)
        ]

    for q in range(pairs):
        for copy in load(q):
            copy.start()
    count = amp.shape[1]
    used = high - 2 * CHUNK
    bf16 = jnp.bfloat16
    gather = functools.partial(
        lax.dot_general, dimension_numbers=(((1,), (1,)), ((), ())), preferred_element_type=jnp.float32
    )
    tall_at = lambda shape: row0 + lax.broadcasted_iota(jnp.int32, shape, 0) + (CHUNK - BASE)
    lane = lax.broadcasted_iota(jnp.int32, (width, LANES), 0)
    col_at = (col0 + jnp.where(lane < cols + PAD // 2, lane, lane - width)).astype(jnp.float32)
    row_at = tall_at((used, LANES)).astype(jnp.float32)
    row_s = jnp.broadcast_to(pos[1:2, :], (8, count))
    col_s = jnp.broadcast_to(pos[2:3, :], (8, count))
    inside = (row_s >= row0 - (BASE - CHUNK)) & (row_s < row0 + used - (BASE - CHUNK))
    inside &= (col_s >= col0 - PAD // 2) & (col_s < col0 + cols + PAD // 2)
    rank = jnp.where(inside, 1.0, 0.0)
    at_lane = lax.broadcasted_iota(jnp.int32, (8, count), 1)
    reach = 1
    while reach < count:
        rank = rank + jnp.where(at_lane >= reach, pltpu.roll(rank, reach, 1), 0.0)
        reach *= 2
    found = jnp.max(rank).astype(jnp.int32)
    rank = jnp.where(inside, rank, 0.0)[:1]
    hi = amp[...].astype(bf16).astype(jnp.float32)
    mid = (amp[...] - hi).astype(bf16).astype(jnp.float32)
    low = amp[...] - hi - mid
    parts = [
        (pos[1:2, :] >> 6).astype(jnp.float32), (pos[1:2, :] & 63).astype(jnp.float32),
        (pos[2:3, :] >> 6).astype(jnp.float32), (pos[2:3, :] & 63).astype(jnp.float32),
        pos[0:1, :].astype(jnp.float32), hi, mid, low,
    ]
    parts = jnp.concatenate(parts, 0).astype(bf16)
    for layer in range(LZ):
        src[layer] = jnp.zeros((high, width), jnp.float32)
    slot = lax.broadcasted_iota(jnp.int32, (LANES, count), 0).astype(jnp.float32)

    def place(group, carry):
        pick = jnp.where(slot + (group * LANES + 1).astype(jnp.float32) == rank, 1.0, 0.0)
        some = gather(parts, pick.astype(bf16))
        row, col = some[0:1] * 64.0 + some[1:2], some[2:3] * 64.0 + some[3:4]
        hit_col = jnp.where(col_at == col, 1.0, 0.0).astype(bf16)
        hit_col = jnp.concatenate([hit_col] * 3, 1)
        hit_row = row_at == row
        for layer in range(LZ):
            hit = hit_row & (some[4:5] == float(layer))
            left = [jnp.where(hit, some[p : p + 1], 0.0).astype(bf16) for p in (5, 6, 7)]
            src[layer, CHUNK : CHUNK + used, :] += gather(jnp.concatenate(left, 1), hit_col)
        return carry

    lax.fori_loop(0, lax.div(found + (LANES - 1), LANES), place, 0)

    def scale_of(index, row, col):
        value = jnp.full(index.shape, eps[0], jnp.float32)
        for material in range(1, NMAT):
            value = jnp.where(index == material, eps[material], value)
        inside = (row >= 0) & (row < grid_rows) & (col >= 0) & (col < grid_cols)
        return jnp.where(inside, courant / value, 0.0)

    col_main = col0 + lax.broadcasted_iota(jnp.int32, (CHUNK, cols), 1)
    lane_pad = lax.broadcasted_iota(jnp.int32, (CHUNK, PAD), 1)
    col_pad = col0 + jnp.where(lane_pad < PAD // 2, cols + lane_pad, lane_pad - PAD)
    row_chunk = row0 + lax.broadcasted_iota(jnp.int32, (CHUNK, cols), 0)

    def shown(block, plane):
        return pltpu.roll(block, PAD - 4 * plane, 1) if plane else block

    def fill(step_index, carry):
        r = pl.multiple_of(step_index * CHUNK, CHUNK)
        near = pl.ds(r, CHUNK)
        far = pl.ds(BASE + r, CHUNK)
        block = col_rim[near, :]
        for layer in range(LZ):
            scale[layer, far, :cols] = scale_of(m_main[layer, near, :], row_chunk + r, col_main)
            scale[layer, far, cols:] = scale_of(
                shown(block, 6 * LZ + layer), row_chunk[:, :PAD] + r, col_pad
            )
        for plane in range(3 * LZ):
            e_ext[plane, far, cols:] = shown(block, plane)
            h_ext[plane, far, cols:] = shown(block, 3 * LZ + plane)
        return carry

    row_eight = row0 + lax.broadcasted_iota(jnp.int32, (8, cols), 0)
    blank = jnp.zeros((8, width), jnp.float32)
    for side, target, offset, spare in (
        (0, BASE + rows, rows, BASE + rows + 8),
        (1, BASE - 8, -8, BASE - 16),
    ):
        here = slice(target, target + 8)
        block = corner[side]
        for layer in range(LZ):
            scale[layer, here, :cols] = scale_of(
                rim_m[side, layer], row_eight + offset, col_main[:8]
            )
            scale[layer, here, cols:] = scale_of(
                shown(block, 6 * LZ + layer), row_eight[:, :PAD] + offset, col_pad[:8]
            )
            scale[layer, spare : spare + 8, :] = blank
        for plane in range(3 * LZ):
            e_ext[plane, here, :cols] = rim_f[side, plane]
            h_ext[plane, here, :cols] = rim_f[side, 3 * LZ + plane]
            e_ext[plane, here, cols:] = shown(block, plane)
            h_ext[plane, here, cols:] = shown(block, 3 * LZ + plane)
            e_ext[plane, spare : spare + 8, :] = blank
            h_ext[plane, spare : spare + 8, :] = blank
    for plane in range(3 * LZ):
        e_ext[plane, high - 16 : high, :] = jnp.zeros((16, width), jnp.float32)
        h_ext[plane, 0:16, :] = jnp.zeros((16, width), jnp.float32)
    lane_c = lax.broadcasted_iota(jnp.int32, (CHUNK, width), 1)
    col_c = col0 + jnp.where(lane_c < cols + PAD // 2, lane_c, lane_c - width)
    weight = jnp.where(col_c >= 0, courant, 0.0)
    top = lax.axis_index("gx") == 0

    def magnetic_pass(index, carry):
        r = pl.multiple_of(index * CHUNK, CHUNK)
        now = pl.ds(r, CHUNK)
        more = pl.ds(r, CHUNK + 8)
        factor = weight * jnp.where(top & (index * CHUNK < BASE), 0.0, 1.0)
        zero = jnp.zeros((CHUNK, width), jnp.float32)
        ex = [e_ext[layer, now, :] for layer in range(LZ)] + [zero]
        ey = [e_ext[LZ + layer, now, :] for layer in range(LZ)] + [zero]
        for layer in range(LZ):
            ez = e_ext[2 * LZ + layer, now, :]
            ez_row = pltpu.roll(e_ext[2 * LZ + layer, more, :], CHUNK + 7, 0)[:CHUNK]
            ey_row = pltpu.roll(e_ext[LZ + layer, more, :], CHUNK + 7, 0)[:CHUNK]
            ez_col = pltpu.roll(ez, width - 1, 1)
            ex_col = pltpu.roll(ex[layer], width - 1, 1)
            curl_x = ez_col - ez - (ey[layer + 1] - ey[layer])
            curl_y = ex[layer + 1] - ex[layer] - (ez_row - ez)
            curl_z = ey_row - ey[layer] - (ex_col - ex[layer])
            for part, curl in enumerate((curl_x, curl_y, curl_z)):
                plane = part * LZ + layer
                h_ext[plane, now, :] = h_ext[plane, now, :] - factor * curl
        return carry

    def electric_pass(moment, last, index, carry):
        r = pl.multiple_of(index * CHUNK, CHUNK)
        now = pl.ds(r, CHUNK)
        more = pl.ds(pl.multiple_of(r - 8, 8), CHUNK + 8)
        drive = math.sin(source_rate * moment)
        zero = jnp.zeros((CHUNK, width), jnp.float32)
        hx = [zero] + [h_ext[layer, now, :] for layer in range(LZ)]
        hy = [zero] + [h_ext[LZ + layer, now, :] for layer in range(LZ)]
        for layer in range(LZ):
            hz = h_ext[2 * LZ + layer, now, :]
            hz_row = pltpu.roll(h_ext[2 * LZ + layer, more, :], 1, 0)[8:]
            hy_row = pltpu.roll(h_ext[LZ + layer, more, :], 1, 0)[8:]
            hx_now, hy_now = hx[layer + 1], hy[layer + 1]
            hz_col = pltpu.roll(hz, 1, 1)
            hx_col = pltpu.roll(hx_now, 1, 1)
            curl_x = hz - hz_col - (hy_now - hy[layer])
            curl_y = hx_now - hx[layer] - (hz - hz_row)
            curl_z = hy_now - hy_row - (hx_now - hx_col)
            factor = scale[layer, now, :]
            new_x = e_ext[layer, now, :] + factor * curl_x
            new_y = e_ext[LZ + layer, now, :] + factor * curl_y
            new_z = e_ext[2 * LZ + layer, now, :] + factor * curl_z + drive * src[layer, now, :]
            e_ext[layer, now, :] = new_x
            e_ext[LZ + layer, now, :] = new_y
            e_ext[2 * LZ + layer, now, :] = new_z
            if layer == FACE:
                faces = (-hy_now, hx_now, new_y, -new_x)
                for item, face in enumerate(faces):
                    if last:
                        old = first[item, now, :]
                        here = pl.ds(r - BASE, CHUNK)
                        for which, value in enumerate((old + face, face - old)):
                            share, place = divmod(which * each + item % each, per)
                            for q in range(cols // LANES):
                                piece = value[:, q * LANES : (q + 1) * LANES].astype(jnp.bfloat16)
                                lanes = pl.ds(place * LANES, LANES)
                                sd[item // each][q * (2 * each // per) + share, here, lanes] = piece
                    else:
                        first[item, now, :] = face
        return carry

    def arrive(q):
        for copy in load(q):
            copy.wait()
        for part in range(PAIR // CHUNK):
            fill(q * (PAIR // CHUNK) + part, 0)

    def advance(n, second):
        magnetic_pass(n, 0)
        electric_pass(1.0, False, n, 0)
        magnetic_pass(n - 1, 0)
        if second:
            electric_pass(2.0, True, n - 1, 0)

    start = BASE // CHUNK
    arrive(0)
    magnetic_pass(start - 1, 0)
    electric_pass(1.0, False, start - 1, 0)
    advance(start, False)

    def wave(q, carry):
        @pl.when(q < pairs - 1)
        def _():
            arrive(q + 1)

        for part in range(PAIR // CHUNK):
            advance(start + 1 + q * (PAIR // CHUNK) + part, True)
        for copy in store(q):
            copy.start()
        return carry

    lax.fori_loop(0, pairs, wave, 0)
    for q in range(pairs):
        for copy in store(q):
            copy.wait()


def yee(e_field, h_field, material, eps_table, src_pos, src_amp):
    rows, cols = material.shape[1:]
    gx = lax.axis_size("gx")
    sets, each, per = split_sets(gx, cols)
    grid_rows = rows * gx
    grid_cols = cols * lax.axis_size("gy")
    planes = 3 * LZ
    e = e_field.reshape(planes, rows, cols)
    h = h_field.reshape(planes, rows, cols)

    high = rows + 2 * BASE
    width = cols + PAD
    f32 = jnp.float32
    out = pl.pallas_call(
        functools.partial(yee_kernel, grid_rows, grid_cols, (sets, each, per)),
        out_shape=(
            jax.ShapeDtypeStruct((planes, rows, cols), f32),
            jax.ShapeDtypeStruct((planes, rows, cols), f32),
        )
        + (jax.ShapeDtypeStruct((gx, rows, per * LANES), jnp.bfloat16),) * sets,
        in_specs=[ANY, ANY, ANY, VM, VM, VM, VM, SM, VM, VM],
        out_specs=(ANY,) * (2 + sets),
        scratch_shapes=[
            pltpu.VMEM((planes, high, width), f32),
            pltpu.VMEM((planes, high, width), f32),
            pltpu.VMEM((LZ, rows, cols), jnp.int32),
            pltpu.VMEM((LZ, high, width), f32),
            pltpu.VMEM((LZ, high, width), f32),
            pltpu.VMEM((4, high, width), f32),
        ]
        + [pltpu.VMEM((gx, rows, per * LANES), jnp.bfloat16)] * sets
        + [
            pltpu.SemaphoreType.DMA((5 + sets, rows // PAIR)),
        ],
        compiler_params=pltpu.CompilerParams(vmem_limit_bytes=BIG),
        name="yee",
    )(
        e, h, material, *halo(e, h, material),
        eps_table, jnp.swapaxes(src_pos, 0, 1), src_amp[None, :],
    )
    return out


SIN = (-1.0 / 6.0, 1.0 / 120.0, -1.0 / 5040.0, 1.0 / 362880.0)
COS = (-0.5, 1.0 / 24.0, -1.0 / 720.0, 1.0 / 40320.0, -1.0 / 3628800.0)


def unit(phase, period):
    eighth = period // 8
    turn = phase & (period - 1)
    quarter = (turn + eighth) // (2 * eighth)
    x = (turn - quarter * (2 * eighth)).astype(jnp.float32) * (2.0 * math.pi / period)
    square = x * x
    sine = jnp.full_like(x, SIN[-1])
    for factor in SIN[-2::-1]:
        sine = sine * square + factor
    sine = x + x * (square * sine)
    cosine = jnp.full_like(x, COS[-1])
    for factor in COS[-2::-1]:
        cosine = cosine * square + factor
    cosine = 1.0 + square * cosine
    odd = (quarter & 1) == 1
    re = jnp.where(odd, sine, cosine)
    im = jnp.where(odd, cosine, sine)
    re = jnp.where(((quarter + 1) & 2) == 2, -re, re)
    im = jnp.where((quarter & 2) == 2, im, -im)
    return re, im


def layout(gx, gy):
    mper = max(8, NA // 2 // (gx * gy))
    return mper, NA // 2 // mper, NA // gx // mper


def build_x(x_tab, mper, owners):
    grid_rows = x_tab.shape[1]
    own = 2 * mper

    def fill_x(m, row):
        low = lax.broadcasted_iota(jnp.int32, m.shape, 1)
        a_re, a_im = unit(m * (low * LANES), zoom_factor * grid_rows)
        b_re, b_im = unit(m * low, zoom_factor * grid_rows)
        for block in range(grid_rows // LANES):
            h_re, h_im = a_re[:, block : block + 1], a_im[:, block : block + 1]
            re = h_re * b_re - h_im * b_im
            im = h_re * b_im + h_im * b_re
            both = jnp.concatenate([re, im], 0).astype(jnp.bfloat16)
            x_tab[pl.ds(row, 2 * m.shape[0]), block * LANES : (block + 1) * LANES] = both

    row = lax.broadcasted_iota(jnp.int32, (mper, LANES), 0)

    def body(t, carry):
        fill_x(row + t * mper, pl.multiple_of(t * own, own))
        return carry

    lax.fori_loop(0, owners, body, 0)
    fill_x(jnp.full((8, LANES), NA // 2, jnp.int32), owners * own)


def far_kernel(grid_rows, grid_cols, plan, freqs, *rest):
    sets, each, per = plan
    sd, outs, rest = rest[:sets], rest[sets : 2 * sets], rest[2 * sets :]
    x_tab, y_tab, v, g, left, left_x, held, held_x, *sems = rest
    send_v, recv_v, send_g, recv_g, send_x, recv_x, send_f, recv_f, send_e = sems
    gx, gy = lax.axis_size("gx"), lax.axis_size("gy")
    i, z = lax.axis_index("gx"), lax.axis_index("gy")
    me = i * gy + z
    count = gx * gy
    rows = grid_rows // gx
    cols = grid_cols // gy
    split = 2 * each // per
    slabs = cols // LANES
    mper, owners, near = layout(gx, gy)
    own = 2 * mper
    vb = NA // gy
    wide = NF * each * 2
    half = gx // 2
    mesh_id = pl.DeviceIdType.MESH

    upper = i >= half
    plane = jnp.where(upper, i - half, half - 1 - i)
    turn = jnp.where(upper, 0, gy) + z
    block_id = plane * near + turn

    def owner(t):
        c, r = lax.div(t, near), lax.rem(t, near)
        return jnp.where(r < gy, half + c, half - 1 - c), lax.rem(r, gy)

    end_i, end_z = owner(jnp.int32(owners - 1))

    def ship(src, dst, where, send_sem, recv_sem):
        here = (where[0] == i) & (where[1] == z)

        @pl.when(~here)
        def _():
            pltpu.make_async_remote_copy(
                src_ref=src, dst_ref=dst, send_sem=send_sem, recv_sem=recv_sem,
                device_id=where, device_id_type=mesh_id,
            ).start()

        @pl.when(here)
        def _():
            pltpu.make_async_copy(src, dst, recv_sem).start()

    def wait(ref, sem):
        pltpu.make_async_copy(ref, ref, sem).wait()

    here = pl.ds(pl.multiple_of(i * rows, rows), rows)
    lane = pl.multiple_of((z * slabs + lax.div(i, split)) * LANES, LANES)
    to = (pl.ds(lax.rem(i, split) * per, per), slice(None), pl.ds(lane, LANES))

    def v_ship(s, offset):
        peer = lax.rem(i + offset, gx)
        ship(sd[s].at[peer], v.at[s, here], (peer, z), send_v.at[s], recv_v.at[s])

    def g_ship(s, t):
        part = g.at[s, :, pl.ds(pl.multiple_of(t * own, own), own), :]
        ship(part, left.at[(s, *to)], owner(t), send_g.at[s], recv_g.at[s])

    def x_ship(s):
        part = g.at[s, :, pl.ds(owners * own, 16), :]
        ship(part, left_x.at[(s, *to)], (end_i, end_z), send_x.at[s], recv_x.at[s])

    def held_at(peer, sign):
        return (peer * 2 + sign) * mper

    def f_ship(s, peer):
        at = pl.ds(pl.multiple_of(turn * mper, mper), mper)
        src = held.at[s, pl.ds(held_at(peer, 0), mper)]
        ship(src, outs[s].at[at], (half + plane, peer), send_f.at[s], recv_f.at[s])
        at = pl.ds((near - 1 - turn) * mper + 1, mper - 1)
        src = held.at[s, pl.ds(held_at(peer, 1), mper - 1)]
        ship(src, outs[s].at[at], (half - 1 - plane, peer), send_f.at[s], recv_f.at[s])
        first = turn == 0
        across = jnp.where(first, half - plane, half - 1 - plane)
        slot = jnp.where(first, 0, near - turn)

        @pl.when(block_id > 0)
        def _():
            src = held.at[s, pl.ds(held_at(peer, 1) + mper - 1, 1)]
            ship(src, outs[s].at[pl.ds(slot * mper, 1)], (across, peer), send_f.at[s], recv_f.at[s])

    def f_sent(s):
        far_up = (gy - 1) * mper + gy * (mper - 1)
        far_low = gy * mper + (gy - 1) * mper
        for case, amount in (
            (upper & (block_id > 0), far_up + gy), (upper & (block_id == 0), far_up), (~upper, far_low),
        ):

            @pl.when(case)
            def _():
                wait(held.at[s, pl.ds(0, amount)], send_f.at[s])

    def e_ship(s, peer):
        ship(held_x.at[s, peer], outs[s].at[pl.ds(0, 1)], (0, peer), send_e.at[s], recv_f.at[s])

    def e_sent(s):
        for case, amount in ((i == 0, gy - 1), (i > 0, gy)):

            @pl.when(case)
            def _():
                wait(held_x.at[s, pl.ds(0, amount)], send_e.at[s])

    def build_y(low_block, high_block):
        tall = 32
        low = lax.broadcasted_iota(jnp.int32, (tall, LANES), 1)
        row = lax.broadcasted_iota(jnp.int32, (tall, LANES), 0)

        def body(d, carry):
            start = pl.multiple_of(d * tall, tall)
            y = row + start
            a_re, a_im = unit(y * (low * LANES + NA // 4), zoom_factor * grid_cols)
            b_re, b_im = unit(y * low, zoom_factor * grid_cols)
            for block in range(NA // LANES):
                h_re, h_im = a_re[:, block : block + 1], a_im[:, block : block + 1]
                at = slice(block * LANES, (block + 1) * LANES)
                y_tab[0, pl.ds(start, tall), at] = (h_re * b_re - h_im * b_im).astype(jnp.bfloat16)
                y_tab[1, pl.ds(start, tall), at] = (h_re * b_im + h_im * b_re).astype(jnp.bfloat16)
            return carry

        lax.fori_loop(grid_cols * low_block // (tall * Y_STEPS), grid_cols * high_block // (tall * Y_STEPS), body, 0)

    inv_norm = 1.0 / math.sqrt(grid_rows * grid_cols)
    mix = []
    for f in range(NF):
        angle = jnp.full((8, LANES), 0.5 * freqs[f], jnp.float32)
        half_re, half_im = jnp.cos(angle), jnp.sin(angle)
        turn_re, turn_im = jnp.cos(3.0 * angle) * inv_norm, jnp.sin(3.0 * angle) * inv_norm
        four = (turn_re * half_re, turn_im * half_re, -turn_im * half_im, turn_re * half_im)
        mix.append([value[:1, :1] for value in four])

    dot = functools.partial(jnp.dot, preferred_element_type=jnp.float32)
    parts = 2
    group = owners // parts

    def transform_rows(s):
        wait(v.at[s], recv_v.at[s])

        def body(c, carry):
            chunk = lax.rem(lax.div(block_id, group) + 1 + c, parts)
            tall = group * own
            start = pl.multiple_of(chunk * tall, tall)
            both = dot(x_tab[pl.ds(start, tall + 16), :], v[s]).astype(jnp.bfloat16)
            for f in range(per):
                g[s, f, pl.ds(start, tall), :] = both[:tall, f * LANES : (f + 1) * LANES]

            @pl.when(chunk == parts - 1)
            def _():
                for f in range(per):
                    g[s, f, owners * own :, :] = both[tall:, f * LANES : (f + 1) * LANES]
                x_ship(s)

            for e in range(group):
                g_ship(s, chunk * group + e)
            return carry

        lax.fori_loop(0, parts, body, 0)

    def one_hot(shape, source):
        row = lax.broadcasted_iota(jnp.int32, shape, 0)
        col = lax.broadcasted_iota(jnp.int32, shape, 1)
        return jnp.where(col == source(row), 1.0, 0.0).astype(jnp.bfloat16)

    size = (wide * mper, wide * mper)
    forth = one_hot(size, lambda row: lax.rem(row, wide) * mper + lax.div(row, wide))
    back = one_hot(size, lambda row: lax.rem(row, wide) * mper + mper - 1 - lax.div(row, wide))
    only = one_hot((wide, wide * 8), lambda row: row * 8)

    def finish(lhs, count_m, peer):
        at = pl.ds(pl.multiple_of(peer * vb, vb), vb)
        p_re, p_im = dot(lhs, y_tab[0, :, at]), dot(lhs, y_tab[1, :, at])
        plus, minus = [], []

        def both_signs(f):
            top = slice(2 * f * count_m, (2 * f + 1) * count_m)
            low = slice((2 * f + 1) * count_m, (2 * f + 2) * count_m)
            a_re, a_im, b_re, b_im = p_re[top], p_im[top], p_re[low], p_im[low]
            return (a_re - b_im, a_im + b_re), (a_re + b_im, a_im - b_re)

        fields = [both_signs(f) for f in range(2 * each)]
        for f in range(NF):
            p0, p1, q0, q1 = mix[f]
            for k in range(each):
                for sign, result in enumerate((plus, minus)):
                    s_re, s_im = fields[k][sign]
                    d_re, d_im = fields[each + k][sign]
                    result.append(p0 * s_re - p1 * s_im + (q0 * d_re - q1 * d_im))
                    result.append(p0 * s_im + p1 * s_re + (q0 * d_im + q1 * d_re))
        pack = lambda result: jnp.concatenate(result, 0).astype(jnp.bfloat16)
        return pack(plus), pack(minus)

    def transform_cols(s):
        wait(left.at[s], recv_g.at[s])
        lhs = left[s].reshape(2 * each * own, grid_cols)
        for step in range(1, gy + 1):
            peer = lax.rem(z + step, gy)
            plus, minus = finish(lhs, mper, peer)
            held[s, pl.ds(held_at(peer, 0), mper)] = dot(forth, plus).reshape(mper, wide, vb).astype(jnp.bfloat16)
            held[s, pl.ds(held_at(peer, 1), mper)] = dot(back, minus).reshape(mper, wide, vb).astype(jnp.bfloat16)
            f_ship(s, peer)

    at_end = (i == end_i) & (z == end_z)

    def transform_end(s):
        wait(left_x.at[s], recv_x.at[s])
        lhs = left_x[s].reshape(2 * each * 16, grid_cols)
        for step in range(1, gy + 1):
            peer = lax.rem(z + step, gy)
            _, minus = finish(lhs, 8, peer)
            held_x[s, peer] = dot(only, minus).reshape(1, wide, vb).astype(jnp.bfloat16)
            e_ship(s, peer)

    def owned(body):
        if near == 2 * gy:
            body()
        else:
            pl.when(turn < near)(body)

    barrier = pltpu.get_barrier_semaphore()
    for offset in range(1, count):
        peer = lax.rem(me + offset, count)
        pl.semaphore_signal(
            barrier, inc=1, device_id=(lax.div(peer, gy), lax.rem(peer, gy)), device_id_type=mesh_id
        )
    build_y(0, Y_EARLY)
    pl.semaphore_wait(barrier, count - 1)

    def send_fields(s):
        for offset in range(gx):
            v_ship(s, offset)

    def do_cols(s):
        owned(functools.partial(transform_cols, s))
        pl.when(at_end)(functools.partial(transform_end, s))

    steps = {"a": send_fields, "y": lambda part: build_y(part, part + 1), "r": transform_rows, "x": lambda _: build_x(x_tab, mper, owners), "c": do_cols}
    for token in ORDER[sets]:
        steps[token[0]](int(token[1:]))
    for s in range(sets):
        wait(outs[s], recv_f.at[s])
    for s in range(sets):
        wait(v.at[s, pl.ds(0, (gx - 1) * rows)], send_v.at[s])
        if near == 2 * gy:
            wait(g.at[s, :, pl.ds(0, (owners - 1) * own), :], send_g.at[s])
        else:
            for case, amount in ((turn < near, owners - 1), (turn >= near, owners)):

                @pl.when(case)
                def _():
                    wait(g.at[s, :, pl.ds(0, amount * own), :], send_g.at[s])

        @pl.when(~at_end)
        def _():
            wait(g.at[s, :, pl.ds(0, 16), :], send_x.at[s])

        owned(functools.partial(f_sent, s))
        pl.when(at_end)(functools.partial(e_sent, s))


def order_kernel(*refs):
    *parts, out = refs
    sets, each = len(parts), 4 // len(parts)
    for s, part in enumerate(parts):
        block = part[...].astype(jnp.float32)
        for f in range(NF):
            for k in range(each):
                at = 2 * (f * each + k)
                out[:, f * 4 + s * each + k] = block[:, at : at + 2]


def far(sd, freqs, grid_rows, grid_cols):
    gx, gy = lax.axis_size("gx"), lax.axis_size("gy")
    count = gx * gy
    nu, vb = NA // gx, NA // gy
    mper, owners, near = layout(gx, gy)
    lanes = sd[0].shape[2]
    sets, each, per = split_sets(gx, grid_cols // gy)
    wide = NF * each * 2
    bf16 = jnp.bfloat16
    dma = pltpu.SemaphoreType.DMA
    done = pl.pallas_call(
        functools.partial(far_kernel, grid_rows, grid_cols, (sets, each, per)),
        out_shape=(jax.ShapeDtypeStruct((nu, wide, vb), bf16),) * sets,
        in_specs=[SM] + [ANY] * sets,
        out_specs=(ANY,) * sets,
        scratch_shapes=[
            pltpu.VMEM((NA + 16, grid_rows), bf16),
            pltpu.VMEM((2, grid_cols, NA), bf16),
            pltpu.VMEM((sets, grid_rows, lanes), bf16),
            pltpu.VMEM((sets, lanes // LANES, NA + 16, LANES), bf16),
            pltpu.VMEM((sets, 2 * each, 2 * mper, grid_cols), bf16),
            pltpu.VMEM((sets, 2 * each, 16, grid_cols), bf16),
            pltpu.VMEM((sets, gy * 2 * mper, wide, vb), bf16),
            pltpu.VMEM((sets, gy, 1, wide, vb), bf16),
        ]
        + [dma((sets,))] * 9,
        compiler_params=pltpu.CompilerParams(
            vmem_limit_bytes=BIG, collective_id=1, has_side_effects=True
        ),
        name="far",
    )(freqs, *sd)
    block = nu // 4
    return pl.pallas_call(
        order_kernel,
        grid=(4,),
        out_shape=jax.ShapeDtypeStruct((nu, NF * 4, 2, vb), jnp.float32),
        in_specs=[pl.BlockSpec((block, wide, vb), lambda n: (n, 0, 0))] * sets,
        out_specs=pl.BlockSpec((block, NF * 4, 2, vb), lambda n: (n, 0, 0, 0)),
        name="order",
    )(*done)


def on_device(e_field, h_field, material, eps_table, src_pos, src_amp, freqs):
    rows, cols = material.shape[1:]
    grid_rows, grid_cols = rows * lax.axis_size("gx"), cols * lax.axis_size("gy")
    e_new, h_new, *sd = yee(e_field, h_field, material, eps_table, src_pos, src_amp)
    shape = e_field.shape
    return (e_new.reshape(shape), h_new.reshape(shape), far(sd, freqs, grid_rows, grid_cols))


def solution(mesh):
    placed = (
        P(None, None, "gx", "gy"),
        P(None, None, "gx", "gy"),
        P(None, "gx", "gy"),
        P(),
        P(),
        P(),
        P(),
    )
    return jax.shard_map(
        on_device,
        mesh=mesh,
        in_specs=placed,
        out_specs=(P(None, None, "gx", "gy"), P(None, None, "gx", "gy"), P("gx", None, None, "gy")),
        check_vma=False,
    )
```

```python
import functools
import math

import jax
import jax.numpy as jnp
from jax import lax
from jax.experimental import pallas as pl
from jax.experimental.pallas import tpu as pltpu
from jax.sharding import PartitionSpec as P

LZ = 3
FACE = 1
STEPS = 2
NF = 2
NA = 1024
NMAT = 8

courant = 0.5
source_rate = 0.7
zoom_factor = 4

BASE = 32
CHUNK = 16
PAIR = 32
LANES = 128
Y_STEPS = 8
Y_EARLY = 2
ORDER = {
    2: ("a0", "a1", "x0", "r0", "y2", "y3", "y4", "y5", "y6", "y7", "r1", "c0", "c1"),
    4: (
        "a0", "a1", "x0", "r0", "a2", "y2", "y3", "r1", "a3", "y4",
        "y5", "y6", "y7", "c0", "r2", "c1", "r3", "c2", "c3",
    ),
}
PAD = 128
ANY = pl.BlockSpec(memory_space=pl.ANY)
VM = pl.BlockSpec(memory_space=pltpu.VMEM)
SM = pl.BlockSpec(memory_space=pltpu.SMEM)
BIG = 60 * 1024 * 1024


def halo_kernel(
    e, h, m, col_rim, corner, rim_f, rim_m,
    edge_f, edge_m, packed, got_col, got_corner, got_f, got_m, load, send, recv,
):
    gx, gy = lax.axis_size("gx"), lax.axis_size("gy")
    i, z = lax.axis_index("gx"), lax.axis_index("gy")
    planes, rows, cols = e.shape
    around = [(a, b) for a in (-1, 0, 1) for b in (-1, 0, 1) if (a, b) != (0, 0)]

    def exists(step):
        row, col = i + step[0], z + step[1]
        return (row >= 0) & (row < gx) & (col >= 0) & (col < gy)

    loads = []
    for side, lane in enumerate((0, cols - LANES)):
        at = pl.ds(lane, LANES)
        loads.append(pltpu.make_async_copy(e.at[:, :, at], edge_f.at[side, pl.ds(0, planes)], load.at[3 * side]))
        loads.append(pltpu.make_async_copy(h.at[:, :, at], edge_f.at[side, pl.ds(planes, planes)], load.at[3 * side + 1]))
        loads.append(pltpu.make_async_copy(m.at[:, :, at], edge_m.at[side], load.at[3 * side + 2]))
    for copy in loads:
        copy.start()
    barrier = pltpu.get_barrier_semaphore()
    total = jnp.int32(0)
    for step in around:
        total += exists(step).astype(jnp.int32)

        @pl.when(exists(step))
        def _():
            pl.semaphore_signal(
                barrier, inc=1, device_id=(i + step[0], z + step[1]), device_id_type=pl.DeviceIdType.MESH
            )

    pl.semaphore_wait(barrier, total)

    def remote(step, src, dst, index):
        copy = pltpu.make_async_remote_copy(
            src_ref=src, dst_ref=dst, send_sem=send.at[index], recv_sem=recv.at[index],
            device_id=(i + step[0], z + step[1]), device_id_type=pl.DeviceIdType.MESH,
        )
        return step, copy

    rows_out, cols_out = [], []
    for side, low in enumerate((0, rows - 2)):
        step = (2 * side - 1, 0)
        at, to = pl.ds(low, 2), pl.ds(6 * side, 2)
        rows_out.append(remote(step, e.at[:, at, :], got_f.at[side, pl.ds(0, planes), to], 3 * side))
        rows_out.append(remote(step, h.at[:, at, :], got_f.at[side, pl.ds(planes, planes), to], 3 * side + 1))
        rows_out.append(remote(step, m.at[:, at, :], got_m.at[side, :, to], 3 * side + 2))
    for side in range(2):
        cols_out.append(remote((0, 2 * side - 1), packed.at[side], got_col.at[side], 6 + side))
        for end, low in enumerate((0, rows - 8)):
            step = (2 * end - 1, 2 * side - 1)
            src = packed.at[side, pl.ds(low, 8)]
            cols_out.append(remote(step, src, got_corner.at[end, side], 8 + 2 * side + end))

    def start(copies):
        for step, copy in copies:

            @pl.when(exists(step))
            def _():
                copy.start()

    start(rows_out)
    tall = 32
    lane = lax.broadcasted_iota(jnp.int32, (tall, LANES), 1)

    def pack(side, c, carry):
        at = pl.ds(pl.multiple_of(c * tall, tall), tall)
        place = ((lane + 2 * side) & (LANES - 1)) >> 2
        block = jnp.zeros((tall, LANES), jnp.float32)
        for p in range(2 * planes + LZ):
            if p < 2 * planes:
                piece = edge_f[side, p, at, :]
            else:
                piece = edge_m[side, p - 2 * planes, at, :].astype(jnp.float32)
            block = jnp.where(place == p, pltpu.roll(piece, 4 * p, 1), block)
        packed[side, at, :] = block
        return carry

    for side in range(2):
        for copy in loads[3 * side : 3 * side + 3]:
            copy.wait()
        lax.fori_loop(0, rows // tall, functools.partial(pack, side), 0)
        start(cols_out[3 * side : 3 * side + 3])
    for step, copy in rows_out + cols_out:

        @pl.when(exists((-step[0], -step[1])))
        def _():
            copy.wait_recv()

    last = (lane & 2) == 0
    after, before = exists((0, 1)), exists((0, -1))

    def merge(c, carry):
        at = pl.ds(pl.multiple_of(c * tall, tall), tall)
        right = jnp.where(after, got_col[0, at, :], 0.0)
        left = jnp.where(before, got_col[1, at, :], 0.0)
        col_rim[at, :] = jnp.where(last, right, left)
        return carry

    lax.fori_loop(0, rows // tall, merge, 0)
    for side in range(2):
        there = exists((1 - 2 * side, 0))
        row = lax.broadcasted_iota(jnp.int32, (8, cols), 0)
        kept = there & ((row >= 6) if side else (row < 2))
        rim_f[side] = jnp.where(kept[None], got_f[side], 0.0)
        rim_m[side] = jnp.where(kept[None], got_m[side], 0)
        right = jnp.where(there & after, got_corner[side, 0], 0.0)
        left = jnp.where(there & before, got_corner[side, 1], 0.0)
        corner[side] = jnp.where(last[:8], right, left)
    for step, copy in rows_out + cols_out:

        @pl.when(exists(step))
        def _():
            copy.wait_send()


def halo(e, h, m):
    planes, rows, cols = e.shape
    f32, i32 = jnp.float32, jnp.int32
    dma = pltpu.SemaphoreType.DMA
    return pl.pallas_call(
        halo_kernel,
        out_shape=(
            jax.ShapeDtypeStruct((rows, LANES), f32),
            jax.ShapeDtypeStruct((2, 8, LANES), f32),
            jax.ShapeDtypeStruct((2, 2 * planes, 8, cols), f32),
            jax.ShapeDtypeStruct((2, LZ, 8, cols), i32),
        ),
        in_specs=[ANY] * 3,
        out_specs=(VM,) * 4,
        scratch_shapes=[
            pltpu.VMEM((2, 2 * planes, rows, LANES), f32),
            pltpu.VMEM((2, LZ, rows, LANES), i32),
            pltpu.VMEM((2, rows, LANES), f32),
            pltpu.VMEM((2, rows, LANES), f32),
            pltpu.VMEM((2, 2, 8, LANES), f32),
            pltpu.VMEM((2, 2 * planes, 8, cols), f32),
            pltpu.VMEM((2, LZ, 8, cols), i32),
            dma((6,)),
            dma((12,)),
            dma((12,)),
        ],
        compiler_params=pltpu.CompilerParams(collective_id=0, has_side_effects=True),
        name="halo",
    )(e, h, m)


def split_sets(gx, cols):
    sets = 4 if 2 * cols >= gx * LANES else 2
    each = 4 // sets
    return sets, each, 2 * each * cols // (gx * LANES)


def yee_kernel(
    grid_rows, grid_cols, plan,
    e_hbm, h_hbm, m_hbm, col_rim, corner, rim_f, rim_m, eps, pos, amp,
    e_out, h_out, *rest,
):
    sets, each, per = plan
    sd_outs, (e_ext, h_ext, m_main, scale, src, first, *sd, sems) = rest[:sets], rest[sets:]
    rows, cols = m_main.shape[1:]
    width = cols + PAD
    high = e_ext.shape[1]
    row0 = lax.axis_index("gx") * rows
    col0 = lax.axis_index("gy") * cols
    pairs = rows // PAIR

    def load(q):
        here, there = pl.ds(PAIR * q, PAIR), pl.ds(BASE + PAIR * q, PAIR)
        return [
            pltpu.make_async_copy(e_hbm.at[:, here, :], e_ext.at[:, there, pl.ds(0, cols)], sems.at[0, q]),
            pltpu.make_async_copy(h_hbm.at[:, here, :], h_ext.at[:, there, pl.ds(0, cols)], sems.at[1, q]),
            pltpu.make_async_copy(m_hbm.at[:, here, :], m_main.at[:, here, :], sems.at[2, q]),
        ]

    def store(q):
        here, there = pl.ds(PAIR * q, PAIR), pl.ds(BASE + PAIR * q, PAIR)
        return [
            pltpu.make_async_copy(e_ext.at[:, there, pl.ds(0, cols)], e_out.at[:, here, :], sems.at[3, q]),
            pltpu.make_async_copy(h_ext.at[:, there, pl.ds(0, cols)], h_out.at[:, here, :], sems.at[4, q]),
        ] + [
            pltpu.make_async_copy(sd[s].at[:, here, :], sd_outs[s].at[:, here, :], sems.at[5 + s, q])
            for s in range(sets)
        ]

    for q in range(pairs):
        for copy in load(q):
            copy.start()
    count = amp.shape[1]
    used = high - 2 * CHUNK
    bf16 = jnp.bfloat16
    gather = functools.partial(
        lax.dot_general, dimension_numbers=(((1,), (1,)), ((), ())), preferred_element_type=jnp.float32
    )
    tall_at = lambda shape: row0 + lax.broadcasted_iota(jnp.int32, shape, 0) + (CHUNK - BASE)
    lane = lax.broadcasted_iota(jnp.int32, (width, LANES), 0)
    col_at = (col0 + jnp.where(lane < cols + PAD // 2, lane, lane - width)).astype(jnp.float32)
    row_at = tall_at((used, LANES)).astype(jnp.float32)
    row_s = jnp.broadcast_to(pos[1:2, :], (8, count))
    col_s = jnp.broadcast_to(pos[2:3, :], (8, count))
    inside = (row_s >= row0 - (BASE - CHUNK)) & (row_s < row0 + used - (BASE - CHUNK))
    inside &= (col_s >= col0 - PAD // 2) & (col_s < col0 + cols + PAD // 2)
    rank = jnp.where(inside, 1.0, 0.0)
    at_lane = lax.broadcasted_iota(jnp.int32, (8, count), 1)
    reach = 1
    while reach < count:
        rank = rank + jnp.where(at_lane >= reach, pltpu.roll(rank, reach, 1), 0.0)
        reach *= 2
    found = jnp.max(rank).astype(jnp.int32)
    rank = jnp.where(inside, rank, 0.0)[:1]
    hi = amp[...].astype(bf16).astype(jnp.float32)
    mid = (amp[...] - hi).astype(bf16).astype(jnp.float32)
    low = amp[...] - hi - mid
    parts = [
        (pos[1:2, :] >> 6).astype(jnp.float32), (pos[1:2, :] & 63).astype(jnp.float32),
        (pos[2:3, :] >> 6).astype(jnp.float32), (pos[2:3, :] & 63).astype(jnp.float32),
        pos[0:1, :].astype(jnp.float32), hi, mid, low,
    ]
    parts = jnp.concatenate(parts, 0).astype(bf16)
    for layer in range(LZ):
        src[layer] = jnp.zeros((high, width), jnp.float32)
    slot = lax.broadcasted_iota(jnp.int32, (LANES, count), 0).astype(jnp.float32)

    def place(group, carry):
        pick = jnp.where(slot + (group * LANES + 1).astype(jnp.float32) == rank, 1.0, 0.0)
        some = gather(parts, pick.astype(bf16))
        row, col = some[0:1] * 64.0 + some[1:2], some[2:3] * 64.0 + some[3:4]
        hit_col = jnp.where(col_at == col, 1.0, 0.0).astype(bf16)
        hit_col = jnp.concatenate([hit_col] * 3, 1)
        hit_row = row_at == row
        for layer in range(LZ):
            hit = hit_row & (some[4:5] == float(layer))
            left = [jnp.where(hit, some[p : p + 1], 0.0).astype(bf16) for p in (5, 6, 7)]
            src[layer, CHUNK : CHUNK + used, :] += gather(jnp.concatenate(left, 1), hit_col)
        return carry

    lax.fori_loop(0, lax.div(found + (LANES - 1), LANES), place, 0)

    def scale_of(index, row, col):
        value = jnp.full(index.shape, eps[0], jnp.float32)
        for material in range(1, NMAT):
            value = jnp.where(index == material, eps[material], value)
        inside = (row >= 0) & (row < grid_rows) & (col >= 0) & (col < grid_cols)
        return jnp.where(inside, courant / value, 0.0)

    col_main = col0 + lax.broadcasted_iota(jnp.int32, (CHUNK, cols), 1)
    lane_pad = lax.broadcasted_iota(jnp.int32, (CHUNK, PAD), 1)
    col_pad = col0 + jnp.where(lane_pad < PAD // 2, cols + lane_pad, lane_pad - PAD)
    row_chunk = row0 + lax.broadcasted_iota(jnp.int32, (CHUNK, cols), 0)

    def shown(block, plane):
        return pltpu.roll(block, PAD - 4 * plane, 1) if plane else block

    def fill(step_index, carry):
        r = pl.multiple_of(step_index * CHUNK, CHUNK)
        near = pl.ds(r, CHUNK)
        far = pl.ds(BASE + r, CHUNK)
        block = col_rim[near, :]
        for layer in range(LZ):
            scale[layer, far, :cols] = scale_of(m_main[layer, near, :], row_chunk + r, col_main)
            scale[layer, far, cols:] = scale_of(
                shown(block, 6 * LZ + layer), row_chunk[:, :PAD] + r, col_pad
            )
        for plane in range(3 * LZ):
            e_ext[plane, far, cols:] = shown(block, plane)
            h_ext[plane, far, cols:] = shown(block, 3 * LZ + plane)
        return carry

    row_eight = row0 + lax.broadcasted_iota(jnp.int32, (8, cols), 0)
    blank = jnp.zeros((8, width), jnp.float32)
    for side, target, offset, spare in (
        (0, BASE + rows, rows, BASE + rows + 8),
        (1, BASE - 8, -8, BASE - 16),
    ):
        here = slice(target, target + 8)
        block = corner[side]
        for layer in range(LZ):
            scale[layer, here, :cols] = scale_of(
                rim_m[side, layer], row_eight + offset, col_main[:8]
            )
            scale[layer, here, cols:] = scale_of(
                shown(block, 6 * LZ + layer), row_eight[:, :PAD] + offset, col_pad[:8]
            )
            scale[layer, spare : spare + 8, :] = blank
        for plane in range(3 * LZ):
            e_ext[plane, here, :cols] = rim_f[side, plane]
            h_ext[plane, here, :cols] = rim_f[side, 3 * LZ + plane]
            e_ext[plane, here, cols:] = shown(block, plane)
            h_ext[plane, here, cols:] = shown(block, 3 * LZ + plane)
            e_ext[plane, spare : spare + 8, :] = blank
            h_ext[plane, spare : spare + 8, :] = blank
    for plane in range(3 * LZ):
        e_ext[plane, high - 16 : high, :] = jnp.zeros((16, width), jnp.float32)
        h_ext[plane, 0:16, :] = jnp.zeros((16, width), jnp.float32)
    lane_c = lax.broadcasted_iota(jnp.int32, (CHUNK, width), 1)
    col_c = col0 + jnp.where(lane_c < cols + PAD // 2, lane_c, lane_c - width)
    weight = jnp.where(col_c >= 0, courant, 0.0)
    top = lax.axis_index("gx") == 0

    def magnetic_pass(index, carry):
        r = pl.multiple_of(index * CHUNK, CHUNK)
        now = pl.ds(r, CHUNK)
        more = pl.ds(r, CHUNK + 8)
        factor = weight * jnp.where(top & (index * CHUNK < BASE), 0.0, 1.0)
        zero = jnp.zeros((CHUNK, width), jnp.float32)
        ex = [e_ext[layer, now, :] for layer in range(LZ)] + [zero]
        ey = [e_ext[LZ + layer, now, :] for layer in range(LZ)] + [zero]
        for layer in range(LZ):
            ez = e_ext[2 * LZ + layer, now, :]
            ez_row = pltpu.roll(e_ext[2 * LZ + layer, more, :], CHUNK + 7, 0)[:CHUNK]
            ey_row = pltpu.roll(e_ext[LZ + layer, more, :], CHUNK + 7, 0)[:CHUNK]
            ez_col = pltpu.roll(ez, width - 1, 1)
            ex_col = pltpu.roll(ex[layer], width - 1, 1)
            curl_x = ez_col - ez - (ey[layer + 1] - ey[layer])
            curl_y = ex[layer + 1] - ex[layer] - (ez_row - ez)
            curl_z = ey_row - ey[layer] - (ex_col - ex[layer])
            for part, curl in enumerate((curl_x, curl_y, curl_z)):
                plane = part * LZ + layer
                h_ext[plane, now, :] = h_ext[plane, now, :] - factor * curl
        return carry

    def electric_pass(moment, last, index, carry):
        r = pl.multiple_of(index * CHUNK, CHUNK)
        now = pl.ds(r, CHUNK)
        more = pl.ds(pl.multiple_of(r - 8, 8), CHUNK + 8)
        drive = math.sin(source_rate * moment)
        zero = jnp.zeros((CHUNK, width), jnp.float32)
        hx = [zero] + [h_ext[layer, now, :] for layer in range(LZ)]
        hy = [zero] + [h_ext[LZ + layer, now, :] for layer in range(LZ)]
        for layer in range(LZ):
            hz = h_ext[2 * LZ + layer, now, :]
            hz_row = pltpu.roll(h_ext[2 * LZ + layer, more, :], 1, 0)[8:]
            hy_row = pltpu.roll(h_ext[LZ + layer, more, :], 1, 0)[8:]
            hx_now, hy_now = hx[layer + 1], hy[layer + 1]
            hz_col = pltpu.roll(hz, 1, 1)
            hx_col = pltpu.roll(hx_now, 1, 1)
            curl_x = hz - hz_col - (hy_now - hy[layer])
            curl_y = hx_now - hx[layer] - (hz - hz_row)
            curl_z = hy_now - hy_row - (hx_now - hx_col)
            factor = scale[layer, now, :]
            new_x = e_ext[layer, now, :] + factor * curl_x
            new_y = e_ext[LZ + layer, now, :] + factor * curl_y
            new_z = e_ext[2 * LZ + layer, now, :] + factor * curl_z + drive * src[layer, now, :]
            e_ext[layer, now, :] = new_x
            e_ext[LZ + layer, now, :] = new_y
            e_ext[2 * LZ + layer, now, :] = new_z
            if layer == FACE:
                faces = (-hy_now, hx_now, new_y, -new_x)
                for item, face in enumerate(faces):
                    if last:
                        old = first[item, now, :]
                        here = pl.ds(r - BASE, CHUNK)
                        for which, value in enumerate((old + face, face - old)):
                            share, place = divmod(which * each + item % each, per)
                            for q in range(cols // LANES):
                                piece = value[:, q * LANES : (q + 1) * LANES].astype(jnp.bfloat16)
                                lanes = pl.ds(place * LANES, LANES)
                                sd[item // each][q * (2 * each // per) + share, here, lanes] = piece
                    else:
                        first[item, now, :] = face
        return carry

    def arrive(q):
        for copy in load(q):
            copy.wait()
        for part in range(PAIR // CHUNK):
            fill(q * (PAIR // CHUNK) + part, 0)

    def advance(n, second):
        magnetic_pass(n, 0)
        electric_pass(1.0, False, n, 0)
        magnetic_pass(n - 1, 0)
        if second:
            electric_pass(2.0, True, n - 1, 0)

    start = BASE // CHUNK
    arrive(0)
    magnetic_pass(start - 1, 0)
    electric_pass(1.0, False, start - 1, 0)
    advance(start, False)

    def wave(q, carry):
        @pl.when(q < pairs - 1)
        def _():
            arrive(q + 1)

        for part in range(PAIR // CHUNK):
            advance(start + 1 + q * (PAIR // CHUNK) + part, True)
        for copy in store(q):
            copy.start()
        return carry

    lax.fori_loop(0, pairs, wave, 0)
    for q in range(pairs):
        for copy in store(q):
            copy.wait()


def yee(e_field, h_field, material, eps_table, src_pos, src_amp):
    rows, cols = material.shape[1:]
    gx = lax.axis_size("gx")
    sets, each, per = split_sets(gx, cols)
    grid_rows = rows * gx
    grid_cols = cols * lax.axis_size("gy")
    planes = 3 * LZ
    e = e_field.reshape(planes, rows, cols)
    h = h_field.reshape(planes, rows, cols)

    high = rows + 2 * BASE
    width = cols + PAD
    f32 = jnp.float32
    out = pl.pallas_call(
        functools.partial(yee_kernel, grid_rows, grid_cols, (sets, each, per)),
        out_shape=(
            jax.ShapeDtypeStruct((planes, rows, cols), f32),
            jax.ShapeDtypeStruct((planes, rows, cols), f32),
        )
        + (jax.ShapeDtypeStruct((gx, rows, per * LANES), jnp.bfloat16),) * sets,
        in_specs=[ANY, ANY, ANY, VM, VM, VM, VM, SM, VM, VM],
        out_specs=(ANY,) * (2 + sets),
        scratch_shapes=[
            pltpu.VMEM((planes, high, width), f32),
            pltpu.VMEM((planes, high, width), f32),
            pltpu.VMEM((LZ, rows, cols), jnp.int32),
            pltpu.VMEM((LZ, high, width), f32),
            pltpu.VMEM((LZ, high, width), f32),
            pltpu.VMEM((4, high, width), f32),
        ]
        + [pltpu.VMEM((gx, rows, per * LANES), jnp.bfloat16)] * sets
        + [
            pltpu.SemaphoreType.DMA((5 + sets, rows // PAIR)),
        ],
        compiler_params=pltpu.CompilerParams(vmem_limit_bytes=BIG),
        name="yee",
    )(
        e, h, material, *halo(e, h, material),
        eps_table, jnp.swapaxes(src_pos, 0, 1), src_amp[None, :],
    )
    return out


SIN = (-1.0 / 6.0, 1.0 / 120.0, -1.0 / 5040.0, 1.0 / 362880.0)
COS = (-0.5, 1.0 / 24.0, -1.0 / 720.0, 1.0 / 40320.0, -1.0 / 3628800.0)


def unit(phase, period):
    eighth = period // 8
    turn = phase & (period - 1)
    quarter = (turn + eighth) // (2 * eighth)
    x = (turn - quarter * (2 * eighth)).astype(jnp.float32) * (2.0 * math.pi / period)
    square = x * x
    sine = jnp.full_like(x, SIN[-1])
    for factor in SIN[-2::-1]:
        sine = sine * square + factor
    sine = x + x * (square * sine)
    cosine = jnp.full_like(x, COS[-1])
    for factor in COS[-2::-1]:
        cosine = cosine * square + factor
    cosine = 1.0 + square * cosine
    odd = (quarter & 1) == 1
    re = jnp.where(odd, sine, cosine)
    im = jnp.where(odd, cosine, sine)
    re = jnp.where(((quarter + 1) & 2) == 2, -re, re)
    im = jnp.where((quarter & 2) == 2, im, -im)
    return re, im


def layout(gx, gy):
    mper = max(8, NA // 2 // (gx * gy))
    return mper, NA // 2 // mper, NA // gx // mper


def build_x(x_tab, mper, owners):
    grid_rows = x_tab.shape[1]
    own = 2 * mper

    def fill_x(m, row):
        low = lax.broadcasted_iota(jnp.int32, m.shape, 1)
        a_re, a_im = unit(m * (low * LANES), zoom_factor * grid_rows)
        b_re, b_im = unit(m * low, zoom_factor * grid_rows)
        for block in range(grid_rows // LANES):
            h_re, h_im = a_re[:, block : block + 1], a_im[:, block : block + 1]
            re = h_re * b_re - h_im * b_im
            im = h_re * b_im + h_im * b_re
            both = jnp.concatenate([re, im], 0).astype(jnp.bfloat16)
            x_tab[pl.ds(row, 2 * m.shape[0]), block * LANES : (block + 1) * LANES] = both

    row = lax.broadcasted_iota(jnp.int32, (mper, LANES), 0)

    def body(t, carry):
        fill_x(row + t * mper, pl.multiple_of(t * own, own))
        return carry

    lax.fori_loop(0, owners, body, 0)
    fill_x(jnp.full((8, LANES), NA // 2, jnp.int32), owners * own)


def far_kernel(grid_rows, grid_cols, plan, freqs, *rest):
    sets, each, per = plan
    sd, outs, rest = rest[:sets], rest[sets : 2 * sets], rest[2 * sets :]
    x_tab, y_tab, v, g, left, left_x, held, held_x, *sems = rest
    send_v, recv_v, send_g, recv_g, send_x, recv_x, send_f, recv_f, send_e = sems
    gx, gy = lax.axis_size("gx"), lax.axis_size("gy")
    i, z = lax.axis_index("gx"), lax.axis_index("gy")
    me = i * gy + z
    count = gx * gy
    rows = grid_rows // gx
    cols = grid_cols // gy
    split = 2 * each // per
    slabs = cols // LANES
    mper, owners, near = layout(gx, gy)
    own = 2 * mper
    vb = NA // gy
    wide = NF * each * 2
    half = gx // 2
    mesh_id = pl.DeviceIdType.MESH

    upper = i >= half
    plane = jnp.where(upper, i - half, half - 1 - i)
    turn = jnp.where(upper, 0, gy) + z
    block_id = plane * near + turn

    def owner(t):
        c, r = lax.div(t, near), lax.rem(t, near)
        return jnp.where(r < gy, half + c, half - 1 - c), lax.rem(r, gy)

    end_i, end_z = owner(jnp.int32(owners - 1))

    def ship(src, dst, where, send_sem, recv_sem):
        here = (where[0] == i) & (where[1] == z)

        @pl.when(~here)
        def _():
            pltpu.make_async_remote_copy(
                src_ref=src, dst_ref=dst, send_sem=send_sem, recv_sem=recv_sem,
                device_id=where, device_id_type=mesh_id,
            ).start()

        @pl.when(here)
        def _():
            pltpu.make_async_copy(src, dst, recv_sem).start()

    def wait(ref, sem):
        pltpu.make_async_copy(ref, ref, sem).wait()

    here = pl.ds(pl.multiple_of(i * rows, rows), rows)
    lane = pl.multiple_of((z * slabs + lax.div(i, split)) * LANES, LANES)
    to = (pl.ds(lax.rem(i, split) * per, per), slice(None), pl.ds(lane, LANES))

    def v_ship(s, offset):
        peer = lax.rem(i + offset, gx)
        ship(sd[s].at[peer], v.at[s, here], (peer, z), send_v.at[s], recv_v.at[s])

    def g_ship(s, t):
        part = g.at[s, :, pl.ds(pl.multiple_of(t * own, own), own), :]
        ship(part, left.at[(s, *to)], owner(t), send_g.at[s], recv_g.at[s])

    def x_ship(s):
        part = g.at[s, :, pl.ds(owners * own, 16), :]
        ship(part, left_x.at[(s, *to)], (end_i, end_z), send_x.at[s], recv_x.at[s])

    def held_at(peer, sign):
        return (peer * 2 + sign) * mper

    def f_ship(s, peer):
        at = pl.ds(pl.multiple_of(turn * mper, mper), mper)
        src = held.at[s, pl.ds(held_at(peer, 0), mper)]
        ship(src, outs[s].at[at], (half + plane, peer), send_f.at[s], recv_f.at[s])
        at = pl.ds((near - 1 - turn) * mper + 1, mper - 1)
        src = held.at[s, pl.ds(held_at(peer, 1), mper - 1)]
        ship(src, outs[s].at[at], (half - 1 - plane, peer), send_f.at[s], recv_f.at[s])
        first = turn == 0
        across = jnp.where(first, half - plane, half - 1 - plane)
        slot = jnp.where(first, 0, near - turn)

        @pl.when(block_id > 0)
        def _():
            src = held.at[s, pl.ds(held_at(peer, 1) + mper - 1, 1)]
            ship(src, outs[s].at[pl.ds(slot * mper, 1)], (across, peer), send_f.at[s], recv_f.at[s])

    def f_sent(s):
        far_up = (gy - 1) * mper + gy * (mper - 1)
        far_low = gy * mper + (gy - 1) * mper
        for case, amount in (
            (upper & (block_id > 0), far_up + gy), (upper & (block_id == 0), far_up), (~upper, far_low),
        ):

            @pl.when(case)
            def _():
                wait(held.at[s, pl.ds(0, amount)], send_f.at[s])

    def e_ship(s, peer):
        ship(held_x.at[s, peer], outs[s].at[pl.ds(0, 1)], (0, peer), send_e.at[s], recv_f.at[s])

    def e_sent(s):
        for case, amount in ((i == 0, gy - 1), (i > 0, gy)):

            @pl.when(case)
            def _():
                wait(held_x.at[s, pl.ds(0, amount)], send_e.at[s])

    def build_y(low_block, high_block):
        tall = 32
        low = lax.broadcasted_iota(jnp.int32, (tall, LANES), 1)
        row = lax.broadcasted_iota(jnp.int32, (tall, LANES), 0)

        def body(d, carry):
            start = pl.multiple_of(d * tall, tall)
            y = row + start
            a_re, a_im = unit(y * (low * LANES + NA // 4), zoom_factor * grid_cols)
            b_re, b_im = unit(y * low, zoom_factor * grid_cols)
            for block in range(NA // LANES):
                h_re, h_im = a_re[:, block : block + 1], a_im[:, block : block + 1]
                at = slice(block * LANES, (block + 1) * LANES)
                y_tab[0, pl.ds(start, tall), at] = (h_re * b_re - h_im * b_im).astype(jnp.bfloat16)
                y_tab[1, pl.ds(start, tall), at] = (h_re * b_im + h_im * b_re).astype(jnp.bfloat16)
            return carry

        lax.fori_loop(grid_cols * low_block // (tall * Y_STEPS), grid_cols * high_block // (tall * Y_STEPS), body, 0)

    inv_norm = 1.0 / math.sqrt(grid_rows * grid_cols)
    mix = []
    for f in range(NF):
        angle = jnp.full((8, LANES), 0.5 * freqs[f], jnp.float32)
        half_re, half_im = jnp.cos(angle), jnp.sin(angle)
        turn_re, turn_im = jnp.cos(3.0 * angle) * inv_norm, jnp.sin(3.0 * angle) * inv_norm
        four = (turn_re * half_re, turn_im * half_re, -turn_im * half_im, turn_re * half_im)
        mix.append([value[:1, :1] for value in four])

    dot = functools.partial(jnp.dot, preferred_element_type=jnp.float32)
    parts = 2
    group = owners // parts

    def transform_rows(s):
        wait(v.at[s], recv_v.at[s])

        def body(c, carry):
            chunk = lax.rem(lax.div(block_id, group) + 1 + c, parts)
            tall = group * own
            start = pl.multiple_of(chunk * tall, tall)
            both = dot(x_tab[pl.ds(start, tall + 16), :], v[s]).astype(jnp.bfloat16)
            for f in range(per):
                g[s, f, pl.ds(start, tall), :] = both[:tall, f * LANES : (f + 1) * LANES]

            @pl.when(chunk == parts - 1)
            def _():
                for f in range(per):
                    g[s, f, owners * own :, :] = both[tall:, f * LANES : (f + 1) * LANES]
                x_ship(s)

            for e in range(group):
                g_ship(s, chunk * group + e)
            return carry

        lax.fori_loop(0, parts, body, 0)

    def one_hot(shape, source):
        row = lax.broadcasted_iota(jnp.int32, shape, 0)
        col = lax.broadcasted_iota(jnp.int32, shape, 1)
        return jnp.where(col == source(row), 1.0, 0.0).astype(jnp.bfloat16)

    size = (wide * mper, wide * mper)
    forth = one_hot(size, lambda row: lax.rem(row, wide) * mper + lax.div(row, wide))
    back = one_hot(size, lambda row: lax.rem(row, wide) * mper + mper - 1 - lax.div(row, wide))
    only = one_hot((wide, wide * 8), lambda row: row * 8)

    def finish(lhs, count_m, peer):
        at = pl.ds(pl.multiple_of(peer * vb, vb), vb)
        p_re, p_im = dot(lhs, y_tab[0, :, at]), dot(lhs, y_tab[1, :, at])
        plus, minus = [], []

        def both_signs(f):
            top = slice(2 * f * count_m, (2 * f + 1) * count_m)
            low = slice((2 * f + 1) * count_m, (2 * f + 2) * count_m)
            a_re, a_im, b_re, b_im = p_re[top], p_im[top], p_re[low], p_im[low]
            return (a_re - b_im, a_im + b_re), (a_re + b_im, a_im - b_re)

        fields = [both_signs(f) for f in range(2 * each)]
        for f in range(NF):
            p0, p1, q0, q1 = mix[f]
            for k in range(each):
                for sign, result in enumerate((plus, minus)):
                    s_re, s_im = fields[k][sign]
                    d_re, d_im = fields[each + k][sign]
                    result.append(p0 * s_re - p1 * s_im + (q0 * d_re - q1 * d_im))
                    result.append(p0 * s_im + p1 * s_re + (q0 * d_im + q1 * d_re))
        pack = lambda result: jnp.concatenate(result, 0).astype(jnp.bfloat16)
        return pack(plus), pack(minus)

    def transform_cols(s):
        wait(left.at[s], recv_g.at[s])
        lhs = left[s].reshape(2 * each * own, grid_cols)
        for step in range(1, gy + 1):
            peer = lax.rem(z + step, gy)
            plus, minus = finish(lhs, mper, peer)
            held[s, pl.ds(held_at(peer, 0), mper)] = dot(forth, plus).reshape(mper, wide, vb).astype(jnp.bfloat16)
            held[s, pl.ds(held_at(peer, 1), mper)] = dot(back, minus).reshape(mper, wide, vb).astype(jnp.bfloat16)
            f_ship(s, peer)

    at_end = (i == end_i) & (z == end_z)

    def transform_end(s):
        wait(left_x.at[s], recv_x.at[s])
        lhs = left_x[s].reshape(2 * each * 16, grid_cols)
        for step in range(1, gy + 1):
            peer = lax.rem(z + step, gy)
            _, minus = finish(lhs, 8, peer)
            held_x[s, peer] = dot(only, minus).reshape(1, wide, vb).astype(jnp.bfloat16)
            e_ship(s, peer)

    def owned(body):
        if near == 2 * gy:
            body()
        else:
            pl.when(turn < near)(body)

    barrier = pltpu.get_barrier_semaphore()
    for offset in range(1, count):
        peer = lax.rem(me + offset, count)
        pl.semaphore_signal(
            barrier, inc=1, device_id=(lax.div(peer, gy), lax.rem(peer, gy)), device_id_type=mesh_id
        )
    build_y(0, Y_EARLY)
    pl.semaphore_wait(barrier, count - 1)

    def send_fields(s):
        for offset in range(gx):
            v_ship(s, offset)

    def do_cols(s):
        owned(functools.partial(transform_cols, s))
        pl.when(at_end)(functools.partial(transform_end, s))

    steps = {"a": send_fields, "y": lambda part: build_y(part, part + 1), "r": transform_rows, "x": lambda _: build_x(x_tab, mper, owners), "c": do_cols}
    for token in ORDER[sets]:
        steps[token[0]](int(token[1:]))
    for s in range(sets):
        wait(outs[s], recv_f.at[s])
    for s in range(sets):
        wait(v.at[s, pl.ds(0, (gx - 1) * rows)], send_v.at[s])
        if near == 2 * gy:
            wait(g.at[s, :, pl.ds(0, (owners - 1) * own), :], send_g.at[s])
        else:
            for case, amount in ((turn < near, owners - 1), (turn >= near, owners)):

                @pl.when(case)
                def _():
                    wait(g.at[s, :, pl.ds(0, amount * own), :], send_g.at[s])

        @pl.when(~at_end)
        def _():
            wait(g.at[s, :, pl.ds(0, 16), :], send_x.at[s])

        owned(functools.partial(f_sent, s))
        pl.when(at_end)(functools.partial(e_sent, s))


def order_kernel(*refs):
    *parts, out = refs
    sets, each = len(parts), 4 // len(parts)
    for s, part in enumerate(parts):
        block = part[...].astype(jnp.float32)
        for f in range(NF):
            for k in range(each):
                at = 2 * (f * each + k)
                out[:, f * 4 + s * each + k] = block[:, at : at + 2]


def far(sd, freqs, grid_rows, grid_cols):
    gx, gy = lax.axis_size("gx"), lax.axis_size("gy")
    count = gx * gy
    nu, vb = NA // gx, NA // gy
    mper, owners, near = layout(gx, gy)
    lanes = sd[0].shape[2]
    sets, each, per = split_sets(gx, grid_cols // gy)
    wide = NF * each * 2
    bf16 = jnp.bfloat16
    dma = pltpu.SemaphoreType.DMA
    done = pl.pallas_call(
        functools.partial(far_kernel, grid_rows, grid_cols, (sets, each, per)),
        out_shape=(jax.ShapeDtypeStruct((nu, wide, vb), bf16),) * sets,
        in_specs=[SM] + [ANY] * sets,
        out_specs=(ANY,) * sets,
        scratch_shapes=[
            pltpu.VMEM((NA + 16, grid_rows), bf16),
            pltpu.VMEM((2, grid_cols, NA), bf16),
            pltpu.VMEM((sets, grid_rows, lanes), bf16),
            pltpu.VMEM((sets, lanes // LANES, NA + 16, LANES), bf16),
            pltpu.VMEM((sets, 2 * each, 2 * mper, grid_cols), bf16),
            pltpu.VMEM((sets, 2 * each, 16, grid_cols), bf16),
            pltpu.VMEM((sets, gy * 2 * mper, wide, vb), bf16),
            pltpu.VMEM((sets, gy, 1, wide, vb), bf16),
        ]
        + [dma((sets,))] * 9,
        compiler_params=pltpu.CompilerParams(
            vmem_limit_bytes=BIG, collective_id=1, has_side_effects=True
        ),
        name="far",
    )(freqs, *sd)
    block = nu // 1
    return pl.pallas_call(
        order_kernel,
        grid=(1,),
        out_shape=jax.ShapeDtypeStruct((nu, NF * 4, 2, vb), jnp.float32),
        in_specs=[pl.BlockSpec((block, wide, vb), lambda n: (n, 0, 0))] * sets,
        out_specs=pl.BlockSpec((block, NF * 4, 2, vb), lambda n: (n, 0, 0, 0)),
        name="order",
    )(*done)


def on_device(e_field, h_field, material, eps_table, src_pos, src_amp, freqs):
    rows, cols = material.shape[1:]
    grid_rows, grid_cols = rows * lax.axis_size("gx"), cols * lax.axis_size("gy")
    e_new, h_new, *sd = yee(e_field, h_field, material, eps_table, src_pos, src_amp)
    shape = e_field.shape
    return (e_new.reshape(shape), h_new.reshape(shape), far(sd, freqs, grid_rows, grid_cols))


def solution(mesh):
    placed = (
        P(None, None, "gx", "gy"),
        P(None, None, "gx", "gy"),
        P(None, "gx", "gy"),
        P(),
        P(),
        P(),
        P(),
    )
    return jax.shard_map(
        on_device,
        mesh=mesh,
        in_specs=placed,
        out_specs=(P(None, None, "gx", "gy"), P(None, None, "gx", "gy"), P("gx", None, None, "gy")),
        check_vma=False,
    )
```

```python
import functools
import math

import jax
import jax.numpy as jnp
from jax import lax
from jax.experimental import pallas as pl
from jax.experimental.pallas import tpu as pltpu
from jax.sharding import PartitionSpec as P

LZ = 3
FACE = 1
STEPS = 2
NF = 2
NA = 1024
NMAT = 8

courant = 0.5
source_rate = 0.7
zoom_factor = 4

BASE = 32
CHUNK = 16
PAIR = 32
LANES = 128
Y_STEPS = 8
Y_EARLY = 2
ORDER = {
    2: ("a0", "a1", "x0", "r0", "y2", "y3", "y4", "y5", "y6", "y7", "r1", "c0", "c1"),
    4: (
        "a0", "a1", "x0", "r0", "a2", "y2", "y3", "r1", "a3", "y4",
        "y5", "y6", "y7", "c0", "r2", "c1", "r3", "c2", "c3",
    ),
}
PAD = 128
ANY = pl.BlockSpec(memory_space=pl.ANY)
VM = pl.BlockSpec(memory_space=pltpu.VMEM)
SM = pl.BlockSpec(memory_space=pltpu.SMEM)
BIG = 60 * 1024 * 1024


def halo_kernel(
    e, h, m, col_rim, corner, rim_f, rim_m,
    edge_f, edge_m, packed, got_col, got_corner, got_f, got_m, load, send, recv,
):
    gx, gy = lax.axis_size("gx"), lax.axis_size("gy")
    i, z = lax.axis_index("gx"), lax.axis_index("gy")
    planes, rows, cols = e.shape
    around = [(a, b) for a in (-1, 0, 1) for b in (-1, 0, 1) if (a, b) != (0, 0)]

    def exists(step):
        row, col = i + step[0], z + step[1]
        return (row >= 0) & (row < gx) & (col >= 0) & (col < gy)

    loads = []
    for side, lane in enumerate((0, cols - LANES)):
        at = pl.ds(lane, LANES)
        loads.append(pltpu.make_async_copy(e.at[:, :, at], edge_f.at[side, pl.ds(0, planes)], load.at[3 * side]))
        loads.append(pltpu.make_async_copy(h.at[:, :, at], edge_f.at[side, pl.ds(planes, planes)], load.at[3 * side + 1]))
        loads.append(pltpu.make_async_copy(m.at[:, :, at], edge_m.at[side], load.at[3 * side + 2]))
    for copy in loads:
        copy.start()
    barrier = pltpu.get_barrier_semaphore()
    total = jnp.int32(0)
    for step in around:
        total += exists(step).astype(jnp.int32)

        @pl.when(exists(step))
        def _():
            pl.semaphore_signal(
                barrier, inc=1, device_id=(i + step[0], z + step[1]), device_id_type=pl.DeviceIdType.MESH
            )

    pl.semaphore_wait(barrier, total)

    def remote(step, src, dst, index):
        copy = pltpu.make_async_remote_copy(
            src_ref=src, dst_ref=dst, send_sem=send.at[index], recv_sem=recv.at[index],
            device_id=(i + step[0], z + step[1]), device_id_type=pl.DeviceIdType.MESH,
        )
        return step, copy

    rows_out, cols_out = [], []
    for side, low in enumerate((0, rows - 2)):
        step = (2 * side - 1, 0)
        at, to = pl.ds(low, 2), pl.ds(6 * side, 2)
        rows_out.append(remote(step, e.at[:, at, :], got_f.at[side, pl.ds(0, planes), to], 3 * side))
        rows_out.append(remote(step, h.at[:, at, :], got_f.at[side, pl.ds(planes, planes), to], 3 * side + 1))
        rows_out.append(remote(step, m.at[:, at, :], got_m.at[side, :, to], 3 * side + 2))
    for side in range(2):
        cols_out.append(remote((0, 2 * side - 1), packed.at[side], got_col.at[side], 6 + side))
        for end, low in enumerate((0, rows - 8)):
            step = (2 * end - 1, 2 * side - 1)
            src = packed.at[side, pl.ds(low, 8)]
            cols_out.append(remote(step, src, got_corner.at[end, side], 8 + 2 * side + end))

    def start(copies):
        for step, copy in copies:

            @pl.when(exists(step))
            def _():
                copy.start()

    start(rows_out)
    for copy in loads:
        copy.wait()
    tall = 32
    lane = lax.broadcasted_iota(jnp.int32, (tall, LANES), 1)

    def pack(c, carry):
        at = pl.ds(pl.multiple_of(c * tall, tall), tall)
        for side in range(2):
            place = ((lane + 2 * side) & (LANES - 1)) >> 2
            block = jnp.zeros((tall, LANES), jnp.float32)
            for p in range(2 * planes + LZ):
                if p < 2 * planes:
                    piece = edge_f[side, p, at, :]
                else:
                    piece = edge_m[side, p - 2 * planes, at, :].astype(jnp.float32)
                block = jnp.where(place == p, pltpu.roll(piece, 4 * p, 1), block)
            packed[side, at, :] = block
        return carry

    lax.fori_loop(0, rows // tall, pack, 0)
    start(cols_out)
    for step, copy in rows_out + cols_out:

        @pl.when(exists((-step[0], -step[1])))
        def _():
            copy.wait_recv()

    last = (lane & 2) == 0
    after, before = exists((0, 1)), exists((0, -1))

    def merge(c, carry):
        at = pl.ds(pl.multiple_of(c * tall, tall), tall)
        right = jnp.where(after, got_col[0, at, :], 0.0)
        left = jnp.where(before, got_col[1, at, :], 0.0)
        col_rim[at, :] = jnp.where(last, right, left)
        return carry

    lax.fori_loop(0, rows // tall, merge, 0)
    for side in range(2):
        there = exists((1 - 2 * side, 0))
        row = lax.broadcasted_iota(jnp.int32, (8, cols), 0)
        kept = there & ((row >= 6) if side else (row < 2))
        rim_f[side] = jnp.where(kept[None], got_f[side], 0.0)
        rim_m[side] = jnp.where(kept[None], got_m[side], 0)
        right = jnp.where(there & after, got_corner[side, 0], 0.0)
        left = jnp.where(there & before, got_corner[side, 1], 0.0)
        corner[side] = jnp.where(last[:8], right, left)
    for step, copy in rows_out + cols_out:

        @pl.when(exists(step))
        def _():
            copy.wait_send()


def halo(e, h, m):
    planes, rows, cols = e.shape
    f32, i32 = jnp.float32, jnp.int32
    dma = pltpu.SemaphoreType.DMA
    return pl.pallas_call(
        halo_kernel,
        out_shape=(
            jax.ShapeDtypeStruct((rows, LANES), f32),
            jax.ShapeDtypeStruct((2, 8, LANES), f32),
            jax.ShapeDtypeStruct((2, 2 * planes, 8, cols), f32),
            jax.ShapeDtypeStruct((2, LZ, 8, cols), i32),
        ),
        in_specs=[ANY] * 3,
        out_specs=(VM,) * 4,
        scratch_shapes=[
            pltpu.VMEM((2, 2 * planes, rows, LANES), f32),
            pltpu.VMEM((2, LZ, rows, LANES), i32),
            pltpu.VMEM((2, rows, LANES), f32),
            pltpu.VMEM((2, rows, LANES), f32),
            pltpu.VMEM((2, 2, 8, LANES), f32),
            pltpu.VMEM((2, 2 * planes, 8, cols), f32),
            pltpu.VMEM((2, LZ, 8, cols), i32),
            dma((6,)),
            dma((12,)),
            dma((12,)),
        ],
        compiler_params=pltpu.CompilerParams(collective_id=0, has_side_effects=True),
        name="halo",
    )(e, h, m)


def split_sets(gx, cols):
    sets = 4 if 2 * cols >= gx * LANES else 2
    each = 4 // sets
    return sets, each, 2 * each * cols // (gx * LANES)


def yee_kernel(
    grid_rows, grid_cols, plan,
    e_hbm, h_hbm, m_hbm, col_rim, corner, rim_f, rim_m, eps, pos, amp,
    e_out, h_out, *rest,
):
    sets, each, per = plan
    sd_outs, (e_ext, h_ext, m_main, scale, src, first, *sd, sems) = rest[:sets], rest[sets:]
    rows, cols = m_main.shape[1:]
    width = cols + PAD
    high = e_ext.shape[1]
    row0 = lax.axis_index("gx") * rows
    col0 = lax.axis_index("gy") * cols
    pairs = rows // PAIR

    def load(q):
        here, there = pl.ds(PAIR * q, PAIR), pl.ds(BASE + PAIR * q, PAIR)
        return [
            pltpu.make_async_copy(e_hbm.at[:, here, :], e_ext.at[:, there, pl.ds(0, cols)], sems.at[0, q]),
            pltpu.make_async_copy(h_hbm.at[:, here, :], h_ext.at[:, there, pl.ds(0, cols)], sems.at[1, q]),
            pltpu.make_async_copy(m_hbm.at[:, here, :], m_main.at[:, here, :], sems.at[2, q]),
        ]

    def store(q):
        here, there = pl.ds(PAIR * q, PAIR), pl.ds(BASE + PAIR * q, PAIR)
        return [
            pltpu.make_async_copy(e_ext.at[:, there, pl.ds(0, cols)], e_out.at[:, here, :], sems.at[3, q]),
            pltpu.make_async_copy(h_ext.at[:, there, pl.ds(0, cols)], h_out.at[:, here, :], sems.at[4, q]),
        ] + [
            pltpu.make_async_copy(sd[s].at[:, here, :], sd_outs[s].at[:, here, :], sems.at[5 + s, q])
            for s in range(sets)
        ]

    for q in range(pairs):
        for copy in load(q):
            copy.start()
    count = amp.shape[1]
    used = high - 2 * CHUNK
    bf16 = jnp.bfloat16
    gather = functools.partial(
        lax.dot_general, dimension_numbers=(((1,), (1,)), ((), ())), preferred_element_type=jnp.float32
    )
    tall_at = lambda shape: row0 + lax.broadcasted_iota(jnp.int32, shape, 0) + (CHUNK - BASE)
    lane = lax.broadcasted_iota(jnp.int32, (width, LANES), 0)
    col_at = (col0 + jnp.where(lane < cols + PAD // 2, lane, lane - width)).astype(jnp.float32)
    row_at = tall_at((used, LANES)).astype(jnp.float32)
    row_s = jnp.broadcast_to(pos[1:2, :], (8, count))
    col_s = jnp.broadcast_to(pos[2:3, :], (8, count))
    inside = (row_s >= row0 - (BASE - CHUNK)) & (row_s < row0 + used - (BASE - CHUNK))
    inside &= (col_s >= col0 - PAD // 2) & (col_s < col0 + cols + PAD // 2)
    rank = jnp.where(inside, 1.0, 0.0)
    at_lane = lax.broadcasted_iota(jnp.int32, (8, count), 1)
    reach = 1
    while reach < count:
        rank = rank + jnp.where(at_lane >= reach, pltpu.roll(rank, reach, 1), 0.0)
        reach *= 2
    found = jnp.max(rank).astype(jnp.int32)
    rank = jnp.where(inside, rank, 0.0)[:1]
    hi = amp[...].astype(bf16).astype(jnp.float32)
    mid = (amp[...] - hi).astype(bf16).astype(jnp.float32)
    low = amp[...] - hi - mid
    parts = [
        (pos[1:2, :] >> 6).astype(jnp.float32), (pos[1:2, :] & 63).astype(jnp.float32),
        (pos[2:3, :] >> 6).astype(jnp.float32), (pos[2:3, :] & 63).astype(jnp.float32),
        pos[0:1, :].astype(jnp.float32), hi, mid, low,
    ]
    parts = jnp.concatenate(parts, 0).astype(bf16)
    for layer in range(LZ):
        src[layer] = jnp.zeros((high, width), jnp.float32)
    slot = lax.broadcasted_iota(jnp.int32, (LANES, count), 0).astype(jnp.float32)

    def place(group, carry):
        pick = jnp.where(slot + (group * LANES + 1).astype(jnp.float32) == rank, 1.0, 0.0)
        some = gather(parts, pick.astype(bf16))
        row, col = some[0:1] * 64.0 + some[1:2], some[2:3] * 64.0 + some[3:4]
        hit_col = jnp.where(col_at == col, 1.0, 0.0).astype(bf16)
        hit_col = jnp.concatenate([hit_col] * 3, 1)
        hit_row = row_at == row
        for layer in range(LZ):
            hit = hit_row & (some[4:5] == float(layer))
            left = [jnp.where(hit, some[p : p + 1], 0.0).astype(bf16) for p in (5, 6, 7)]
            src[layer, CHUNK : CHUNK + used, :] += gather(jnp.concatenate(left, 1), hit_col)
        return carry

    lax.fori_loop(0, lax.div(found + (LANES - 1), LANES), place, 0)

    def scale_of(index, row, col):
        value = jnp.full(index.shape, eps[0], jnp.float32)
        for material in range(1, NMAT):
            value = jnp.where(index == material, eps[material], value)
        inside = (row >= 0) & (row < grid_rows) & (col >= 0) & (col < grid_cols)
        return jnp.where(inside, courant / value, 0.0)

    col_main = col0 + lax.broadcasted_iota(jnp.int32, (CHUNK, cols), 1)
    lane_pad = lax.broadcasted_iota(jnp.int32, (CHUNK, PAD), 1)
    col_pad = col0 + jnp.where(lane_pad < PAD // 2, cols + lane_pad, lane_pad - PAD)
    row_chunk = row0 + lax.broadcasted_iota(jnp.int32, (CHUNK, cols), 0)

    def shown(block, plane):
        return pltpu.roll(block, PAD - 4 * plane, 1) if plane else block

    def fill(step_index, carry):
        r = pl.multiple_of(step_index * CHUNK, CHUNK)
        near = pl.ds(r, CHUNK)
        far = pl.ds(BASE + r, CHUNK)
        block = col_rim[near, :]
        for layer in range(LZ):
            scale[layer, far, :cols] = scale_of(m_main[layer, near, :], row_chunk + r, col_main)
            scale[layer, far, cols:] = scale_of(
                shown(block, 6 * LZ + layer), row_chunk[:, :PAD] + r, col_pad
            )
        for plane in range(3 * LZ):
            e_ext[plane, far, cols:] = shown(block, plane)
            h_ext[plane, far, cols:] = shown(block, 3 * LZ + plane)
        return carry

    row_eight = row0 + lax.broadcasted_iota(jnp.int32, (8, cols), 0)
    blank = jnp.zeros((8, width), jnp.float32)
    for side, target, offset, spare in (
        (0, BASE + rows, rows, BASE + rows + 8),
        (1, BASE - 8, -8, BASE - 16),
    ):
        here = slice(target, target + 8)
        block = corner[side]
        for layer in range(LZ):
            scale[layer, here, :cols] = scale_of(
                rim_m[side, layer], row_eight + offset, col_main[:8]
            )
            scale[layer, here, cols:] = scale_of(
                shown(block, 6 * LZ + layer), row_eight[:, :PAD] + offset, col_pad[:8]
            )
            scale[layer, spare : spare + 8, :] = blank
        for plane in range(3 * LZ):
            e_ext[plane, here, :cols] = rim_f[side, plane]
            h_ext[plane, here, :cols] = rim_f[side, 3 * LZ + plane]
            e_ext[plane, here, cols:] = shown(block, plane)
            h_ext[plane, here, cols:] = shown(block, 3 * LZ + plane)
            e_ext[plane, spare : spare + 8, :] = blank
            h_ext[plane, spare : spare + 8, :] = blank
    for plane in range(3 * LZ):
        e_ext[plane, high - 16 : high, :] = jnp.zeros((16, width), jnp.float32)
        h_ext[plane, 0:16, :] = jnp.zeros((16, width), jnp.float32)
    lane_c = lax.broadcasted_iota(jnp.int32, (CHUNK, width), 1)
    col_c = col0 + jnp.where(lane_c < cols + PAD // 2, lane_c, lane_c - width)
    weight = jnp.where(col_c >= 0, courant, 0.0)
    top = lax.axis_index("gx") == 0

    def magnetic_pass(index, carry):
        r = pl.multiple_of(index * CHUNK, CHUNK)
        now = pl.ds(r, CHUNK)
        more = pl.ds(r, CHUNK + 8)
        factor = weight * jnp.where(top & (index * CHUNK < BASE), 0.0, 1.0)
        zero = jnp.zeros((CHUNK, width), jnp.float32)
        ex = [e_ext[layer, now, :] for layer in range(LZ)] + [zero]
        ey = [e_ext[LZ + layer, now, :] for layer in range(LZ)] + [zero]
        for layer in range(LZ):
            ez = e_ext[2 * LZ + layer, now, :]
            ez_row = pltpu.roll(e_ext[2 * LZ + layer, more, :], CHUNK + 7, 0)[:CHUNK]
            ey_row = pltpu.roll(e_ext[LZ + layer, more, :], CHUNK + 7, 0)[:CHUNK]
            ez_col = pltpu.roll(ez, width - 1, 1)
            ex_col = pltpu.roll(ex[layer], width - 1, 1)
            curl_x = ez_col - ez - (ey[layer + 1] - ey[layer])
            curl_y = ex[layer + 1] - ex[layer] - (ez_row - ez)
            curl_z = ey_row - ey[layer] - (ex_col - ex[layer])
            for part, curl in enumerate((curl_x, curl_y, curl_z)):
                plane = part * LZ + layer
                h_ext[plane, now, :] = h_ext[plane, now, :] - factor * curl
        return carry

    def electric_pass(moment, last, index, carry):
        r = pl.multiple_of(index * CHUNK, CHUNK)
        now = pl.ds(r, CHUNK)
        more = pl.ds(pl.multiple_of(r - 8, 8), CHUNK + 8)
        drive = math.sin(source_rate * moment)
        zero = jnp.zeros((CHUNK, width), jnp.float32)
        hx = [zero] + [h_ext[layer, now, :] for layer in range(LZ)]
        hy = [zero] + [h_ext[LZ + layer, now, :] for layer in range(LZ)]
        for layer in range(LZ):
            hz = h_ext[2 * LZ + layer, now, :]
            hz_row = pltpu.roll(h_ext[2 * LZ + layer, more, :], 1, 0)[8:]
            hy_row = pltpu.roll(h_ext[LZ + layer, more, :], 1, 0)[8:]
            hx_now, hy_now = hx[layer + 1], hy[layer + 1]
            hz_col = pltpu.roll(hz, 1, 1)
            hx_col = pltpu.roll(hx_now, 1, 1)
            curl_x = hz - hz_col - (hy_now - hy[layer])
            curl_y = hx_now - hx[layer] - (hz - hz_row)
            curl_z = hy_now - hy_row - (hx_now - hx_col)
            factor = scale[layer, now, :]
            new_x = e_ext[layer, now, :] + factor * curl_x
            new_y = e_ext[LZ + layer, now, :] + factor * curl_y
            new_z = e_ext[2 * LZ + layer, now, :] + factor * curl_z + drive * src[layer, now, :]
            e_ext[layer, now, :] = new_x
            e_ext[LZ + layer, now, :] = new_y
            e_ext[2 * LZ + layer, now, :] = new_z
            if layer == FACE:
                faces = (-hy_now, hx_now, new_y, -new_x)
                for item, face in enumerate(faces):
                    if last:
                        old = first[item, now, :]
                        here = pl.ds(r - BASE, CHUNK)
                        for which, value in enumerate((old + face, face - old)):
                            share, place = divmod(which * each + item % each, per)
                            for q in range(cols // LANES):
                                piece = value[:, q * LANES : (q + 1) * LANES].astype(jnp.bfloat16)
                                lanes = pl.ds(place * LANES, LANES)
                                sd[item // each][q * (2 * each // per) + share, here, lanes] = piece
                    else:
                        first[item, now, :] = face
        return carry

    def arrive(q):
        for copy in load(q):
            copy.wait()
        for part in range(PAIR // CHUNK):
            fill(q * (PAIR // CHUNK) + part, 0)

    def advance(n, second):
        magnetic_pass(n, 0)
        electric_pass(1.0, False, n, 0)
        magnetic_pass(n - 1, 0)
        if second:
            electric_pass(2.0, True, n - 1, 0)

    start = BASE // CHUNK
    arrive(0)
    magnetic_pass(start - 1, 0)
    electric_pass(1.0, False, start - 1, 0)
    advance(start, False)

    def wave(q, carry):
        @pl.when(q < pairs - 1)
        def _():
            arrive(q + 1)

        for part in range(PAIR // CHUNK):
            advance(start + 1 + q * (PAIR // CHUNK) + part, True)
        for copy in store(q):
            copy.start()
        return carry

    lax.fori_loop(0, pairs, wave, 0)
    for q in range(pairs):
        for copy in store(q):
            copy.wait()


def yee(e_field, h_field, material, eps_table, src_pos, src_amp):
    rows, cols = material.shape[1:]
    gx = lax.axis_size("gx")
    sets, each, per = split_sets(gx, cols)
    grid_rows = rows * gx
    grid_cols = cols * lax.axis_size("gy")
    planes = 3 * LZ
    e = e_field.reshape(planes, rows, cols)
    h = h_field.reshape(planes, rows, cols)

    high = rows + 2 * BASE
    width = cols + PAD
    f32 = jnp.float32
    out = pl.pallas_call(
        functools.partial(yee_kernel, grid_rows, grid_cols, (sets, each, per)),
        out_shape=(
            jax.ShapeDtypeStruct((planes, rows, cols), f32),
            jax.ShapeDtypeStruct((planes, rows, cols), f32),
        )
        + (jax.ShapeDtypeStruct((gx, rows, per * LANES), jnp.bfloat16),) * sets,
        in_specs=[ANY, ANY, ANY, VM, VM, VM, VM, SM, VM, VM],
        out_specs=(ANY,) * (2 + sets),
        scratch_shapes=[
            pltpu.VMEM((planes, high, width), f32),
            pltpu.VMEM((planes, high, width), f32),
            pltpu.VMEM((LZ, rows, cols), jnp.int32),
            pltpu.VMEM((LZ, high, width), f32),
            pltpu.VMEM((LZ, high, width), f32),
            pltpu.VMEM((4, high, width), f32),
        ]
        + [pltpu.VMEM((gx, rows, per * LANES), jnp.bfloat16)] * sets
        + [
            pltpu.SemaphoreType.DMA((5 + sets, rows // PAIR)),
        ],
        compiler_params=pltpu.CompilerParams(vmem_limit_bytes=BIG),
        name="yee",
    )(
        e, h, material, *halo(e, h, material),
        eps_table, jnp.swapaxes(src_pos, 0, 1), src_amp[None, :],
    )
    return out


SIN = (-1.0 / 6.0, 1.0 / 120.0, -1.0 / 5040.0, 1.0 / 362880.0)
COS = (-0.5, 1.0 / 24.0, -1.0 / 720.0, 1.0 / 40320.0, -1.0 / 3628800.0)


def unit(phase, period):
    eighth = period // 8
    turn = phase & (period - 1)
    quarter = (turn + eighth) // (2 * eighth)
    x = (turn - quarter * (2 * eighth)).astype(jnp.float32) * (2.0 * math.pi / period)
    square = x * x
    sine = jnp.full_like(x, SIN[-1])
    for factor in SIN[-2::-1]:
        sine = sine * square + factor
    sine = x + x * (square * sine)
    cosine = jnp.full_like(x, COS[-1])
    for factor in COS[-2::-1]:
        cosine = cosine * square + factor
    cosine = 1.0 + square * cosine
    odd = (quarter & 1) == 1
    re = jnp.where(odd, sine, cosine)
    im = jnp.where(odd, cosine, sine)
    re = jnp.where(((quarter + 1) & 2) == 2, -re, re)
    im = jnp.where((quarter & 2) == 2, im, -im)
    return re, im


def layout(gx, gy):
    mper = max(8, NA // 2 // (gx * gy))
    return mper, NA // 2 // mper, NA // gx // mper


def build_x(x_tab, mper, owners):
    grid_rows = x_tab.shape[1]
    own = 2 * mper

    def fill_x(m, row):
        low = lax.broadcasted_iota(jnp.int32, m.shape, 1)
        a_re, a_im = unit(m * (low * LANES), zoom_factor * grid_rows)
        b_re, b_im = unit(m * low, zoom_factor * grid_rows)
        for block in range(grid_rows // LANES):
            h_re, h_im = a_re[:, block : block + 1], a_im[:, block : block + 1]
            re = h_re * b_re - h_im * b_im
            im = h_re * b_im + h_im * b_re
            both = jnp.concatenate([re, im], 0).astype(jnp.bfloat16)
            x_tab[pl.ds(row, 2 * m.shape[0]), block * LANES : (block + 1) * LANES] = both

    row = lax.broadcasted_iota(jnp.int32, (mper, LANES), 0)

    def body(t, carry):
        fill_x(row + t * mper, pl.multiple_of(t * own, own))
        return carry

    lax.fori_loop(0, owners, body, 0)
    fill_x(jnp.full((8, LANES), NA // 2, jnp.int32), owners * own)


def far_kernel(grid_rows, grid_cols, plan, freqs, *rest):
    sets, each, per = plan
    sd, outs, rest = rest[:sets], rest[sets : 2 * sets], rest[2 * sets :]
    x_tab, y_tab, v, g, left, left_x, held, held_x, *sems = rest
    send_v, recv_v, send_g, recv_g, send_x, recv_x, send_f, recv_f, send_e = sems
    gx, gy = lax.axis_size("gx"), lax.axis_size("gy")
    i, z = lax.axis_index("gx"), lax.axis_index("gy")
    me = i * gy + z
    count = gx * gy
    rows = grid_rows // gx
    cols = grid_cols // gy
    split = 2 * each // per
    slabs = cols // LANES
    mper, owners, near = layout(gx, gy)
    own = 2 * mper
    vb = NA // gy
    wide = NF * each * 2
    half = gx // 2
    mesh_id = pl.DeviceIdType.MESH

    upper = i >= half
    plane = jnp.where(upper, i - half, half - 1 - i)
    turn = jnp.where(upper, 0, gy) + z
    block_id = plane * near + turn

    def owner(t):
        c, r = lax.div(t, near), lax.rem(t, near)
        return jnp.where(r < gy, half + c, half - 1 - c), lax.rem(r, gy)

    end_i, end_z = owner(jnp.int32(owners - 1))

    def ship(src, dst, where, send_sem, recv_sem):
        here = (where[0] == i) & (where[1] == z)

        @pl.when(~here)
        def _():
            pltpu.make_async_remote_copy(
                src_ref=src, dst_ref=dst, send_sem=send_sem, recv_sem=recv_sem,
                device_id=where, device_id_type=mesh_id,
            ).start()

        @pl.when(here)
        def _():
            pltpu.make_async_copy(src, dst, recv_sem).start()

    def wait(ref, sem):
        pltpu.make_async_copy(ref, ref, sem).wait()

    here = pl.ds(pl.multiple_of(i * rows, rows), rows)
    lane = pl.multiple_of((z * slabs + lax.div(i, split)) * LANES, LANES)
    to = (pl.ds(lax.rem(i, split) * per, per), slice(None), pl.ds(lane, LANES))

    def v_ship(s, offset):
        peer = lax.rem(i + offset, gx)
        ship(sd[s].at[peer], v.at[s, here], (peer, z), send_v.at[s], recv_v.at[s])

    def g_ship(s, t):
        part = g.at[s, :, pl.ds(pl.multiple_of(t * own, own), own), :]
        ship(part, left.at[(s, *to)], owner(t), send_g.at[s], recv_g.at[s])

    def x_ship(s):
        part = g.at[s, :, pl.ds(owners * own, 16), :]
        ship(part, left_x.at[(s, *to)], (end_i, end_z), send_x.at[s], recv_x.at[s])

    def held_at(peer, sign):
        return (peer * 2 + sign) * mper

    def f_ship(s, peer):
        at = pl.ds(pl.multiple_of(turn * mper, mper), mper)
        src = held.at[s, pl.ds(held_at(peer, 0), mper)]
        ship(src, outs[s].at[at], (half + plane, peer), send_f.at[s], recv_f.at[s])
        at = pl.ds((near - 1 - turn) * mper + 1, mper - 1)
        src = held.at[s, pl.ds(held_at(peer, 1), mper - 1)]
        ship(src, outs[s].at[at], (half - 1 - plane, peer), send_f.at[s], recv_f.at[s])
        first = turn == 0
        across = jnp.where(first, half - plane, half - 1 - plane)
        slot = jnp.where(first, 0, near - turn)

        @pl.when(block_id > 0)
        def _():
            src = held.at[s, pl.ds(held_at(peer, 1) + mper - 1, 1)]
            ship(src, outs[s].at[pl.ds(slot * mper, 1)], (across, peer), send_f.at[s], recv_f.at[s])

    def f_sent(s):
        far_up = (gy - 1) * mper + gy * (mper - 1)
        far_low = gy * mper + (gy - 1) * mper
        for case, amount in (
            (upper & (block_id > 0), far_up + gy), (upper & (block_id == 0), far_up), (~upper, far_low),
        ):

            @pl.when(case)
            def _():
                wait(held.at[s, pl.ds(0, amount)], send_f.at[s])

    def e_ship(s, peer):
        ship(held_x.at[s, peer], outs[s].at[pl.ds(0, 1)], (0, peer), send_e.at[s], recv_f.at[s])

    def e_sent(s):
        for case, amount in ((i == 0, gy - 1), (i > 0, gy)):

            @pl.when(case)
            def _():
                wait(held_x.at[s, pl.ds(0, amount)], send_e.at[s])

    def build_y(low_block, high_block):
        tall = 32
        low = lax.broadcasted_iota(jnp.int32, (tall, LANES), 1)
        row = lax.broadcasted_iota(jnp.int32, (tall, LANES), 0)

        def body(d, carry):
            start = pl.multiple_of(d * tall, tall)
            y = row + start
            a_re, a_im = unit(y * (low * LANES + NA // 4), zoom_factor * grid_cols)
            b_re, b_im = unit(y * low, zoom_factor * grid_cols)
            for block in range(NA // LANES):
                h_re, h_im = a_re[:, block : block + 1], a_im[:, block : block + 1]
                at = slice(block * LANES, (block + 1) * LANES)
                y_tab[0, pl.ds(start, tall), at] = (h_re * b_re - h_im * b_im).astype(jnp.bfloat16)
                y_tab[1, pl.ds(start, tall), at] = (h_re * b_im + h_im * b_re).astype(jnp.bfloat16)
            return carry

        lax.fori_loop(grid_cols * low_block // (tall * Y_STEPS), grid_cols * high_block // (tall * Y_STEPS), body, 0)

    inv_norm = 1.0 / math.sqrt(grid_rows * grid_cols)
    mix = []
    for f in range(NF):
        angle = jnp.full((8, LANES), 0.5 * freqs[f], jnp.float32)
        half_re, half_im = jnp.cos(angle), jnp.sin(angle)
        turn_re, turn_im = jnp.cos(3.0 * angle) * inv_norm, jnp.sin(3.0 * angle) * inv_norm
        four = (turn_re * half_re, turn_im * half_re, -turn_im * half_im, turn_re * half_im)
        mix.append([value[:1, :1] for value in four])

    dot = functools.partial(jnp.dot, preferred_element_type=jnp.float32)
    parts = 2
    group = owners // parts

    def transform_rows(s):
        wait(v.at[s], recv_v.at[s])

        def body(c, carry):
            chunk = lax.rem(lax.div(block_id, group) + 1 + c, parts)
            tall = group * own
            start = pl.multiple_of(chunk * tall, tall)
            both = dot(x_tab[pl.ds(start, tall + 16), :], v[s]).astype(jnp.bfloat16)
            for f in range(per):
                g[s, f, pl.ds(start, tall), :] = both[:tall, f * LANES : (f + 1) * LANES]

            @pl.when(chunk == parts - 1)
            def _():
                for f in range(per):
                    g[s, f, owners * own :, :] = both[tall:, f * LANES : (f + 1) * LANES]
                x_ship(s)

            for e in range(group):
                g_ship(s, chunk * group + e)
            return carry

        lax.fori_loop(0, parts, body, 0)

    def one_hot(shape, source):
        row = lax.broadcasted_iota(jnp.int32, shape, 0)
        col = lax.broadcasted_iota(jnp.int32, shape, 1)
        return jnp.where(col == source(row), 1.0, 0.0).astype(jnp.bfloat16)

    size = (wide * mper, wide * mper)
    forth = one_hot(size, lambda row: lax.rem(row, wide) * mper + lax.div(row, wide))
    back = one_hot(size, lambda row: lax.rem(row, wide) * mper + mper - 1 - lax.div(row, wide))
    only = one_hot((wide, wide * 8), lambda row: row * 8)

    def finish(lhs, count_m, peer):
        at = pl.ds(pl.multiple_of(peer * vb, vb), vb)
        p_re, p_im = dot(lhs, y_tab[0, :, at]), dot(lhs, y_tab[1, :, at])
        plus, minus = [], []

        def both_signs(f):
            top = slice(2 * f * count_m, (2 * f + 1) * count_m)
            low = slice((2 * f + 1) * count_m, (2 * f + 2) * count_m)
            a_re, a_im, b_re, b_im = p_re[top], p_im[top], p_re[low], p_im[low]
            return (a_re - b_im, a_im + b_re), (a_re + b_im, a_im - b_re)

        fields = [both_signs(f) for f in range(2 * each)]
        for f in range(NF):
            p0, p1, q0, q1 = mix[f]
            for k in range(each):
                for sign, result in enumerate((plus, minus)):
                    s_re, s_im = fields[k][sign]
                    d_re, d_im = fields[each + k][sign]
                    result.append(p0 * s_re - p1 * s_im + (q0 * d_re - q1 * d_im))
                    result.append(p0 * s_im + p1 * s_re + (q0 * d_im + q1 * d_re))
        pack = lambda result: jnp.concatenate(result, 0).astype(jnp.bfloat16)
        return pack(plus), pack(minus)

    def transform_cols(s):
        wait(left.at[s], recv_g.at[s])
        lhs = left[s].reshape(2 * each * own, grid_cols)
        for step in range(1, gy + 1):
            peer = lax.rem(z + step, gy)
            plus, minus = finish(lhs, mper, peer)
            held[s, pl.ds(held_at(peer, 0), mper)] = dot(forth, plus).reshape(mper, wide, vb).astype(jnp.bfloat16)
            held[s, pl.ds(held_at(peer, 1), mper)] = dot(back, minus).reshape(mper, wide, vb).astype(jnp.bfloat16)
            f_ship(s, peer)

    at_end = (i == end_i) & (z == end_z)

    def transform_end(s):
        wait(left_x.at[s], recv_x.at[s])
        lhs = left_x[s].reshape(2 * each * 16, grid_cols)
        for step in range(1, gy + 1):
            peer = lax.rem(z + step, gy)
            _, minus = finish(lhs, 8, peer)
            held_x[s, peer] = dot(only, minus).reshape(1, wide, vb).astype(jnp.bfloat16)
            e_ship(s, peer)

    def owned(body):
        if near == 2 * gy:
            body()
        else:
            pl.when(turn < near)(body)

    barrier = pltpu.get_barrier_semaphore()
    for offset in range(1, count):
        peer = lax.rem(me + offset, count)
        pl.semaphore_signal(
            barrier, inc=1, device_id=(lax.div(peer, gy), lax.rem(peer, gy)), device_id_type=mesh_id
        )
    build_y(0, Y_EARLY)
    pl.semaphore_wait(barrier, count - 1)

    def send_fields(s):
        for offset in range(gx):
            v_ship(s, offset)

    def do_cols(s):
        owned(functools.partial(transform_cols, s))
        pl.when(at_end)(functools.partial(transform_end, s))

    steps = {"a": send_fields, "y": lambda part: build_y(part, part + 1), "r": transform_rows, "x": lambda _: build_x(x_tab, mper, owners), "c": do_cols}
    for token in ORDER[sets]:
        steps[token[0]](int(token[1:]))
    for s in range(sets):
        wait(outs[s], recv_f.at[s])
    for s in range(sets):
        wait(v.at[s, pl.ds(0, (gx - 1) * rows)], send_v.at[s])
        if near == 2 * gy:
            wait(g.at[s, :, pl.ds(0, (owners - 1) * own), :], send_g.at[s])
        else:
            for case, amount in ((turn < near, owners - 1), (turn >= near, owners)):

                @pl.when(case)
                def _():
                    wait(g.at[s, :, pl.ds(0, amount * own), :], send_g.at[s])

        @pl.when(~at_end)
        def _():
            wait(g.at[s, :, pl.ds(0, 16), :], send_x.at[s])

        owned(functools.partial(f_sent, s))
        pl.when(at_end)(functools.partial(e_sent, s))


def order_kernel(*refs):
    *parts, out = refs
    sets, each = len(parts), 4 // len(parts)
    for s, part in enumerate(parts):
        block = part[...].astype(jnp.float32)
        for f in range(NF):
            for k in range(each):
                at = 2 * (f * each + k)
                out[:, f * 4 + s * each + k] = block[:, at : at + 2]


def far(sd, freqs, grid_rows, grid_cols):
    gx, gy = lax.axis_size("gx"), lax.axis_size("gy")
    count = gx * gy
    nu, vb = NA // gx, NA // gy
    mper, owners, near = layout(gx, gy)
    lanes = sd[0].shape[2]
    sets, each, per = split_sets(gx, grid_cols // gy)
    wide = NF * each * 2
    bf16 = jnp.bfloat16
    dma = pltpu.SemaphoreType.DMA
    done = pl.pallas_call(
        functools.partial(far_kernel, grid_rows, grid_cols, (sets, each, per)),
        out_shape=(jax.ShapeDtypeStruct((nu, wide, vb), bf16),) * sets,
        in_specs=[SM] + [ANY] * sets,
        out_specs=(ANY,) * sets,
        scratch_shapes=[
            pltpu.VMEM((NA + 16, grid_rows), bf16),
            pltpu.VMEM((2, grid_cols, NA), bf16),
            pltpu.VMEM((sets, grid_rows, lanes), bf16),
            pltpu.VMEM((sets, lanes // LANES, NA + 16, LANES), bf16),
            pltpu.VMEM((sets, 2 * each, 2 * mper, grid_cols), bf16),
            pltpu.VMEM((sets, 2 * each, 16, grid_cols), bf16),
            pltpu.VMEM((sets, gy * 2 * mper, wide, vb), bf16),
            pltpu.VMEM((sets, gy, 1, wide, vb), bf16),
        ]
        + [dma((sets,))] * 9,
        compiler_params=pltpu.CompilerParams(
            vmem_limit_bytes=BIG, collective_id=1, has_side_effects=True
        ),
        name="far",
    )(freqs, *sd)
    block = nu
    return pl.pallas_call(
        order_kernel,
        grid=(1,),
        out_shape=jax.ShapeDtypeStruct((nu, NF * 4, 2, vb), jnp.float32),
        in_specs=[pl.BlockSpec((block, wide, vb), lambda n: (n, 0, 0))] * sets,
        out_specs=pl.BlockSpec((block, NF * 4, 2, vb), lambda n: (n, 0, 0, 0)),
        name="order",
    )(*done)


def on_device(e_field, h_field, material, eps_table, src_pos, src_amp, freqs):
    rows, cols = material.shape[1:]
    grid_rows, grid_cols = rows * lax.axis_size("gx"), cols * lax.axis_size("gy")
    e_new, h_new, *sd = yee(e_field, h_field, material, eps_table, src_pos, src_amp)
    shape = e_field.shape
    return (e_new.reshape(shape), h_new.reshape(shape), far(sd, freqs, grid_rows, grid_cols))


def solution(mesh):
    placed = (
        P(None, None, "gx", "gy"),
        P(None, None, "gx", "gy"),
        P(None, "gx", "gy"),
        P(),
        P(),
        P(),
        P(),
    )
    return jax.shard_map(
        on_device,
        mesh=mesh,
        in_specs=placed,
        out_specs=(P(None, None, "gx", "gy"), P(None, None, "gx", "gy"), P("gx", None, None, "gy")),
        check_vma=False,
    )
```
